32 devices in a mesh: section: 8 (over z, x), dp: 4 (over y, core).
Axes of the slice: x: 2, y: 2, z: 4, core: 2. Of those that a mesh axis runs over, the one named last changes fastest.
Arguments:
- act_in: bfloat16 [8, 128, 2048], P('section', None, 'dp'), may hold values from -6 to 6
- saved_act: bfloat16 [8, 128, 2048], P('section', None, 'dp'), may hold values from -6 to 6
- cotangent: bfloat16 [8, 128, 2048], P('section', None, 'dp'), may hold values from -6 to 6
- weight_xz: bfloat16 [8, 2048, 8192], P('section', 'dp'), may hold values from -0.125 to 0.125
- weight_bcdt: bfloat16 [8, 320, 2048], P('section', None, 'dp'), may hold values from -0.125 to 0.125
- weight_out: bfloat16 [8, 4096, 2048], P('section', None, 'dp'), may hold values from -0.09375 to 0.09375
- conv_x: float32 [8, 4, 4096], P('section', None, 'dp'), may hold values from -3 to 3
- conv_bc: float32 [8, 4, 256], P('section'), may hold values from -3 to 3
- dt_bias: float32 [8, 64], P('section', 'dp'), may hold values from -8 to -2
- a_log: float32 [8, 64], P('section', 'dp'), may hold values from 0 to 2.7
- d_skip: float32 [8, 64], P('section', 'dp'), may hold values from 0.5 to 1.5
- norm_gain: float32 [8, 4096], P('section', 'dp'), may hold values from 0.1 to 1.9
Outputs:
- next_act: bfloat16 [8, 128, 2048], P('section', None, 'dp')
- prev_grad: bfloat16 [8, 128, 2048], P('section', None, 'dp')
- grad_xz: float32 [8, 2048, 8192], P('section', 'dp')
- grad_bcdt: float32 [8, 320, 2048], P('section', None, 'dp')
- grad_out: float32 [8, 4096, 2048], P('section', None, 'dp')
The draws below stay inside these ranges and needn't reach their ends.
All inputs are finite; a program needn't handle non-finite values.
Results may differ from the reference program's by a relative error of at most 0.0084.
Values may be sent and summed in bfloat16 or wider, within the bound.
A program may use at most 128 MiB of HBM per device.

```python
import jax
import jax.numpy as jnp
from jax import lax

D = 2048
HEAD_DIM = 64
NSTATE = 128
HEADS = 64
KCONV = 4
SEQ = 128
INNER = 4096
SECTIONS = 8


def levels(stream_key, dims, pieces, smallest, largest):
    def one(axis_at, parts):
        steps = jax.random.uniform(jax.random.fold_in(jax.random.fold_in(stream_key, 6), axis_at), (parts,), jnp.float32, smallest / len(pieces), largest / len(pieces))
        return jnp.repeat(jnp.exp(steps), dims[axis_at] // parts).reshape((-1,) + (1,) * (len(dims) - axis_at - 1))

    gain = one(*pieces[0])
    for cut in pieces[1:]:
        gain = gain * one(*cut)
    return gain


def bell_draw(own_key, shape, scale, limit, shards=(), kind=jnp.bfloat16):
    factor_of = levels(own_key, shape, shards, -0.22, 0.18) if shards else 1.0
    array = jax.random.normal(own_key, shape, jnp.float32) * scale * factor_of
    return jnp.minimum(jnp.maximum(array, -limit), limit).astype(kind)


def setup_inputs(seed: int = 0) -> dict:
    keys = jax.random.split(jax.random.key(seed), 13)
    act_in = bell_draw(keys[0], (SECTIONS, SEQ, D), 1.0, 6.0, ((0, 8), (2, 4)))
    saved_act = bell_draw(keys[1], (SECTIONS, SEQ, D), 1.0, 6.0, ((0, 8), (2, 4)))
    cotangent = bell_draw(keys[2], (SECTIONS, SEQ, D), 1.0, 6.0, ((0, 8), (2, 4)))
    weight_xz = bell_draw(keys[3], (SECTIONS, D, 2 * INNER), D ** -0.5, 0.125, ((0, 8), (1, 4)))
    weight_bcdt = bell_draw(keys[4], (SECTIONS, 2 * NSTATE + HEADS, D), D ** -0.5, 0.125, ((0, 8), (2, 4)))
    weight_out = bell_draw(keys[5], (SECTIONS, INNER, D), INNER ** -0.5, 0.09375, ((0, 8), (2, 4)))
    conv_x = bell_draw(keys[6], (SECTIONS, KCONV, INNER), KCONV ** -0.5, 3.0, ((0, 8), (2, 4)), jnp.float32)
    conv_bc = bell_draw(keys[7], (SECTIONS, KCONV, 2 * NSTATE), KCONV ** -0.5, 3.0, ((0, 8),), jnp.float32)
    dt_bias = jnp.clip(-8.0 + 6.0 * jax.random.uniform(keys[8], (SECTIONS, HEADS), jnp.float32) ** levels(keys[8], (SECTIONS, HEADS), ((0, 8), (1, 4)), -0.2, 0.2), -8.0, -2.0)
    a_log = jnp.clip(2.7 * jax.random.uniform(keys[9], (SECTIONS, HEADS), jnp.float32) ** levels(keys[9], (SECTIONS, HEADS), ((0, 8), (1, 4)), -0.2, 0.2), 0.0, 2.7)
    d_skip = jnp.clip(0.5 + 1.0 * jax.random.uniform(keys[10], (SECTIONS, HEADS), jnp.float32) ** levels(keys[10], (SECTIONS, HEADS), ((0, 8), (1, 4)), -0.2, 0.2), 0.5, 1.5)
    norm_gain = jnp.clip(1.0 + 0.18 * jax.random.normal(keys[11], (SECTIONS, INNER), jnp.float32), 0.1, 1.9)
    return dict(act_in=act_in, saved_act=saved_act, cotangent=cotangent, weight_xz=weight_xz, weight_bcdt=weight_bcdt, weight_out=weight_out, conv_x=conv_x, conv_bc=conv_bc, dt_bias=dt_bias, a_log=a_log, d_skip=d_skip, norm_gain=norm_gain)


def causal_conv(values, kernel_taps):
    kernel = kernel_taps.shape[0]
    length = values.shape[1]
    padded = jnp.pad(values, ((0, 0), (kernel - 1, 0), (0, 0)))
    running = jnp.zeros_like(values)
    for offset in range(kernel):
        running = running + kernel_taps[offset] * padded[:, offset:offset + length]
    return running

def map_scores(maps):
    input_map = maps[:, :, :NSTATE]
    output_map = maps[:, :, NSTATE:]
    return lax.dot_general(output_map, input_map, (((2,), (2,)), ((0,), (0,))), preferred_element_type=jnp.float32)

def map_grads(d_scores, maps):
    values = maps.astype(jnp.float32)
    input_map = values[:, :, :NSTATE]
    output_map = values[:, :, NSTATE:]
    d_input = jnp.einsum('bts,btn->bsn', d_scores, output_map, precision=lax.Precision.HIGHEST)
    d_output = jnp.einsum('bts,bsn->btn', d_scores, input_map, precision=lax.Precision.HIGHEST)
    return jnp.concatenate([d_input, d_output], axis=2)

def mixer(proj_x, proj_z, proj_dt, scores, conv_taps, dt_offset, log_rate, skip_gain):
    batch, length, width = proj_x.shape
    nheads = dt_offset.shape[0]
    head_width = width // nheads
    xconv = jax.nn.silu(causal_conv(proj_x, conv_taps))
    steps = jax.nn.softplus(proj_dt + dt_offset)
    cumul = jnp.cumsum(steps * -jnp.exp(log_rate), axis=1)
    position = jnp.arange(length)
    causal = (position[:, None] >= position[None, :])[None, None]
    heads_cum = jnp.swapaxes(cumul, 1, 2)
    spread = heads_cum[:, :, :, None] - heads_cum[:, :, None, :]
    decay = jnp.where(causal, jnp.exp(jnp.where(causal, spread, 0.0)), 0.0)
    weights = decay * scores[:, None] * jnp.swapaxes(steps, 1, 2)[:, :, None, :]
    heads_in = xconv.reshape(batch, length, nheads, head_width)
    result = jnp.einsum('bhts,bshp->bthp', weights, heads_in, precision=lax.Precision.HIGHEST)
    result = result + skip_gain[None, None, :, None] * heads_in
    gate_in = jax.nn.silu(proj_z.reshape(batch, length, nheads, head_width))
    return (result * gate_in).reshape(batch * length, width)

def project(rows, weight_xz, weight_bcdt, conv_bc):
    values = rows.astype(jnp.float32)
    scales = lax.rsqrt(lax.optimization_barrier(jnp.mean(values * values, axis=1, keepdims=True)) + 1e-05)
    normed = (values * scales).astype(jnp.bfloat16)
    proj_xz = jnp.dot(normed, weight_xz, preferred_element_type=jnp.float32)
    proj_bcdt = lax.dot_general(normed, weight_bcdt, (((1,), (1,)), ((), ())), preferred_element_type=jnp.float32)
    pre_maps = proj_bcdt[:, :2 * NSTATE]
    maps = jax.nn.silu(causal_conv(pre_maps[None], conv_bc))[0].astype(jnp.bfloat16)
    return (values, normed, scales, proj_xz, pre_maps, maps, proj_bcdt[:, 2 * NSTATE:])

def gate_parts(projected, conv_x, dt_bias, a_log, d_skip, norm_gain):
    values, normed, scales, proj_xz, pre_maps, maps, proj_dt = projected
    length = proj_xz.shape[0]
    split_xz = proj_xz.reshape(1, length, HEADS, 2, HEAD_DIM)
    mix_x = split_xz[:, :, :, 0].reshape(1, length, INNER)
    mix_z = split_xz[:, :, :, 1].reshape(1, length, INNER)
    maps_three = maps[None]
    scores = map_scores(maps_three)

    def local_mix(in_x, in_z, in_dt, in_scores):
        return mixer(in_x, in_z, in_dt, in_scores, conv_x, dt_bias, a_log, d_skip)
    gated, mix_back = jax.vjp(local_mix, mix_x, mix_z, proj_dt[None], scores)
    inverse = lax.rsqrt(lax.optimization_barrier(jnp.sum(gated * gated, axis=1)) / INNER + 1e-05)[:, None]
    mixed_in = (gated * inverse * norm_gain).astype(jnp.bfloat16)
    return (gated, mix_back, inverse, mixed_in, maps_three)

def one_section(packed):
    act_in, saved_act, cotangent, weight_xz, weight_bcdt, weight_out, conv_x, conv_bc, dt_bias, a_log, d_skip, norm_gain = packed
    forward_proj = project(act_in, weight_xz, weight_bcdt, conv_bc)
    mixed_in = gate_parts(forward_proj, conv_x, dt_bias, a_log, d_skip, norm_gain)[3]
    mixed = jnp.dot(mixed_in, weight_out, preferred_element_type=jnp.float32)
    section_out = (act_in.astype(jnp.float32) + mixed).astype(jnp.bfloat16)
    back_proj = project(saved_act, weight_xz, weight_bcdt, conv_bc)
    values, normed, scales, proj_xz, pre_maps, maps, proj_dt = back_proj
    gated, mix_back, inverse, mixed_in, maps_three = gate_parts(back_proj, conv_x, dt_bias, a_log, d_skip, norm_gain)
    length = values.shape[0]
    grad_out = jnp.dot(mixed_in.T, cotangent, preferred_element_type=jnp.float32)
    d_mixed = jnp.dot(cotangent, weight_out.T, preferred_element_type=jnp.float32)
    dots = lax.optimization_barrier(jnp.sum(d_mixed * norm_gain * gated, axis=1))
    d_gated = inverse * norm_gain * d_mixed - gated * (inverse * inverse * inverse) * dots[:, None] / INNER
    d_px, d_pz, d_pdt, d_scores = mix_back(d_gated)
    d_maps = map_grads(d_scores, maps_three)
    conv_out, conv_back = jax.vjp(lambda inner_v: jax.nn.silu(causal_conv(inner_v, conv_bc)), pre_maps[None])
    d_pre = conv_back(d_maps)[0][0]
    round_bcdt = jnp.concatenate([d_pre, d_pdt.reshape(length, HEADS)], axis=1).astype(jnp.bfloat16)
    round_xz = jnp.stack([d_px.reshape(length, HEADS, HEAD_DIM), d_pz.reshape(length, HEADS, HEAD_DIM)], axis=2).reshape(length, 2 * INNER).astype(jnp.bfloat16)
    grad_xz = jnp.dot(normed.T, round_xz, preferred_element_type=jnp.float32)
    grad_bcdt = jnp.dot(round_bcdt.T, normed, preferred_element_type=jnp.float32)
    d_normed = jnp.dot(round_xz, weight_xz.T, preferred_element_type=jnp.float32)
    d_normed = d_normed + jnp.dot(round_bcdt, weight_bcdt, preferred_element_type=jnp.float32)
    inner_sum = lax.optimization_barrier(jnp.sum(d_normed * values, axis=1, keepdims=True))
    d_norm_in = scales * d_normed - values * (scales * scales * scales) * inner_sum / D
    d_input = (cotangent.astype(jnp.float32) + d_norm_in).astype(jnp.bfloat16)
    return (section_out, d_input, grad_xz, grad_bcdt, grad_out)

def reference(act_in, saved_act, cotangent, weight_xz, weight_bcdt, weight_out, conv_x, conv_bc, dt_bias, a_log, d_skip, norm_gain):
    results = lax.map(one_section, (act_in, saved_act, cotangent, weight_xz, weight_bcdt, weight_out, conv_x, conv_bc, dt_bias, a_log, d_skip, norm_gain))
    section_out, d_input, grad_xz, grad_bcdt, grad_out = results
    next_act = jnp.roll(section_out, 1, axis=0)
    prev_grad = jnp.roll(d_input, -1, axis=0)
    return (next_act, prev_grad, grad_xz, grad_bcdt, grad_out)
```

```python
import functools

import jax
import jax.numpy as jnp
from jax import lax
from jax.experimental import pallas as pl
from jax.experimental.pallas import tpu as pltpu
from jax.sharding import PartitionSpec as P

D = 2048
HEAD_DIM = 64
NSTATE = 128
HEADS = 64
SEQ = 128
INNER = 4096
KCONV = 4
MAPS = 2 * NSTATE


def from_behind(x, axis, by):
    length = lax.axis_size(axis)
    return lax.ppermute(x, axis, [(i, (i + by) % length) for i in range(length)])


def swap(x, mask):
    length = lax.axis_size("dp")
    return lax.ppermute(x, "dp", [(i, i ^ mask) for i in range(length)])


def masks():
    length = lax.axis_size("dp")
    out = []
    bit = 1
    while bit < length:
        out.append(bit)
        bit *= 2
    return out


def sum_all(x):
    for bit in masks():
        x = x + swap(x, bit)
    return x


def tied(x, other):
    return lax.optimization_barrier((x, other))[0]


def sum_first(part):
    length = lax.axis_size("dp")
    came = {j - 1: swap(part(j).astype(jnp.bfloat16), 1) for j in range(1, length, 2)}
    return {j: part(j) + came[j].astype(jnp.float32) for j in sorted(came, reverse=True)}


def sum_rest(held, after=None):
    first = begun = None
    for bit in masks()[1:]:
        sent = {j: held[j].astype(jnp.bfloat16) for j in held if j & bit}
        if after is not None and first is None:
            sent = {j: tied(x, after) for j, x in sent.items()}
        came = {j ^ bit: swap(x, bit) for j, x in sent.items()}
        if first is None:
            first = came[0]
            begun = sent[bit]
        held = {j: held[j] + came[j].astype(jnp.float32) for j in came}
    return held[0], first, begun


def sum_both(x, after):
    me = lax.axis_index("dp")
    odd = (me & 1) != 0
    x = x + swap(x, 1)
    mine = tied(jnp.where(odd, x[SEQ:], x[:SEQ]), after)
    for bit in masks()[1:]:
        mine = mine + swap(mine, bit)
    other = swap(mine, 1)
    return jnp.where(odd, other, mine), jnp.where(odd, mine, other)


def gather_cols(block, after=None):
    me = lax.axis_index("dp")
    length = lax.axis_size("dp")
    if after is not None:
        block = tied(block, after)
    held = [block]
    order = [0]
    for bit in reversed(masks()):
        held = held + [swap(b, bit) for b in held]
        order = order + [j ^ bit for j in order]
    by_mask = {j: b for j, b in zip(order, held)}
    level = [by_mask[j] for j in range(length)]
    for bit in masks():
        flip = (me & bit) != 0
        level = [jnp.where(flip, level[j ^ bit], level[j]) for j in range(length)]
    return jnp.concatenate(level, axis=1), held[-1]


def causal_conv(values, kernel_taps):
    kernel = kernel_taps.shape[0]
    length = values.shape[0]
    padded = jnp.pad(values, ((kernel - 1, 0), (0, 0)))
    running = jnp.zeros_like(values)
    for offset in range(kernel):
        running = running + kernel_taps[offset] * padded[offset : offset + length]
    return running


def mixer(proj_x, proj_z, proj_dt, scores, conv_taps, dt_offset, log_rate, skip_gain):
    length, width = proj_x.shape
    nheads = dt_offset.shape[0]
    head_width = width // nheads
    xconv = jax.nn.silu(causal_conv(proj_x, conv_taps))
    steps = jax.nn.softplus(proj_dt + dt_offset)
    position = jnp.arange(length)
    causal = position[:, None] >= position[None, :]
    cumul = jnp.dot(
        causal.astype(jnp.float32), steps * -jnp.exp(log_rate), precision=lax.Precision.HIGHEST
    )
    heads_cum = cumul.T
    spread = heads_cum[:, :, None] - heads_cum[:, None, :]
    decay = jnp.where(causal[None], jnp.exp(jnp.where(causal[None], spread, 0.0)), 0.0)
    weights = decay * scores[None] * steps.T[:, None, :]
    heads_in = xconv.reshape(length, nheads, head_width)
    result = jnp.einsum("hts,shp->thp", weights, heads_in, precision=lax.Precision.HIGH)
    result = result + skip_gain[None, :, None] * heads_in
    gate_in = jax.nn.silu(proj_z.reshape(length, nheads, head_width))
    return (result * gate_in).reshape(length, width)


def times_transposed(left, right):
    return lax.dot_general(
        left, right, (((1,), (1,)), ((), ())), preferred_element_type=jnp.float32
    )


def transposed_times(left, right):
    return lax.dot_general(
        left, right, (((0,), (0,)), ((), ())), preferred_element_type=jnp.float32
    )


def per_device(
    act_in,
    saved_act,
    cotangent,
    weight_xz,
    weight_bcdt,
    weight_out,
    conv_x,
    conv_bc,
    dt_bias,
    a_log,
    d_skip,
    norm_gain,
):
    input_rows = act_in[0]
    saved_rows = saved_act[0]
    cot_rows = cotangent[0]
    local_xz = weight_xz[0]
    local_bcdt = weight_bcdt[0]
    local_out = weight_out[0]
    taps_x = conv_x[0]
    taps_bc = conv_bc[0]
    dt_offset = dt_bias[0]
    log_rate = a_log[0]
    skip_gain = d_skip[0]
    gain_local = norm_gain[0]
    own_heads = dt_offset.shape[0]
    me = lax.axis_index("dp")
    head_first = me * own_heads
    width = own_heads * HEAD_DIM

    def whole_act(pre_part):
        return jax.nn.silu(causal_conv(pre_part, taps_bc))

    both = jnp.concatenate([saved_rows, input_rows], axis=0)
    both_values = both.astype(jnp.float32)
    squares = jnp.sum(both_values * both_values, axis=1, keepdims=True)
    def xz_part(j):
        cols = lax.dynamic_slice_in_dim(local_xz, (me ^ j) * 2 * width, 2 * width, 1)
        return jnp.dot(both, cols, preferred_element_type=jnp.float32)

    held_xz = sum_first(xz_part)
    back_raw, back_first, back_begun = sum_rest({j: x[:SEQ] for j, x in held_xz.items()})
    back_small, forward_small = sum_both(
        jnp.concatenate([times_transposed(both, local_bcdt), squares], axis=1), back_begun
    )

    def mixed_part(j):
        taken = lax.dynamic_slice_in_dim(local_out, (me ^ j) * width, width, 0)
        return times_transposed(cot_rows, taken)

    d_mixed = sum_rest(sum_first(mixed_part), back_begun)[0]
    forward_raw = sum_rest({j: x[SEQ:] for j, x in held_xz.items()}, back_first)[0]

    def project(rows, small, raw_xz):
        raw_cols = small[:, : MAPS + HEADS]
        scales = lax.rsqrt(small[:, MAPS + HEADS :] / D + 1e-05)
        return (rows.astype(jnp.float32), scales, raw_xz, raw_cols)

    back_proj = project(saved_rows, back_small, back_raw)
    forward_proj = project(input_rows, forward_small, forward_raw)

    def gate_parts(projected):
        values, scales, raw_xz, raw_cols = projected
        own_xz = raw_xz * scales
        whole_cols = raw_cols * scales
        pre_part = whole_cols[:, :MAPS]
        maps = whole_act(pre_part).astype(jnp.bfloat16)
        own_dt = lax.dynamic_slice_in_dim(whole_cols[:, MAPS:], head_first, own_heads, 1)
        split_xz = own_xz.reshape(SEQ, own_heads, 2, HEAD_DIM)
        mix_x = split_xz[:, :, 0].reshape(SEQ, width)
        mix_z = split_xz[:, :, 1].reshape(SEQ, width)
        scores = times_transposed(maps[:, NSTATE:], maps[:, :NSTATE])

        def local_mix(in_x, in_z, in_dt, in_scores):
            return mixer(in_x, in_z, in_dt, in_scores, taps_x, dt_offset, log_rate, skip_gain)

        gated, mix_back = jax.vjp(local_mix, mix_x, mix_z, own_dt, scores)
        return (gated, mix_back, maps, pre_part)

    values, scales, raw_xz, raw_cols = back_proj
    gated, mix_back, maps, pre_part = gate_parts(back_proj)
    gained = gated * gain_local
    row_sums = sum_all(
        jnp.stack([jnp.sum(gated * gated, axis=1), jnp.sum(d_mixed * gained, axis=1)])
    )
    inverse = lax.rsqrt(row_sums[0] / INNER + 1e-05)[:, None]
    dots = row_sums[1][:, None]
    mixed_in = (gained * inverse).astype(jnp.bfloat16)
    d_gated = inverse * gain_local * d_mixed - gated * (inverse * inverse * inverse) * dots / INNER
    d_px, d_pz, d_pdt, d_scores = mix_back(d_gated)
    own_round = (
        jnp.stack(
            [
                d_px.reshape(SEQ, own_heads, HEAD_DIM),
                d_pz.reshape(SEQ, own_heads, HEAD_DIM),
            ],
            axis=2,
        )
        .reshape(SEQ, own_heads * 2 * HEAD_DIM)
        .astype(jnp.bfloat16)
    )
    round_xz, round_last = gather_cols(own_round)
    inner_own = jnp.sum(own_round.astype(jnp.float32) * raw_xz, axis=1, keepdims=True)
    wide_maps = maps.astype(jnp.float32)
    d_maps = jnp.concatenate(
        [
            jnp.dot(d_scores.T, wide_maps[:, NSTATE:], precision=lax.Precision.HIGH),
            jnp.dot(d_scores, wide_maps[:, :NSTATE], precision=lax.Precision.HIGH),
        ],
        axis=1,
    )
    d_dt_full = lax.dynamic_update_slice_in_dim(
        jnp.zeros((SEQ, HEADS), jnp.float32), d_pdt, head_first, 1
    )
    summed = sum_all(jnp.concatenate([d_maps, d_dt_full, inner_own], axis=1))
    conv_out, conv_back = jax.vjp(whole_act, pre_part)
    d_pre = conv_back(summed[:, :MAPS])[0]
    round_bcdt = jnp.concatenate([d_pre, summed[:, MAPS : MAPS + HEADS]], axis=1).astype(
        jnp.bfloat16
    )
    inner_sum = summed[:, MAPS + HEADS :] + jnp.sum(
        round_bcdt.astype(jnp.float32) * raw_cols, axis=1, keepdims=True
    )

    fwd_gated = gate_parts(forward_proj)[0]
    fwd_all, _ = gather_cols((fwd_gated * gain_local).astype(jnp.bfloat16), round_last)
    fwd_sum = sum_all(jnp.sum(fwd_gated * fwd_gated, axis=1)[None])
    fwd_inverse = lax.rsqrt(fwd_sum[0] / INNER + 1e-05)[:, None]
    mixed = jnp.dot(fwd_all, local_out, preferred_element_type=jnp.float32) * fwd_inverse
    section_out = (input_rows.astype(jnp.float32) + mixed).astype(jnp.bfloat16)
    next_act = from_behind(section_out, "section", 1)

    normed = (values * scales).astype(jnp.bfloat16)
    d_normed = times_transposed(round_xz, local_xz)
    d_normed = d_normed + jnp.dot(round_bcdt, local_bcdt, preferred_element_type=jnp.float32)
    d_norm_in = scales * d_normed - values * (scales * scales * scales) * inner_sum / D
    d_input = (cot_rows.astype(jnp.float32) + d_norm_in).astype(jnp.bfloat16)
    prev_grad = from_behind(d_input, "section", -1)

    grad_out = transposed_times(gather_cols(mixed_in, round_last)[0], cot_rows)
    grad_xz = transposed_times(normed, round_xz)
    grad_bcdt = transposed_times(round_bcdt, normed)
    return (next_act[None], prev_grad[None], grad_xz[None], grad_bcdt[None], grad_out[None])


BF16 = jnp.bfloat16
F32 = jnp.float32
MESH_ID = pl.DeviceIdType.MESH
NN = (((1,), (0,)), ((), ()))
NT = (((1,), (1,)), ((), ()))
TN = (((0,), (0,)), ((), ()))


def dot1(a, b, dims):
    return lax.dot_general(a, b, dims, preferred_element_type=F32)


def dot_full(a, b, dims):
    return lax.dot_general(
        a, b, dims, precision=lax.Precision.HIGHEST, preferred_element_type=F32
    )


def halves(x):
    high = x.astype(BF16)
    return high, (x - high.astype(F32)).astype(BF16)


def dot3(a, b, dims):
    a_high, a_low = halves(a)
    b_high, b_low = halves(b)
    return dot1(a_high, b_high, dims) + (dot1(a_high, b_low, dims) + dot1(a_low, b_high, dims))


def sigmoid(x):
    return 1.0 / (1.0 + jnp.exp(-x))


def d_silu(x, s):
    return s * (1.0 + x * (1.0 - s))


def rows_of(shape):
    return lax.broadcasted_iota(jnp.int32, shape, 0)


def lanes_of(shape):
    return lax.broadcasted_iota(jnp.int32, shape, 1)


def conv_rows(v, taps):
    row = rows_of(v.shape)
    out = taps[KCONV - 1 : KCONV] * v
    for s in range(1, KCONV):
        moved = jnp.where(row >= s, pltpu.roll(v, s, 0), 0.0)
        out = out + taps[KCONV - 1 - s : KCONV - s] * moved
    return out


def conv_rows_back(d, taps):
    row = rows_of(d.shape)
    out = taps[KCONV - 1 : KCONV] * d
    for s in range(1, KCONV):
        moved = jnp.where(row < SEQ - s, pltpu.roll(d, SEQ - s, 0), 0.0)
        out = out + taps[KCONV - 1 - s : KCONV - s] * moved
    return out


def as_column(row):
    return jnp.broadcast_to(row, (SEQ, SEQ)).T


def row_sums(values):
    return dot_full(jnp.ones((8, values.shape[1]), F32), values, NT)


def wide(col, n):
    return jnp.concatenate([col] * n, axis=1)


def scratch_table():
    dma = pltpu.SemaphoreType.DMA
    vm = pltpu.VMEM
    table = dict(
        w=vm((16, 512, 512), BF16),
        wo=vm((16, 256, 512), BF16),
        wbc=vm((384, 512), BF16),
        x2=vm((2, SEQ, 512), BF16),
        xzd_s=vm((2, 2, 4, SEQ, 512), BF16),
        xzd_r=vm((2, 2, 4, SEQ, 512), BF16),
        xzy_s=vm((2, 4, SEQ, 512), BF16),
        xzy_r=vm((2, 4, SEQ, 512), BF16),
        md_s=vm((2, 4, SEQ, 256), BF16),
        md_r=vm((2, 4, SEQ, 256), BF16),
        my_s=vm((4, SEQ, 256), BF16),
        my_r=vm((4, SEQ, 256), BF16),
        smd_s=vm((SEQ, 384), F32),
        smd_r=vm((SEQ, 384), F32),
        smy_s=vm((SEQ, 384), BF16),
        smy_r=vm((SEQ, 384), BF16),
        sm=vm((2, SEQ, 384), F32),
        sq=vm((4, 8, SEQ), F32),
        rs=vm((4, 8, SEQ), F32),
        rf=vm((4, 8, SEQ), F32),
        tg=vm((4, 24, SEQ), F32),
        dsd_s=vm((64, SEQ), F32),
        dsd_r=vm((64, SEQ), F32),
        dsy_s=vm((64, SEQ), F32),
        dsy_r=vm((64, SEQ), F32),
        ds_tot=vm((2, 64, SEQ), F32),
        ds_acc=vm((2, 64, SEQ), F32),
        ga_round=vm((4, 4, SEQ, 512), BF16),
        ga_mix=vm((4, 4, SEQ, 256), BF16),
        ga_fwd=vm((4, 4, SEQ, 256), BF16),
        big_l=vm((16, SEQ, SEQ), F32),
        xc=vm((8, SEQ, SEQ), F32),
        ys=vm((8, SEQ, SEQ), F32),
        gz=vm((8, SEQ, SEQ), F32),
        dcv=vm((8, SEQ, SEQ), F32),
        dzs=vm((8, SEQ, SEQ), F32),
        dm=vm((8, SEQ, SEQ), F32),
        raw=vm((4, SEQ, 512), F32),
        acc0=vm((SEQ, SEQ), F32),
        acc1=vm((SEQ, SEQ), F32),
        dn=vm((SEQ, 512), F32),
        pdt=vm((SEQ, SEQ), F32),
        dtT=vm((2, 16, SEQ), F32),
        cumT=vm((2, 16, SEQ), F32),
        sgT=vm((16, SEQ), F32),
        negA=vm((16, SEQ), F32),
        dirT=vm((16, SEQ), F32),
        rowT=vm((16, SEQ), F32),
        scores=vm((2, SEQ, SEQ), F32),
        maps=vm((SEQ, 256), BF16),
        dcm=vm((SEQ, 256), F32),
        scale=vm((2, SEQ, SEQ), F32),
        cx=vm((8, KCONV, SEQ), F32),
        gain=vm((8, 1, SEQ), F32),
        dsk=vm((8, 1, SEQ), F32),
        rbc=vm((SEQ, 384), BF16),
        s_w=dma((16,)),
        s_wo=dma((16,)),
        s_out=dma((2,)),
    )
    for name, shape in dict(
        xzd=(2, 2, 4), xzy=(2, 4), md=(2, 4), my=(4,), smd=(1,), smy=(1,), smt=(1,), sq=(3,), rs=(3,),
        rf=(3,), tg=(3,), dsd=(1,), dsy=(1,), dst=(1,), ry=(4,), rd=(4,), rw=(4,), my2=(4,), md2=(4,),
        mw=(4,), fy=(4,), fd=(4,), fw=(4,),
    ).items():
        table["a_" + name] = dma(shape)
        table["b_" + name] = dma(shape)
    return table


class Names:
    pass


def chain_kernel(names, *refs):
    (saved, act, cot, wxz_h, wbc_in, wout_h, convx, convbc, dtb, alog, dskip, gain_in,
     round_o, mixed_o, normed_o, rbc_o, dinput_o, secout_o) = refs[:18]
    v = Names()
    for name, ref in zip(names, refs[18:]):
        setattr(v, name, ref)

    me = lax.axis_index("dp")
    core = lax.rem(me, 2)
    mate = me + 1 - 2 * core
    ypeer = me + 2 - 4 * (me // 2)
    diag = 3 - me
    peers = (mate, ypeer, diag)

    def remote(src, dst, kind, index, dev):
        return pltpu.make_async_remote_copy(
            src_ref=src,
            dst_ref=dst,
            send_sem=getattr(v, "a_" + kind).at[index],
            recv_sem=getattr(v, "b_" + kind).at[index],
            device_id={"dp": dev},
            device_id_type=MESH_ID,
        )

    def xzd(mb, role, j):
        return remote(v.xzd_s.at[mb, role, j], v.xzd_r.at[mb, role, j], "xzd", (mb, role, j), mate)

    def xzy(mb, j):
        return remote(v.xzy_s.at[mb, j], v.xzy_r.at[mb, j], "xzy", (mb, j), ypeer)

    def md(role, j):
        return remote(v.md_s.at[role, j], v.md_r.at[role, j], "md", (role, j), mate)

    def my(j):
        return remote(v.my_s.at[j], v.my_r.at[j], "my", (j,), ypeer)

    def smd():
        return remote(v.smd_s, v.smd_r, "smd", (0,), mate)

    def smy():
        return remote(v.smy_s, v.smy_r, "smy", (0,), ypeer)

    def smt(mb):
        return remote(v.sm.at[mb], v.sm.at[mb], "smt", (0,), mate)

    def spread(buf, kind, i, slot):
        return remote(buf.at[slot], buf.at[slot], kind, (i,), peers[i])

    def spread_start(buf, kind):
        for i in range(3):
            spread(buf, kind, i, me).start()

    def spread_wait(buf, kind):
        for i in range(3):
            spread(buf, kind, i, peers[i]).wait_recv()

    def dsd():
        return remote(v.dsd_s, v.dsd_r, "dsd", (0,), mate)

    def dsy():
        return remote(v.dsy_s, v.dsy_r, "dsy", (0,), ypeer)

    def dst(half):
        return remote(v.ds_tot.at[half], v.ds_tot.at[half], "dst", (0,), mate)

    def gather(buf, kind, q, j, dev):
        return remote(buf.at[q, j], buf.at[q, j], kind, (j,), dev)

    def load_w(i):
        cols = pl.ds(pl.multiple_of(i * 512, 512), 512)
        return pltpu.make_async_copy(wxz_h.at[:, cols], v.w.at[i], v.s_w.at[i])

    def load_wo(i):
        return pltpu.make_async_copy(
            wout_h.at[pl.ds(pl.multiple_of(i * 256, 256), 256)], v.wo.at[i], v.s_wo.at[i]
        )

    def loop(fn, n=4):
        def step(j, carry):
            fn(j)
            return carry
        lax.fori_loop(0, n, step, 0)

    for q in (diag, ypeer):
        loop(lambda j: load_w(4 * q + j).start())
    for q in (diag, ypeer):
        loop(lambda j: load_wo(4 * q + j).start())
    for q in (mate, me):
        loop(lambda j: load_w(4 * q + j).start())
    for q in (mate, me):
        loop(lambda j: load_wo(4 * q + j).start())

    barrier = pltpu.get_barrier_semaphore()
    for peer in peers:
        pl.semaphore_signal(barrier, 1, device_id={"dp": peer}, device_id_type=MESH_ID)

    v.wbc[:320] = wbc_in[...]
    v.wbc[320:] = jnp.zeros((64, 512), BF16)
    v.x2[0] = saved[...]
    v.x2[1] = act[...]
    v.smd_s[...] = dot1(v.x2[1 - core], v.wbc[...], NT)
    pl.semaphore_wait(barrier, 3)
    smd().start()

    def xz_first(j):
        load_w(4 * diag + j).wait()
        v.xzd_s[0, 0, j] = dot1(saved[...], v.w[4 * diag + j], NN).astype(BF16)
        xzd(0, 0, j).start()

    loop(xz_first)
    squares = []
    for x_ref in (saved, act):
        wide_x = x_ref[...].astype(F32)
        squares.append(row_sums(wide_x * wide_x))
    v.sq[me] = jnp.where(rows_of((8, SEQ)) == 0, squares[0], squares[1])
    spread_start(v.sq, "sq")

    own_small = dot1(v.x2[core], v.wbc[...], NT)
    smd().wait_recv()
    own_small = own_small + v.smd_r[...]
    v.smy_s[...] = own_small.astype(BF16)
    smy().start()
    v.sm[core] = own_small

    def xz_sum(mb, x_ref):
        def fn(j):
            part = dot1(x_ref[...], v.w[4 * ypeer + j], NN)
            xzd(mb, 0, j).wait_recv()
            v.xzy_s[mb, j] = (part + v.xzd_r[mb, 0, j].astype(F32)).astype(BF16)
        return fn

    def xz_back(j):
        load_w(4 * ypeer + j).wait()
        xz_sum(0, saved)(j)
        xzy(0, j).start()

    loop(xz_back)

    def m_first(j):
        load_wo(4 * diag + j).wait()
        v.md_s[0, j] = dot1(cot[...], v.wo[4 * diag + j], NT).astype(BF16)
        md(0, j).start()

    loop(m_first)

    def xz_mate(j):
        load_w(4 * mate + j).wait()
        v.xzd_s[0, 1, j] = dot1(saved[...], v.w[4 * mate + j], NN).astype(BF16)
        xzd(0, 1, j).start()

    loop(xz_mate)

    def m_sum(j):
        load_wo(4 * ypeer + j).wait()
        part = dot1(cot[...], v.wo[4 * ypeer + j], NT)
        md(0, j).wait_recv()
        v.my_s[j] = (part + v.md_r[0, j].astype(F32)).astype(BF16)

    loop(m_sum)

    def m_mate(j):
        load_wo(4 * mate + j).wait()
        v.md_s[1, j] = dot1(cot[...], v.wo[4 * mate + j], NT).astype(BF16)
        md(1, j).start()

    loop(m_mate)

    smy().wait_recv()
    v.sm[core] = v.sm[core] + v.smy_r[...].astype(F32)
    smt(core).start()

    expand = (lanes_of((16, 1024)) // HEAD_DIM == rows_of((16, 1024))).astype(F32)
    skip_wide = dot_full(dskip[...], expand, NN)
    for p in range(8):
        cols = slice(128 * p, 128 * p + 128)
        v.cx[p] = convx[:, cols]
        v.gain[p] = gain_in[:, cols]
        v.dsk[p] = skip_wide[:, cols]
    bias_col = jnp.broadcast_to(dtb[...], (SEQ, 16)).T
    v.negA[...] = -jnp.exp(jnp.broadcast_to(alog[...], (SEQ, 16)).T)
    row_id = rows_of((SEQ, SEQ))
    lane_id = lanes_of((SEQ, SEQ))
    causal = row_id >= lane_id
    low = lane_id < HEAD_DIM

    spread_wait(v.sq, "sq")
    total_sq = v.sq[0] + v.sq[1] + v.sq[2] + v.sq[3]
    for mb in range(2):
        v.scale[mb] = lax.rsqrt(as_column(total_sq[mb : mb + 1]) / D + 1e-05)

    smt(1 - core).wait_recv()

    def prepare(mb):
        scale = v.scale[mb]
        small = v.sm[mb] * wide(scale, 3)
        conv = conv_rows(small[:, :MAPS], convbc[...])
        sig = sigmoid(conv)
        maps = (conv * sig).astype(BF16)
        v.scores[mb] = dot1(maps[:, NSTATE:], maps[:, :NSTATE], NT)
        if mb == 0:
            v.maps[...] = maps
            v.dcm[...] = d_silu(conv, sig)
        v.pdt[...] = small[:, MAPS:].T
        logits = v.pdt[pl.ds(pl.multiple_of(16 * me, 16), 16)] + bias_col
        steps = jnp.maximum(logits, 0.0) + jnp.log1p(jnp.exp(-jnp.abs(logits)))
        if mb == 0:
            v.sgT[...] = sigmoid(logits)
        v.dtT[mb] = steps
        v.cumT[mb] = dot_full(
            steps * v.negA[...], (row_id <= lane_id).astype(F32), NN
        )

    prepare(0)

    def split_pair(first, second):
        head_x = jnp.where(low, first, pltpu.roll(second, 64, 1))
        head_z = jnp.where(low, pltpu.roll(first, 64, 1), second)
        return head_x, head_z

    def mix(mb, pair, block, save):
        scale = v.scale[mb]
        x, z = split_pair(block[:, :128] * scale, block[:, 128:] * scale)
        conv = conv_rows(x, v.cx[pair])
        sig = sigmoid(conv)
        xc = conv * sig
        sig_z = sigmoid(z)
        gate = z * sig_z
        weights = []
        for k in range(2):
            head = pl.ds(2 * pair + k, 1)
            row = v.cumT[mb, head]
            decay = jnp.exp(jnp.where(causal, as_column(row) - row, -1e30))
            if save:
                v.big_l[2 * pair + k] = decay
            weights.append(decay * v.scores[mb] * v.dtT[mb, head])
        stacked = jnp.concatenate([jnp.where(low, xc, 0.0), jnp.where(low, 0.0, xc)], axis=0)
        y = dot3(jnp.concatenate(weights, axis=1), stacked, NN)
        if save:
            v.xc[pair] = xc
            v.ys[pair] = y
            v.gz[pair] = gate
            v.dcv[pair] = d_silu(conv, sig)
            v.dzs[pair] = d_silu(z, sig_z)
        return (y + v.dsk[pair] * xc) * gate

    def raw_block(mb, x_ref, j):
        return (
            dot1(x_ref[...], v.w[4 * me + j], NN)
            + v.xzd_r[mb, 1, j].astype(F32)
            + v.xzy_r[mb, j].astype(F32)
        )

    v.acc0[...] = jnp.zeros((SEQ, SEQ), F32)

    def stage_a(j):
        load_w(4 * me + j).wait()
        xzd(0, 1, j).wait_recv()
        xzy(0, j).wait_recv()
        my(j).start()
        raw = raw_block(0, saved, j)
        v.raw[j] = raw
        for k in range(2):
            gated = mix(0, 2 * j + k, raw[:, 256 * k : 256 * k + 256], True)
            v.acc0[...] += gated * gated

    loop(stage_a)

    def fwd_first(j):
        v.xzd_s[1, 0, j] = dot1(act[...], v.w[4 * diag + j], NN).astype(BF16)
        xzd(1, 0, j).start()

    def fwd_mate(j):
        v.xzd_s[1, 1, j] = dot1(act[...], v.w[4 * mate + j], NN).astype(BF16)
        xzd(1, 1, j).start()

    loop(fwd_first)
    loop(fwd_mate)
    loop(xz_sum(1, act))

    v.acc1[...] = jnp.zeros((SEQ, SEQ), F32)

    def stage_b(j):
        load_wo(4 * me + j).wait()
        md(1, j).wait_recv()
        my(j).wait_recv()
        xzy(1, j).start()
        d_mixed = (
            dot1(cot[...], v.wo[4 * me + j], NT)
            + v.md_r[1, j].astype(F32)
            + v.my_r[j].astype(F32)
        )
        for k in range(2):
            pair = 2 * j + k
            part = d_mixed[:, 128 * k : 128 * k + 128]
            v.dm[pair] = part
            gated = (v.ys[pair] + v.dsk[pair] * v.xc[pair]) * v.gz[pair]
            v.acc1[...] += part * v.gain[pair] * gated

    loop(stage_b)

    v.rs[me] = jnp.where(
        rows_of((8, SEQ)) == 0, row_sums(v.acc0[...]), row_sums(v.acc1[...])
    )
    spread_start(v.rs, "rs")
    prepare(1)
    for k in range(4):
        cols = slice(128 * k, 128 * k + 128)
        normed = (saved[:, cols].astype(F32) * v.scale[0]).astype(BF16)
        normed_o[cols] = normed.astype(F32).T.astype(BF16)
    spread_wait(v.rs, "rs")
    total_rs = v.rs[0] + v.rs[1] + v.rs[2] + v.rs[3]
    v.acc0[...] = lax.rsqrt(as_column(total_rs[0:1]) / INNER + 1e-05)
    v.acc1[...] = as_column(total_rs[1:2]) / INNER

    v.pdt[...] = jnp.zeros((SEQ, SEQ), F32)
    v.ds_acc[...] = jnp.zeros((2, 64, SEQ), F32)
    head_rows = (
        lanes_of((8, SEQ)) // HEAD_DIM == rows_of((8, SEQ))
    ).astype(F32)

    def stage_c(j):
        inverse = v.acc0[...]
        lower = inverse * inverse * inverse * v.acc1[...]
        for k in range(2):
            pair = 2 * j + k
            xc = v.xc[pair]
            y = v.ys[pair]
            gate = v.gz[pair]
            skip = v.dsk[pair]
            gained = inverse * v.gain[pair]
            y_full = y + skip * xc
            gated = y_full * gate
            v.ga_mix[me, j, :, 128 * k : 128 * k + 128] = (gated * gained).astype(BF16)
            d_gated = gained * v.dm[pair] - gated * lower
            d_y = d_gated * gate
            d_gate = d_gated * y_full
            d_ys = jnp.concatenate([jnp.where(low, d_y, 0.0), jnp.where(low, 0.0, d_y)], axis=0)
            d_w = dot3(d_ys, xc, NT)
            scores = v.scores[0]
            weights = []
            d_scores = None
            for h in range(2):
                head = pl.ds(2 * pair + h, 1)
                decay = v.big_l[2 * pair + h]
                steps = v.dtT[0, head]
                scored = decay * scores
                weights.append(scored * steps)
                d_head = d_w[SEQ * h : SEQ * h + SEQ]
                term = d_head * (decay * steps)
                d_scores = term if d_scores is None else d_scores + term
                v.dirT[head] = jnp.sum(d_head * scored, axis=0, keepdims=True)
            v.ds_acc[0] += d_scores[:64]
            v.ds_acc[1] += d_scores[64:]
            sums = dot_full(head_rows, d_y * y, NT)
            v.rowT[pl.ds(2 * pair, 1)] = sums[0:1]
            v.rowT[pl.ds(2 * pair + 1, 1)] = sums[1:2]
            d_xc = dot3(jnp.concatenate(weights, axis=0), d_ys, TN) + skip * d_y
            d_x = conv_rows_back(d_xc * v.dcv[pair], v.cx[pair])
            d_z = d_gate * v.dzs[pair]
            first, second = split_pair(d_x, d_z)
            first = first.astype(BF16)
            second = second.astype(BF16)
            v.ga_round[me, j, :, 256 * k : 256 * k + 128] = first
            v.ga_round[me, j, :, 256 * k + 128 : 256 * k + 256] = second
            v.pdt[...] += (
                first.astype(F32) * v.raw[j, :, 256 * k : 256 * k + 128]
                + second.astype(F32) * v.raw[j, :, 256 * k + 128 : 256 * k + 256]
            )
        gather(v.ga_round, "ry", me, j, ypeer).start()
        gather(v.ga_round, "rd", me, j, mate).start()
        gather(v.ga_mix, "my2", me, j, ypeer).start()
        gather(v.ga_mix, "md2", me, j, mate).start()

    loop(stage_c)

    v.dsd_s[...] = v.ds_acc[1 - core]
    dsd().start()
    d_cum = v.rowT[...] - v.dtT[0] * v.dirT[...]
    d_a = dot_full(d_cum, (row_id >= lane_id).astype(F32), NN)
    v.tg[me, 0:16] = (v.dirT[...] + v.negA[...] * d_a) * v.sgT[...]
    v.tg[me, 16:24] = row_sums(v.pdt[...])
    spread_start(v.tg, "tg")
    dsd().wait_recv()
    v.dsy_s[...] = v.ds_acc[core] + v.dsd_r[...]
    dsy().start()

    v.acc0[...] = jnp.zeros((SEQ, SEQ), F32)

    def stage_e(j):
        xzd(1, 1, j).wait_recv()
        xzy(1, j).wait_recv()
        raw = raw_block(1, act, j)
        for k in range(2):
            pair = 2 * j + k
            gated = mix(1, pair, raw[:, 256 * k : 256 * k + 256], False)
            v.acc0[...] += gated * gated
            v.ga_fwd[me, j, :, 128 * k : 128 * k + 128] = (gated * v.gain[pair]).astype(BF16)
        gather(v.ga_fwd, "fy", me, j, ypeer).start()
        gather(v.ga_fwd, "fd", me, j, mate).start()

    loop(stage_e)
    v.rf[me] = row_sums(v.acc0[...])
    spread_start(v.rf, "rf")

    v.dn[...] = jnp.zeros((SEQ, 512), F32)

    def add_dn(q, j):
        v.dn[...] += dot1(v.ga_round[q, j], v.w[4 * q + j], NT)

    loop(lambda j: add_dn(me, j))

    dsy().wait_recv()
    v.ds_tot[core] = v.dsy_s[...] + v.dsy_r[...]
    dst(core).start()

    def add_mate(j):
        gather(v.ga_round, "rd", mate, j, mate).wait_recv()
        add_dn(mate, j)

    loop(add_mate)
    dst(1 - core).wait_recv()
    d_scores = jnp.concatenate([v.ds_tot[0], v.ds_tot[1]], axis=0)
    ds_high, ds_low = halves(d_scores)
    maps = v.maps[...]
    d_input_map = dot1(ds_high, maps[:, NSTATE:], TN) + dot1(ds_low, maps[:, NSTATE:], TN)
    d_output_map = dot1(ds_high, maps[:, :NSTATE], NN) + dot1(ds_low, maps[:, :NSTATE], NN)
    d_maps = jnp.concatenate([d_input_map, d_output_map], axis=1)
    d_pre = conv_rows_back(d_maps * v.dcm[...], convbc[...])
    v.rbc[:, :MAPS] = d_pre.astype(BF16)
    spread_wait(v.tg, "tg")
    v.pdt[...] = jnp.zeros((SEQ, SEQ), F32)
    for q in range(4):
        v.pdt[16 * q : 16 * q + 16] = v.tg[q, 0:16]
    v.rbc[:, MAPS:] = v.pdt[...].T.astype(BF16)
    rbc_o[...] = v.rbc[...]
    product = v.rbc[...].astype(F32) * v.sm[0]
    inner = row_sums(product[:, :128] + product[:, 128:256] + product[:, 256:])
    inner = inner + v.tg[0, 16:24] + v.tg[1, 16:24] + v.tg[2, 16:24] + v.tg[3, 16:24]
    v.acc1[...] = as_column(inner[0:1]) / D
    v.dn[...] += dot1(v.rbc[...], v.wbc[...], NN)

    def pass_on(j):
        gather(v.ga_round, "ry", ypeer, j, ypeer).wait_recv()
        gather(v.ga_round, "rw", ypeer, j, mate).start()
        add_dn(ypeer, j)

    loop(pass_on)

    def pass_mix(j):
        gather(v.ga_mix, "my2", ypeer, j, ypeer).wait_recv()
        gather(v.ga_mix, "mw", ypeer, j, mate).start()

    loop(pass_mix)

    def add_diag(j):
        gather(v.ga_round, "rw", diag, j, mate).wait_recv()
        add_dn(diag, j)

    loop(add_diag)
    round_copy = pltpu.make_async_copy(v.ga_round, round_o, v.s_out.at[0])
    round_copy.start()
    for k in range(4):
        cols = slice(128 * k, 128 * k + 128)
        scale = v.scale[0]
        d_in = scale * v.dn[:, cols] - saved[:, cols].astype(F32) * (
            scale * scale * scale
        ) * v.acc1[...]
        dinput_o[:, cols] = (cot[:, cols].astype(F32) + d_in).astype(BF16)

    v.dn[...] = jnp.zeros((SEQ, 512), F32)

    def add_out(q, j):
        v.dn[...] += dot1(v.ga_fwd[q, j], v.wo[4 * q + j], NN)

    loop(lambda j: add_out(me, j))

    def out_mate(j):
        gather(v.ga_fwd, "fd", mate, j, mate).wait_recv()
        add_out(mate, j)

    loop(out_mate)
    loop(lambda j: gather(v.ga_mix, "md2", mate, j, mate).wait_recv())
    loop(lambda j: gather(v.ga_mix, "mw", diag, j, mate).wait_recv())
    mixed_copy = pltpu.make_async_copy(v.ga_mix, mixed_o, v.s_out.at[1])
    mixed_copy.start()
    spread_wait(v.rf, "rf")
    total_rf = v.rf[0] + v.rf[1] + v.rf[2] + v.rf[3]
    v.acc0[...] = lax.rsqrt(as_column(total_rf[0:1]) / INNER + 1e-05)

    def out_peer(j):
        gather(v.ga_fwd, "fy", ypeer, j, ypeer).wait_recv()
        gather(v.ga_fwd, "fw", ypeer, j, mate).start()
        add_out(ypeer, j)

    loop(out_peer)

    def out_diag(j):
        gather(v.ga_fwd, "fw", diag, j, mate).wait_recv()
        add_out(diag, j)

    loop(out_diag)
    for k in range(4):
        cols = slice(128 * k, 128 * k + 128)
        mixed = v.dn[:, cols] * v.acc0[...]
        secout_o[:, cols] = (act[:, cols].astype(F32) + mixed).astype(BF16)

    smd().wait_send()
    smy().wait_send()
    smt(core).wait_send()
    dsd().wait_send()
    dsy().wait_send()
    dst(core).wait_send()
    for buf, kind in ((v.sq, "sq"), (v.rs, "rs"), (v.rf, "rf"), (v.tg, "tg")):
        for i in range(3):
            spread(buf, kind, i, me).wait_send()

    def drain(j):
        for mb in range(2):
            for role in range(2):
                xzd(mb, role, j).wait_send()
            xzy(mb, j).wait_send()
        md(0, j).wait_send()
        md(1, j).wait_send()
        my(j).wait_send()
        for buf, kinds in (
            (v.ga_round, ("ry", "rd", "rw")),
            (v.ga_mix, ("my2", "md2", "mw")),
            (v.ga_fwd, ("fy", "fd", "fw")),
        ):
            gather(buf, kinds[0], me, j, ypeer).wait_send()
            gather(buf, kinds[1], me, j, mate).wait_send()
            gather(buf, kinds[2], ypeer, j, mate).wait_send()

    loop(drain)
    round_copy.wait()
    mixed_copy.wait()


def chain(saved, act, cot, wxz, wbc, wout, convx, convbc, dtb, alog, dskip, gain):
    table = scratch_table()
    vm = pl.BlockSpec(memory_space=pltpu.VMEM)
    hbm = pl.BlockSpec(memory_space=pl.ANY)
    shape = jax.ShapeDtypeStruct
    return pl.pallas_call(
        functools.partial(chain_kernel, tuple(table)),
        out_shape=(
            shape((4, 4, SEQ, 512), BF16),
            shape((4, 4, SEQ, 256), BF16),
            shape((512, SEQ), BF16),
            shape((SEQ, 384), BF16),
            shape((SEQ, 512), BF16),
            shape((SEQ, 512), BF16),
        ),
        in_specs=[vm, vm, vm, hbm, vm, hbm, vm, vm, vm, vm, vm, vm],
        out_specs=(hbm, hbm, vm, vm, vm, vm),
        scratch_shapes=list(table.values()),
        compiler_params=pltpu.CompilerParams(
            collective_id=0, has_side_effects=True, vmem_limit_bytes=54 * 1024 * 1024
        ),
        cost_estimate=pl.CostEstimate(
            flops=4_300_000_000, bytes_accessed=18_000_000, transcendentals=2_000_000
        ),
        name="chain",
    )(saved, act, cot, wxz, wbc, wout, convx, convbc, dtb, alog, dskip, gain)


def grads_kernel(round_ref, mixed_ref, normed_ref, rbc_ref, cot_ref, xz_o, out_o, bc_o):
    for k in range(2):
        xz_o[:, 512 * k : 512 * k + 512] = dot1(normed_ref[...], round_ref[k], NN)
        out_o[256 * k : 256 * k + 256] = dot1(mixed_ref[k], cot_ref[...], TN)

    @pl.when(pl.program_id(0) == 0)
    def _():
        bc_o[...] = dot1(rbc_ref[:, :320], normed_ref[...], (((0,), (1,)), ((), ())))


def grads(round_all, mixed_all, normed, rbc, cot):
    shape = jax.ShapeDtypeStruct
    return pl.pallas_call(
        grads_kernel,
        grid=(8,),
        out_shape=(
            shape((512, 8192), F32),
            shape((4096, 512), F32),
            shape((320, 512), F32),
        ),
        in_specs=[
            pl.BlockSpec((2, SEQ, 512), lambda i: (i, 0, 0)),
            pl.BlockSpec((2, SEQ, 256), lambda i: (i, 0, 0)),
            pl.BlockSpec((512, SEQ), lambda i: (0, 0)),
            pl.BlockSpec((SEQ, 384), lambda i: (0, 0)),
            pl.BlockSpec((SEQ, 512), lambda i: (0, 0)),
        ],
        out_specs=(
            pl.BlockSpec((512, 1024), lambda i: (0, i)),
            pl.BlockSpec((512, 512), lambda i: (i, 0)),
            pl.BlockSpec((320, 512), lambda i: (0, 0)),
        ),
        compiler_params=pltpu.CompilerParams(vmem_limit_bytes=32 * 1024 * 1024),
        cost_estimate=pl.CostEstimate(
            flops=1_700_000_000, bytes_accessed=29_000_000, transcendentals=0
        ),
        name="grads",
    )(round_all.reshape(16, SEQ, 512), mixed_all.reshape(16, SEQ, 256), normed, rbc, cot)


def per_device_four(
    act_in,
    saved_act,
    cotangent,
    weight_xz,
    weight_bcdt,
    weight_out,
    conv_x,
    conv_bc,
    dt_bias,
    a_log,
    d_skip,
    norm_gain,
):
    round_all, mixed_all, normed, rbc, d_input, section_out = chain(
        saved_act[0],
        act_in[0],
        cotangent[0],
        weight_xz[0],
        weight_bcdt[0],
        weight_out[0],
        conv_x[0],
        conv_bc[0],
        dt_bias,
        a_log,
        d_skip,
        norm_gain,
    )
    next_act = from_behind(section_out, "section", 1)
    prev_grad = from_behind(d_input, "section", -1)
    grad_xz, grad_out, grad_bcdt = grads(round_all, mixed_all, normed, rbc, cotangent[0])
    return (next_act[None], prev_grad[None], grad_xz[None], grad_bcdt[None], grad_out[None])


def solution(mesh):
    return jax.shard_map(
        per_device_four if mesh.shape["dp"] == 4 else per_device,
        mesh=mesh,
        in_specs=(
            P("section", None, "dp"),
            P("section", None, "dp"),
            P("section", None, "dp"),
            P("section", "dp", None),
            P("section", None, "dp"),
            P("section", None, "dp"),
            P("section", None, "dp"),
            P("section", None, None),
            P("section", "dp"),
            P("section", "dp"),
            P("section", "dp"),
            P("section", "dp"),
        ),
        out_specs=(
            P("section", None, "dp"),
            P("section", None, "dp"),
            P("section", "dp", None),
            P("section", None, "dp"),
            P("section", None, "dp"),
        ),
        check_vma=False,
    )
```

```python
import functools

import jax
import jax.numpy as jnp
from jax import lax
from jax.experimental import pallas as pl
from jax.experimental.pallas import tpu as pltpu
from jax.sharding import PartitionSpec as P

D = 2048
HEAD_DIM = 64
NSTATE = 128
HEADS = 64
SEQ = 128
INNER = 4096
KCONV = 4
MAPS = 2 * NSTATE


def from_behind(x, axis, by):
    length = lax.axis_size(axis)
    return lax.ppermute(x, axis, [(i, (i + by) % length) for i in range(length)])


def swap(x, mask):
    length = lax.axis_size("dp")
    return lax.ppermute(x, "dp", [(i, i ^ mask) for i in range(length)])


def masks():
    length = lax.axis_size("dp")
    out = []
    bit = 1
    while bit < length:
        out.append(bit)
        bit *= 2
    return out


def sum_all(x):
    for bit in masks():
        x = x + swap(x, bit)
    return x


def tied(x, other):
    return lax.optimization_barrier((x, other))[0]


def sum_first(part):
    length = lax.axis_size("dp")
    came = {j - 1: swap(part(j).astype(jnp.bfloat16), 1) for j in range(1, length, 2)}
    return {j: part(j) + came[j].astype(jnp.float32) for j in sorted(came, reverse=True)}


def sum_rest(held, after=None):
    first = begun = None
    for bit in masks()[1:]:
        sent = {j: held[j].astype(jnp.bfloat16) for j in held if j & bit}
        if after is not None and first is None:
            sent = {j: tied(x, after) for j, x in sent.items()}
        came = {j ^ bit: swap(x, bit) for j, x in sent.items()}
        if first is None:
            first = came[0]
            begun = sent[bit]
        held = {j: held[j] + came[j].astype(jnp.float32) for j in came}
    return held[0], first, begun


def sum_both(x, after):
    me = lax.axis_index("dp")
    odd = (me & 1) != 0
    x = x + swap(x, 1)
    mine = tied(jnp.where(odd, x[SEQ:], x[:SEQ]), after)
    for bit in masks()[1:]:
        mine = mine + swap(mine, bit)
    other = swap(mine, 1)
    return jnp.where(odd, other, mine), jnp.where(odd, mine, other)


def gather_cols(block, after=None):
    me = lax.axis_index("dp")
    length = lax.axis_size("dp")
    if after is not None:
        block = tied(block, after)
    held = [block]
    order = [0]
    for bit in reversed(masks()):
        held = held + [swap(b, bit) for b in held]
        order = order + [j ^ bit for j in order]
    by_mask = {j: b for j, b in zip(order, held)}
    level = [by_mask[j] for j in range(length)]
    for bit in masks():
        flip = (me & bit) != 0
        level = [jnp.where(flip, level[j ^ bit], level[j]) for j in range(length)]
    return jnp.concatenate(level, axis=1), held[-1]


def causal_conv(values, kernel_taps):
    kernel = kernel_taps.shape[0]
    length = values.shape[0]
    padded = jnp.pad(values, ((kernel - 1, 0), (0, 0)))
    running = jnp.zeros_like(values)
    for offset in range(kernel):
        running = running + kernel_taps[offset] * padded[offset : offset + length]
    return running


def mixer(proj_x, proj_z, proj_dt, scores, conv_taps, dt_offset, log_rate, skip_gain):
    length, width = proj_x.shape
    nheads = dt_offset.shape[0]
    head_width = width // nheads
    xconv = jax.nn.silu(causal_conv(proj_x, conv_taps))
    steps = jax.nn.softplus(proj_dt + dt_offset)
    position = jnp.arange(length)
    causal = position[:, None] >= position[None, :]
    cumul = jnp.dot(
        causal.astype(jnp.float32), steps * -jnp.exp(log_rate), precision=lax.Precision.HIGHEST
    )
    heads_cum = cumul.T
    spread = heads_cum[:, :, None] - heads_cum[:, None, :]
    decay = jnp.where(causal[None], jnp.exp(jnp.where(causal[None], spread, 0.0)), 0.0)
    weights = decay * scores[None] * steps.T[:, None, :]
    heads_in = xconv.reshape(length, nheads, head_width)
    result = jnp.einsum("hts,shp->thp", weights, heads_in, precision=lax.Precision.HIGH)
    result = result + skip_gain[None, :, None] * heads_in
    gate_in = jax.nn.silu(proj_z.reshape(length, nheads, head_width))
    return (result * gate_in).reshape(length, width)


def times_transposed(left, right):
    return lax.dot_general(
        left, right, (((1,), (1,)), ((), ())), preferred_element_type=jnp.float32
    )


def transposed_times(left, right):
    return lax.dot_general(
        left, right, (((0,), (0,)), ((), ())), preferred_element_type=jnp.float32
    )


def per_device(
    act_in,
    saved_act,
    cotangent,
    weight_xz,
    weight_bcdt,
    weight_out,
    conv_x,
    conv_bc,
    dt_bias,
    a_log,
    d_skip,
    norm_gain,
):
    input_rows = act_in[0]
    saved_rows = saved_act[0]
    cot_rows = cotangent[0]
    local_xz = weight_xz[0]
    local_bcdt = weight_bcdt[0]
    local_out = weight_out[0]
    taps_x = conv_x[0]
    taps_bc = conv_bc[0]
    dt_offset = dt_bias[0]
    log_rate = a_log[0]
    skip_gain = d_skip[0]
    gain_local = norm_gain[0]
    own_heads = dt_offset.shape[0]
    me = lax.axis_index("dp")
    head_first = me * own_heads
    width = own_heads * HEAD_DIM

    def whole_act(pre_part):
        return jax.nn.silu(causal_conv(pre_part, taps_bc))

    both = jnp.concatenate([saved_rows, input_rows], axis=0)
    both_values = both.astype(jnp.float32)
    squares = jnp.sum(both_values * both_values, axis=1, keepdims=True)
    def xz_part(j):
        cols = lax.dynamic_slice_in_dim(local_xz, (me ^ j) * 2 * width, 2 * width, 1)
        return jnp.dot(both, cols, preferred_element_type=jnp.float32)

    held_xz = sum_first(xz_part)
    back_raw, back_first, back_begun = sum_rest({j: x[:SEQ] for j, x in held_xz.items()})
    back_small, forward_small = sum_both(
        jnp.concatenate([times_transposed(both, local_bcdt), squares], axis=1), back_begun
    )

    def mixed_part(j):
        taken = lax.dynamic_slice_in_dim(local_out, (me ^ j) * width, width, 0)
        return times_transposed(cot_rows, taken)

    d_mixed = sum_rest(sum_first(mixed_part), back_begun)[0]
    forward_raw = sum_rest({j: x[SEQ:] for j, x in held_xz.items()}, back_first)[0]

    def project(rows, small, raw_xz):
        raw_cols = small[:, : MAPS + HEADS]
        scales = lax.rsqrt(small[:, MAPS + HEADS :] / D + 1e-05)
        return (rows.astype(jnp.float32), scales, raw_xz, raw_cols)

    back_proj = project(saved_rows, back_small, back_raw)
    forward_proj = project(input_rows, forward_small, forward_raw)

    def gate_parts(projected):
        values, scales, raw_xz, raw_cols = projected
        own_xz = raw_xz * scales
        whole_cols = raw_cols * scales
        pre_part = whole_cols[:, :MAPS]
        maps = whole_act(pre_part).astype(jnp.bfloat16)
        own_dt = lax.dynamic_slice_in_dim(whole_cols[:, MAPS:], head_first, own_heads, 1)
        split_xz = own_xz.reshape(SEQ, own_heads, 2, HEAD_DIM)
        mix_x = split_xz[:, :, 0].reshape(SEQ, width)
        mix_z = split_xz[:, :, 1].reshape(SEQ, width)
        scores = times_transposed(maps[:, NSTATE:], maps[:, :NSTATE])

        def local_mix(in_x, in_z, in_dt, in_scores):
            return mixer(in_x, in_z, in_dt, in_scores, taps_x, dt_offset, log_rate, skip_gain)

        gated, mix_back = jax.vjp(local_mix, mix_x, mix_z, own_dt, scores)
        return (gated, mix_back, maps, pre_part)

    values, scales, raw_xz, raw_cols = back_proj
    gated, mix_back, maps, pre_part = gate_parts(back_proj)
    gained = gated * gain_local
    row_sums = sum_all(
        jnp.stack([jnp.sum(gated * gated, axis=1), jnp.sum(d_mixed * gained, axis=1)])
    )
    inverse = lax.rsqrt(row_sums[0] / INNER + 1e-05)[:, None]
    dots = row_sums[1][:, None]
    mixed_in = (gained * inverse).astype(jnp.bfloat16)
    d_gated = inverse * gain_local * d_mixed - gated * (inverse * inverse * inverse) * dots / INNER
    d_px, d_pz, d_pdt, d_scores = mix_back(d_gated)
    own_round = (
        jnp.stack(
            [
                d_px.reshape(SEQ, own_heads, HEAD_DIM),
                d_pz.reshape(SEQ, own_heads, HEAD_DIM),
            ],
            axis=2,
        )
        .reshape(SEQ, own_heads * 2 * HEAD_DIM)
        .astype(jnp.bfloat16)
    )
    round_xz, round_last = gather_cols(own_round)
    inner_own = jnp.sum(own_round.astype(jnp.float32) * raw_xz, axis=1, keepdims=True)
    wide_maps = maps.astype(jnp.float32)
    d_maps = jnp.concatenate(
        [
            jnp.dot(d_scores.T, wide_maps[:, NSTATE:], precision=lax.Precision.HIGH),
            jnp.dot(d_scores, wide_maps[:, :NSTATE], precision=lax.Precision.HIGH),
        ],
        axis=1,
    )
    d_dt_full = lax.dynamic_update_slice_in_dim(
        jnp.zeros((SEQ, HEADS), jnp.float32), d_pdt, head_first, 1
    )
    summed = sum_all(jnp.concatenate([d_maps, d_dt_full, inner_own], axis=1))
    conv_out, conv_back = jax.vjp(whole_act, pre_part)
    d_pre = conv_back(summed[:, :MAPS])[0]
    round_bcdt = jnp.concatenate([d_pre, summed[:, MAPS : MAPS + HEADS]], axis=1).astype(
        jnp.bfloat16
    )
    inner_sum = summed[:, MAPS + HEADS :] + jnp.sum(
        round_bcdt.astype(jnp.float32) * raw_cols, axis=1, keepdims=True
    )

    fwd_gated = gate_parts(forward_proj)[0]
    fwd_all, _ = gather_cols((fwd_gated * gain_local).astype(jnp.bfloat16), round_last)
    fwd_sum = sum_all(jnp.sum(fwd_gated * fwd_gated, axis=1)[None])
    fwd_inverse = lax.rsqrt(fwd_sum[0] / INNER + 1e-05)[:, None]
    mixed = jnp.dot(fwd_all, local_out, preferred_element_type=jnp.float32) * fwd_inverse
    section_out = (input_rows.astype(jnp.float32) + mixed).astype(jnp.bfloat16)
    next_act = from_behind(section_out, "section", 1)

    normed = (values * scales).astype(jnp.bfloat16)
    d_normed = times_transposed(round_xz, local_xz)
    d_normed = d_normed + jnp.dot(round_bcdt, local_bcdt, preferred_element_type=jnp.float32)
    d_norm_in = scales * d_normed - values * (scales * scales * scales) * inner_sum / D
    d_input = (cot_rows.astype(jnp.float32) + d_norm_in).astype(jnp.bfloat16)
    prev_grad = from_behind(d_input, "section", -1)

    grad_out = transposed_times(gather_cols(mixed_in, round_last)[0], cot_rows)
    grad_xz = transposed_times(normed, round_xz)
    grad_bcdt = transposed_times(round_bcdt, normed)
    return (next_act[None], prev_grad[None], grad_xz[None], grad_bcdt[None], grad_out[None])


BF16 = jnp.bfloat16
F32 = jnp.float32
MESH_ID = pl.DeviceIdType.MESH
NN = (((1,), (0,)), ((), ()))
NT = (((1,), (1,)), ((), ()))
TN = (((0,), (0,)), ((), ()))


def dot1(a, b, dims):
    return lax.dot_general(a, b, dims, preferred_element_type=F32)


def dot_full(a, b, dims):
    return lax.dot_general(
        a, b, dims, precision=lax.Precision.HIGHEST, preferred_element_type=F32
    )


def halves(x):
    high = x.astype(BF16)
    return high, (x - high.astype(F32)).astype(BF16)


def dot3(a, b, dims):
    a_high, a_low = halves(a)
    b_high, b_low = halves(b)
    return dot1(a_high, b_high, dims) + (dot1(a_high, b_low, dims) + dot1(a_low, b_high, dims))


def sigmoid(x):
    return 1.0 / (1.0 + jnp.exp(-x))


def d_silu(x, s):
    return s * (1.0 + x * (1.0 - s))


def rows_of(shape):
    return lax.broadcasted_iota(jnp.int32, shape, 0)


def lanes_of(shape):
    return lax.broadcasted_iota(jnp.int32, shape, 1)


def conv_rows(v, taps):
    row = rows_of(v.shape)
    out = taps[KCONV - 1 : KCONV] * v
    for s in range(1, KCONV):
        moved = jnp.where(row >= s, pltpu.roll(v, s, 0), 0.0)
        out = out + taps[KCONV - 1 - s : KCONV - s] * moved
    return out


def conv_rows_back(d, taps):
    row = rows_of(d.shape)
    out = taps[KCONV - 1 : KCONV] * d
    for s in range(1, KCONV):
        moved = jnp.where(row < SEQ - s, pltpu.roll(d, SEQ - s, 0), 0.0)
        out = out + taps[KCONV - 1 - s : KCONV - s] * moved
    return out


def as_column(row):
    return jnp.broadcast_to(row, (SEQ, SEQ)).T


def row_sums(values):
    return dot_full(jnp.ones((8, values.shape[1]), F32), values, NT)


def wide(col, n):
    return jnp.concatenate([col] * n, axis=1)


def scratch_table():
    dma = pltpu.SemaphoreType.DMA
    vm = pltpu.VMEM
    table = dict(
        w=vm((16, 512, 512), BF16),
        wo=vm((16, 256, 512), BF16),
        wbc=vm((384, 512), BF16),
        x2=vm((2, SEQ, 512), BF16),
        cot=vm((SEQ, 512), BF16),
        sec=vm((2, SEQ, 512), BF16),
        normed=vm((512, SEQ), BF16),
        xzd_s=vm((2, 2, 4, SEQ, 512), BF16),
        xzd_r=vm((2, 2, 4, SEQ, 512), BF16),
        xzy_s=vm((2, 4, SEQ, 512), BF16),
        xzy_r=vm((2, 4, SEQ, 512), BF16),
        md_s=vm((2, 4, SEQ, 256), BF16),
        md_r=vm((2, 4, SEQ, 256), BF16),
        my_s=vm((4, SEQ, 256), BF16),
        my_r=vm((4, SEQ, 256), BF16),
        smd_s=vm((SEQ, 384), F32),
        smd_r=vm((SEQ, 384), F32),
        smy_s=vm((SEQ, 384), BF16),
        smy_r=vm((SEQ, 384), BF16),
        sm=vm((2, SEQ, 384), F32),
        sq=vm((4, 8, SEQ), F32),
        rs=vm((4, 8, SEQ), F32),
        rf=vm((4, 8, SEQ), F32),
        tg=vm((4, 24, SEQ), F32),
        dsd_s=vm((64, SEQ), F32),
        dsd_r=vm((64, SEQ), F32),
        dsy_s=vm((64, SEQ), F32),
        dsy_r=vm((64, SEQ), F32),
        ds_tot=vm((2, 64, SEQ), F32),
        ds_acc=vm((2, 64, SEQ), F32),
        ga_round=vm((4, 4, SEQ, 512), BF16),
        ga_mix=vm((4, 4, 256, SEQ), BF16),
        ga_fwd=vm((4, 4, SEQ, 256), BF16),
        big_l=vm((16, SEQ, SEQ), F32),
        xc=vm((8, SEQ, SEQ), F32),
        ys=vm((8, SEQ, SEQ), F32),
        gz=vm((8, SEQ, SEQ), F32),
        dcv=vm((8, SEQ, SEQ), F32),
        dzs=vm((8, SEQ, SEQ), F32),
        dm=vm((8, SEQ, SEQ), F32),
        raw=vm((4, SEQ, 512), F32),
        acc0=vm((SEQ, SEQ), F32),
        acc1=vm((SEQ, SEQ), F32),
        dn=vm((SEQ, 512), F32),
        pdt=vm((SEQ, SEQ), F32),
        dtT=vm((2, 16, SEQ), F32),
        cumT=vm((2, 16, SEQ), F32),
        sgT=vm((16, SEQ), F32),
        negA=vm((16, SEQ), F32),
        dirT=vm((16, SEQ), F32),
        rowT=vm((16, SEQ), F32),
        scores=vm((2, SEQ, SEQ), F32),
        maps=vm((SEQ, 256), BF16),
        dcm=vm((SEQ, 256), F32),
        scale=vm((2, SEQ, SEQ), F32),
        cx=vm((8, KCONV, SEQ), F32),
        gain=vm((8, 1, SEQ), F32),
        dsk=vm((8, 1, SEQ), F32),
        rbc=vm((SEQ, 384), BF16),
        s_w=dma((16,)),
        s_wo=dma((16,)),
        s_in=dma((4,)),
        s_out=dma((10,)),
    )
    for name, shape in dict(
        xzd=(2, 2, 4), xzy=(2, 4), md=(2, 4), my=(4,), smd=(1,), smy=(1,), smt=(1,), sq=(3,), rs=(3,),
        rf=(3,), tg=(3,), dsd=(1,), dsy=(1,), dst=(1,), ry=(4,), rd=(4,), rw=(4,), my2=(4,), md2=(4,),
        mw=(4,), fy=(4,), fd=(4,), fw=(4,), sec=(2,),
    ).items():
        table["a_" + name] = dma(shape)
        table["b_" + name] = dma(shape)
    return table


class Names:
    pass


def chain_kernel(names, *refs):
    (saved_h, act_h, cot_h, wxz_h, wbc_h, wout_h, convx, convbc, dtb, alog, dskip, gain_in,
     round_o, mixed_o, normed_o, rbc_o, prev_o, next_o) = refs[:18]
    v = Names()
    for name, ref in zip(names, refs[18:]):
        setattr(v, name, ref)
    saved, act, cot = v.x2.at[0], v.x2.at[1], v.cot

    me = lax.axis_index("dp")
    core = lax.rem(me, 2)
    mate = me + 1 - 2 * core
    ypeer = me + 2 - 4 * (me // 2)
    diag = 3 - me
    peers = (mate, ypeer, diag)
    sections = lax.axis_size("section")
    place = lax.axis_index("section")
    ahead = lax.rem(place + 1, sections)
    behind = lax.rem(place + sections - 1, sections)

    def remote(src, dst, kind, index, dev):
        return pltpu.make_async_remote_copy(
            src_ref=src,
            dst_ref=dst,
            send_sem=getattr(v, "a_" + kind).at[index],
            recv_sem=getattr(v, "b_" + kind).at[index],
            device_id={"dp": dev},
            device_id_type=MESH_ID,
        )

    def xzd(mb, role, j):
        return remote(v.xzd_s.at[mb, role, j], v.xzd_r.at[mb, role, j], "xzd", (mb, role, j), mate)

    def xzy(mb, j):
        return remote(v.xzy_s.at[mb, j], v.xzy_r.at[mb, j], "xzy", (mb, j), ypeer)

    def md(role, j):
        return remote(v.md_s.at[role, j], v.md_r.at[role, j], "md", (role, j), mate)

    def my(j):
        return remote(v.my_s.at[j], v.my_r.at[j], "my", (j,), ypeer)

    def smd():
        return remote(v.smd_s, v.smd_r, "smd", (0,), mate)

    def smy():
        return remote(v.smy_s, v.smy_r, "smy", (0,), ypeer)

    def smt(mb):
        return remote(v.sm.at[mb], v.sm.at[mb], "smt", (0,), mate)

    def spread(buf, kind, i, slot):
        return remote(buf.at[slot], buf.at[slot], kind, (i,), peers[i])

    def spread_start(buf, kind):
        for i in range(3):
            spread(buf, kind, i, me).start()

    def spread_wait(buf, kind):
        for i in range(3):
            spread(buf, kind, i, peers[i]).wait_recv()

    def dsd():
        return remote(v.dsd_s, v.dsd_r, "dsd", (0,), mate)

    def dsy():
        return remote(v.dsy_s, v.dsy_r, "dsy", (0,), ypeer)

    def dst(half):
        return remote(v.ds_tot.at[half], v.ds_tot.at[half], "dst", (0,), mate)

    def gather(buf, kind, q, j, dev):
        return remote(buf.at[q, j], buf.at[q, j], kind, (j,), dev)

    def send_section(i):
        return pltpu.make_async_remote_copy(
            src_ref=v.sec.at[i],
            dst_ref=(prev_o, next_o)[i],
            send_sem=v.a_sec.at[i],
            recv_sem=v.b_sec.at[i],
            device_id={"section": (behind, ahead)[i]},
            device_id_type=MESH_ID,
        )

    def hand_out(kind, q):
        buf, out = ((v.ga_round, round_o), (v.ga_mix, mixed_o))[kind]
        return pltpu.make_async_copy(buf.at[q], out.at[q], v.s_out.at[4 * kind + q])

    def load_w(i):
        cols = pl.ds(pl.multiple_of(i * 512, 512), 512)
        return pltpu.make_async_copy(wxz_h.at[:, cols], v.w.at[i], v.s_w.at[i])

    def load_wo(i):
        return pltpu.make_async_copy(
            wout_h.at[pl.ds(pl.multiple_of(i * 256, 256), 256)], v.wo.at[i], v.s_wo.at[i]
        )

    def loop(fn, n=4):
        def step(j, carry):
            fn(j)
            return carry
        lax.fori_loop(0, n, step, 0)

    barrier = pltpu.get_barrier_semaphore()
    for peer in peers:
        pl.semaphore_signal(barrier, 1, device_id={"dp": peer}, device_id_type=MESH_ID)
    for other in (ahead, behind):
        pl.semaphore_signal(barrier, 1, device_id={"section": other}, device_id_type=MESH_ID)

    loads = [
        pltpu.make_async_copy(src, dst, v.s_in.at[i])
        for i, (src, dst) in enumerate(
            ((saved_h, saved), (act_h, act), (wbc_h, v.wbc.at[0:320]), (cot_h, v.cot))
        )
    ]
    loads[0].start()
    loop(lambda j: load_w(4 * diag + j).start())
    for load in loads[1:]:
        load.start()
    loop(lambda j: load_w(4 * ypeer + j).start())
    for q in (diag, ypeer):
        loop(lambda j: load_wo(4 * q + j).start())
    for q in (mate, me):
        loop(lambda j: load_w(4 * q + j).start())
    for q in (mate, me):
        loop(lambda j: load_wo(4 * q + j).start())

    def xz_first(j, ready=None):
        load_w(4 * diag + j).wait()
        v.xzd_s[0, 0, j] = dot1(saved[...], v.w[4 * diag + j], NN).astype(BF16)
        if ready is not None:
            ready()
        xzd(0, 0, j).start()

    def xz_sum(mb, x_ref):
        def fn(j):
            part = dot1(x_ref[...], v.w[4 * ypeer + j], NN)
            xzd(mb, 0, j).wait_recv()
            v.xzy_s[mb, j] = (part + v.xzd_r[mb, 0, j].astype(F32)).astype(BF16)
        return fn

    def xz_back(j):
        load_w(4 * ypeer + j).wait()
        xz_sum(0, saved)(j)
        xzy(0, j).start()

    v.wbc[320:] = jnp.zeros((64, 512), BF16)
    loads[0].wait()
    xz_first(0, lambda: pl.semaphore_wait(barrier, 5))
    xz_first(1)
    loads[1].wait()
    loads[2].wait()
    v.smd_s[...] = dot1(v.x2[1 - core], v.wbc[...], NT)
    smd().start()
    xz_back(0)
    xz_first(2)
    xz_back(1)
    xz_first(3)
    own_small = dot1(v.x2[core], v.wbc[...], NT)
    smd().wait_recv()
    own_small = own_small + v.smd_r[...]
    v.smy_s[...] = own_small.astype(BF16)
    smy().start()
    v.sm[core] = own_small
    xz_back(2)
    squares = []
    for x_ref in (saved, act):
        wide_x = x_ref[...].astype(F32)
        squares.append(row_sums(wide_x * wide_x))
    v.sq[me] = jnp.where(rows_of((8, SEQ)) == 0, squares[0], squares[1])
    spread_start(v.sq, "sq")
    xz_back(3)
    loads[3].wait()

    def m_first(j):
        load_wo(4 * diag + j).wait()
        v.md_s[0, j] = dot1(cot[...], v.wo[4 * diag + j], NT).astype(BF16)
        md(0, j).start()

    loop(m_first)

    def m_sum(j):
        load_wo(4 * ypeer + j).wait()
        part = dot1(cot[...], v.wo[4 * ypeer + j], NT)
        md(0, j).wait_recv()
        v.my_s[j] = (part + v.md_r[0, j].astype(F32)).astype(BF16)
        my(j).start()

    loop(m_sum)

    def xz_mate(j):
        load_w(4 * mate + j).wait()
        v.xzd_s[0, 1, j] = dot1(saved[...], v.w[4 * mate + j], NN).astype(BF16)
        xzd(0, 1, j).start()

    loop(xz_mate)

    def m_mate(j):
        load_wo(4 * mate + j).wait()
        v.md_s[1, j] = dot1(cot[...], v.wo[4 * mate + j], NT).astype(BF16)
        md(1, j).start()

    loop(m_mate)

    def fwd_first(j):
        v.xzd_s[1, 0, j] = dot1(act[...], v.w[4 * diag + j], NN).astype(BF16)
        xzd(1, 0, j).start()

    loop(fwd_first)

    smy().wait_recv()
    v.sm[core] = v.sm[core] + v.smy_r[...].astype(F32)
    smt(core).start()

    expand = (lanes_of((16, 1024)) // HEAD_DIM == rows_of((16, 1024))).astype(F32)
    skip_wide = dot_full(dskip[...], expand, NN)
    for p in range(8):
        cols = slice(128 * p, 128 * p + 128)
        v.cx[p] = convx[:, cols]
        v.gain[p] = gain_in[:, cols]
        v.dsk[p] = skip_wide[:, cols]
    bias_col = jnp.broadcast_to(dtb[...], (SEQ, 16)).T
    v.negA[...] = -jnp.exp(jnp.broadcast_to(alog[...], (SEQ, 16)).T)
    row_id = rows_of((SEQ, SEQ))
    lane_id = lanes_of((SEQ, SEQ))
    causal = row_id >= lane_id
    low = lane_id < HEAD_DIM

    spread_wait(v.sq, "sq")
    total_sq = v.sq[0] + v.sq[1] + v.sq[2] + v.sq[3]
    for mb in range(2):
        v.scale[mb] = lax.rsqrt(as_column(total_sq[mb : mb + 1]) / D + 1e-05)

    smt(1 - core).wait_recv()

    def prepare(mb):
        scale = v.scale[mb]
        small = v.sm[mb] * wide(scale, 3)
        conv = conv_rows(small[:, :MAPS], convbc[...])
        sig = sigmoid(conv)
        maps = (conv * sig).astype(BF16)
        v.scores[mb] = dot1(maps[:, NSTATE:], maps[:, :NSTATE], NT)
        if mb == 0:
            v.maps[...] = maps
            v.dcm[...] = d_silu(conv, sig)
        v.pdt[...] = small[:, MAPS:].T
        logits = v.pdt[pl.ds(pl.multiple_of(16 * me, 16), 16)] + bias_col
        steps = jnp.maximum(logits, 0.0) + jnp.log1p(jnp.exp(-jnp.abs(logits)))
        if mb == 0:
            v.sgT[...] = sigmoid(logits)
        v.dtT[mb] = steps
        v.cumT[mb] = dot_full(
            steps * v.negA[...], (row_id <= lane_id).astype(F32), NN
        )

    prepare(0)

    def split_pair(first, second):
        head_x = jnp.where(low, first, pltpu.roll(second, 64, 1))
        head_z = jnp.where(low, pltpu.roll(first, 64, 1), second)
        return head_x, head_z

    def mix(mb, pair, block, save):
        scale = v.scale[mb]
        x, z = split_pair(block[:, :128] * scale, block[:, 128:] * scale)
        conv = conv_rows(x, v.cx[pair])
        sig = sigmoid(conv)
        xc = conv * sig
        sig_z = sigmoid(z)
        gate = z * sig_z
        weights = []
        for k in range(2):
            head = pl.ds(2 * pair + k, 1)
            row = v.cumT[mb, head]
            decay = jnp.exp(jnp.where(causal, as_column(row) - row, -1e30))
            if save:
                v.big_l[2 * pair + k] = decay
            weights.append(decay * v.scores[mb] * v.dtT[mb, head])
        stacked = jnp.concatenate([jnp.where(low, xc, 0.0), jnp.where(low, 0.0, xc)], axis=0)
        y = dot3(jnp.concatenate(weights, axis=1), stacked, NN)
        if save:
            v.xc[pair] = xc
            v.ys[pair] = y
            v.gz[pair] = gate
            v.dcv[pair] = d_silu(conv, sig)
            v.dzs[pair] = d_silu(z, sig_z)
        return (y + v.dsk[pair] * xc) * gate

    def raw_block(mb, x_ref, j):
        return (
            dot1(x_ref[...], v.w[4 * me + j], NN)
            + v.xzd_r[mb, 1, j].astype(F32)
            + v.xzy_r[mb, j].astype(F32)
        )

    v.acc0[...] = jnp.zeros((SEQ, SEQ), F32)

    def stage_a(j):
        load_w(4 * me + j).wait()
        xzd(0, 1, j).wait_recv()
        xzy(0, j).wait_recv()
        raw = raw_block(0, saved, j)
        v.raw[j] = raw
        for k in range(2):
            gated = mix(0, 2 * j + k, raw[:, 256 * k : 256 * k + 256], True)
            v.acc0[...] += gated * gated

    loop(stage_a)

    def fwd_mate(j):
        v.xzd_s[1, 1, j] = dot1(act[...], v.w[4 * mate + j], NN).astype(BF16)
        xzd(1, 1, j).start()

    loop(xz_sum(1, act))
    loop(fwd_mate)

    v.acc1[...] = jnp.zeros((SEQ, SEQ), F32)

    def stage_b(j):
        load_wo(4 * me + j).wait()
        md(1, j).wait_recv()
        my(j).wait_recv()

        @pl.when(j == 2)
        def _():
            xzy(1, 0).start()

        d_mixed = (
            dot1(cot[...], v.wo[4 * me + j], NT)
            + v.md_r[1, j].astype(F32)
            + v.my_r[j].astype(F32)
        )
        for k in range(2):
            pair = 2 * j + k
            part = d_mixed[:, 128 * k : 128 * k + 128]
            v.dm[pair] = part
            gated = (v.ys[pair] + v.dsk[pair] * v.xc[pair]) * v.gz[pair]
            v.acc1[...] += part * v.gain[pair] * gated

    loop(stage_b)

    v.rs[me] = jnp.where(
        rows_of((8, SEQ)) == 0, row_sums(v.acc0[...]), row_sums(v.acc1[...])
    )
    spread_start(v.rs, "rs")
    loop(lambda j: xzy(1, j + 1).start(), 3)
    prepare(1)
    for k in range(4):
        cols = slice(128 * k, 128 * k + 128)
        normed = (saved[:, cols].astype(F32) * v.scale[0]).astype(BF16)
        v.normed[cols] = normed.astype(F32).T.astype(BF16)
    normed_copy = pltpu.make_async_copy(v.normed, normed_o, v.s_out.at[8])
    normed_copy.start()
    spread_wait(v.rs, "rs")
    total_rs = v.rs[0] + v.rs[1] + v.rs[2] + v.rs[3]
    v.acc0[...] = lax.rsqrt(as_column(total_rs[0:1]) / INNER + 1e-05)
    v.acc1[...] = as_column(total_rs[1:2]) / INNER

    v.pdt[...] = jnp.zeros((SEQ, SEQ), F32)
    v.ds_acc[...] = jnp.zeros((2, 64, SEQ), F32)
    head_rows = (
        lanes_of((8, SEQ)) // HEAD_DIM == rows_of((8, SEQ))
    ).astype(F32)

    def stage_c(j):
        inverse = v.acc0[...]
        lower = inverse * inverse * inverse * v.acc1[...]
        for k in range(2):
            pair = 2 * j + k
            xc = v.xc[pair]
            y = v.ys[pair]
            gate = v.gz[pair]
            skip = v.dsk[pair]
            gained = inverse * v.gain[pair]
            y_full = y + skip * xc
            gated = y_full * gate
            v.ga_mix[me, j, 128 * k : 128 * k + 128] = (gated * gained).T.astype(BF16)
            d_gated = gained * v.dm[pair] - gated * lower
            d_y = d_gated * gate
            d_gate = d_gated * y_full
            d_ys = jnp.concatenate([jnp.where(low, d_y, 0.0), jnp.where(low, 0.0, d_y)], axis=0)
            d_w = dot3(d_ys, xc, NT)
            scores = v.scores[0]
            weights = []
            d_scores = None
            for h in range(2):
                head = pl.ds(2 * pair + h, 1)
                decay = v.big_l[2 * pair + h]
                steps = v.dtT[0, head]
                scored = decay * scores
                weights.append(scored * steps)
                d_head = d_w[SEQ * h : SEQ * h + SEQ]
                term = d_head * (decay * steps)
                d_scores = term if d_scores is None else d_scores + term
                v.dirT[head] = jnp.sum(d_head * scored, axis=0, keepdims=True)
            v.ds_acc[0] += d_scores[:64]
            v.ds_acc[1] += d_scores[64:]
            sums = dot_full(head_rows, d_y * y, NT)
            v.rowT[pl.ds(2 * pair, 1)] = sums[0:1]
            v.rowT[pl.ds(2 * pair + 1, 1)] = sums[1:2]
            d_xc = dot3(jnp.concatenate(weights, axis=0), d_ys, TN) + skip * d_y
            d_x = conv_rows_back(d_xc * v.dcv[pair], v.cx[pair])
            d_z = d_gate * v.dzs[pair]
            first, second = split_pair(d_x, d_z)
            first = first.astype(BF16)
            second = second.astype(BF16)
            v.ga_round[me, j, :, 256 * k : 256 * k + 128] = first
            v.ga_round[me, j, :, 256 * k + 128 : 256 * k + 256] = second
            v.pdt[...] += (
                first.astype(F32) * v.raw[j, :, 256 * k : 256 * k + 128]
                + second.astype(F32) * v.raw[j, :, 256 * k + 128 : 256 * k + 256]
            )
        gather(v.ga_round, "ry", me, j, ypeer).start()
        gather(v.ga_round, "rd", me, j, mate).start()
        gather(v.ga_mix, "md2", me, j, mate).start()

    loop(stage_c)
    hand_out(0, me).start()
    hand_out(1, me).start()

    v.dsd_s[...] = v.ds_acc[1 - core]
    dsd().start()
    d_cum = v.rowT[...] - v.dtT[0] * v.dirT[...]
    d_a = dot_full(d_cum, (row_id >= lane_id).astype(F32), NN)
    v.tg[me, 0:16] = (v.dirT[...] + v.negA[...] * d_a) * v.sgT[...]
    v.tg[me, 16:24] = row_sums(v.pdt[...])
    spread_start(v.tg, "tg")
    dsd().wait_recv()
    v.dsy_s[...] = v.ds_acc[core] + v.dsd_r[...]
    dsy().start()

    v.acc0[...] = jnp.zeros((SEQ, SEQ), F32)

    def stage_e(j):
        xzd(1, 1, j).wait_recv()
        xzy(1, j).wait_recv()
        raw = raw_block(1, act, j)
        for k in range(2):
            pair = 2 * j + k
            gated = mix(1, pair, raw[:, 256 * k : 256 * k + 256], False)
            v.acc0[...] += gated * gated
            v.ga_fwd[me, j, :, 128 * k : 128 * k + 128] = (gated * v.gain[pair]).astype(BF16)
        gather(v.ga_fwd, "fy", me, j, ypeer).start()
        gather(v.ga_fwd, "fd", me, j, mate).start()

    loop(stage_e)
    loop(lambda j: gather(v.ga_mix, "my2", me, j, ypeer).start())
    v.rf[me] = row_sums(v.acc0[...])
    spread_start(v.rf, "rf")

    v.dn[...] = jnp.zeros((SEQ, 512), F32)

    def add_dn(q, j):
        v.dn[...] += dot1(v.ga_round[q, j], v.w[4 * q + j], NT)

    loop(lambda j: add_dn(me, j))

    dsy().wait_recv()
    v.ds_tot[core] = v.dsy_s[...] + v.dsy_r[...]
    dst(core).start()

    def add_mate(j):
        gather(v.ga_round, "rd", mate, j, mate).wait_recv()
        add_dn(mate, j)

    loop(add_mate)
    hand_out(0, mate).start()
    dst(1 - core).wait_recv()
    d_scores = jnp.concatenate([v.ds_tot[0], v.ds_tot[1]], axis=0)
    ds_high, ds_low = halves(d_scores)
    maps = v.maps[...]
    d_input_map = dot1(ds_high, maps[:, NSTATE:], TN) + dot1(ds_low, maps[:, NSTATE:], TN)
    d_output_map = dot1(ds_high, maps[:, :NSTATE], NN) + dot1(ds_low, maps[:, :NSTATE], NN)
    d_maps = jnp.concatenate([d_input_map, d_output_map], axis=1)
    d_pre = conv_rows_back(d_maps * v.dcm[...], convbc[...])
    v.rbc[:, :MAPS] = d_pre.astype(BF16)
    spread_wait(v.tg, "tg")
    v.pdt[...] = jnp.zeros((SEQ, SEQ), F32)
    for q in range(4):
        v.pdt[16 * q : 16 * q + 16] = v.tg[q, 0:16]
    v.rbc[:, MAPS:] = v.pdt[...].T.astype(BF16)
    rbc_copy = pltpu.make_async_copy(v.rbc, rbc_o, v.s_out.at[9])
    rbc_copy.start()
    product = v.rbc[...].astype(F32) * v.sm[0]
    inner = row_sums(product[:, :128] + product[:, 128:256] + product[:, 256:])
    inner = inner + v.tg[0, 16:24] + v.tg[1, 16:24] + v.tg[2, 16:24] + v.tg[3, 16:24]
    v.acc1[...] = as_column(inner[0:1]) / D
    v.dn[...] += dot1(v.rbc[...], v.wbc[...], NN)

    def pass_on(j):
        gather(v.ga_round, "ry", ypeer, j, ypeer).wait_recv()
        gather(v.ga_round, "rw", ypeer, j, mate).start()
        add_dn(ypeer, j)

    loop(pass_on)
    hand_out(0, ypeer).start()

    def add_diag(j):
        gather(v.ga_round, "rw", diag, j, mate).wait_recv()
        add_dn(diag, j)

    loop(add_diag)
    hand_out(0, diag).start()
    for k in range(4):
        cols = slice(128 * k, 128 * k + 128)
        scale = v.scale[0]
        d_in = scale * v.dn[:, cols] - saved[:, cols].astype(F32) * (
            scale * scale * scale
        ) * v.acc1[...]
        v.sec[0, :, cols] = (cot[:, cols].astype(F32) + d_in).astype(BF16)
    send_section(0).start()

    v.dn[...] = jnp.zeros((SEQ, 512), F32)

    def add_out(q, j):
        v.dn[...] += dot1(v.ga_fwd[q, j], v.wo[4 * q + j], NN)

    loop(lambda j: add_out(me, j))

    def out_mate(j):
        gather(v.ga_fwd, "fd", mate, j, mate).wait_recv()
        add_out(mate, j)

    loop(out_mate)
    loop(lambda j: gather(v.ga_mix, "md2", mate, j, mate).wait_recv())
    hand_out(1, mate).start()
    spread_wait(v.rf, "rf")
    total_rf = v.rf[0] + v.rf[1] + v.rf[2] + v.rf[3]
    v.acc0[...] = lax.rsqrt(as_column(total_rf[0:1]) / INNER + 1e-05)

    def out_peer(j):
        gather(v.ga_fwd, "fy", ypeer, j, ypeer).wait_recv()
        gather(v.ga_fwd, "fw", ypeer, j, mate).start()
        add_out(ypeer, j)

    loop(out_peer)

    def out_diag(j):
        gather(v.ga_fwd, "fw", diag, j, mate).wait_recv()
        add_out(diag, j)

    loop(out_diag)
    for k in range(4):
        cols = slice(128 * k, 128 * k + 128)
        mixed = v.dn[:, cols] * v.acc0[...]
        v.sec[1, :, cols] = (act[:, cols].astype(F32) + mixed).astype(BF16)
    send_section(1).start()

    def pass_mix(j):
        gather(v.ga_mix, "my2", ypeer, j, ypeer).wait_recv()
        gather(v.ga_mix, "mw", ypeer, j, mate).start()

    loop(pass_mix)
    hand_out(1, ypeer).start()
    loop(lambda j: gather(v.ga_mix, "mw", diag, j, mate).wait_recv())
    hand_out(1, diag).start()

    smd().wait_send()
    smy().wait_send()
    smt(core).wait_send()
    dsd().wait_send()
    dsy().wait_send()
    dst(core).wait_send()
    for buf, kind in ((v.sq, "sq"), (v.rs, "rs"), (v.rf, "rf"), (v.tg, "tg")):
        for i in range(3):
            spread(buf, kind, i, me).wait_send()

    def drain(j):
        for mb in range(2):
            for role in range(2):
                xzd(mb, role, j).wait_send()
            xzy(mb, j).wait_send()
        md(0, j).wait_send()
        md(1, j).wait_send()
        my(j).wait_send()
        for buf, kinds in (
            (v.ga_round, ("ry", "rd", "rw")),
            (v.ga_mix, ("my2", "md2", "mw")),
            (v.ga_fwd, ("fy", "fd", "fw")),
        ):
            gather(buf, kinds[0], me, j, ypeer).wait_send()
            gather(buf, kinds[1], me, j, mate).wait_send()
            gather(buf, kinds[2], ypeer, j, mate).wait_send()

    loop(drain)
    for i in range(2):
        send_section(i).wait()
    normed_copy.wait()
    rbc_copy.wait()
    for q in range(4):
        hand_out(0, q).wait()
        hand_out(1, q).wait()


def chain(saved, act, cot, wxz, wbc, wout, convx, convbc, dtb, alog, dskip, gain):
    table = scratch_table()
    vm = pl.BlockSpec(memory_space=pltpu.VMEM)
    hbm = pl.BlockSpec(memory_space=pl.ANY)
    shape = jax.ShapeDtypeStruct
    return pl.pallas_call(
        functools.partial(chain_kernel, tuple(table)),
        out_shape=(
            shape((4, 4, SEQ, 512), BF16),
            shape((4, 4, 256, SEQ), BF16),
            shape((512, SEQ), BF16),
            shape((SEQ, 384), BF16),
            shape((SEQ, 512), BF16),
            shape((SEQ, 512), BF16),
        ),
        in_specs=[hbm] * 6 + [vm] * 6,
        out_specs=(hbm,) * 6,
        scratch_shapes=list(table.values()),
        compiler_params=pltpu.CompilerParams(
            collective_id=0, has_side_effects=True, vmem_limit_bytes=54 * 1024 * 1024
        ),
        cost_estimate=pl.CostEstimate(
            flops=4_300_000_000, bytes_accessed=18_000_000, transcendentals=2_000_000
        ),
        name="chain",
    )(saved, act, cot, wxz, wbc, wout, convx, convbc, dtb, alog, dskip, gain)


def grads_kernel(
    round_ref, mixed_ref, normed_ref, rbc_ref, cot_ref, prev_ref, next_ref,
    xz_o, out_o, bc_o, prev_o, next_o,
):
    for k in range(2):
        xz_o[:, 512 * k : 512 * k + 512] = dot1(normed_ref[...], round_ref[k], NN)
        out_o[256 * k : 256 * k + 256] = dot1(mixed_ref[k], cot_ref[...], NN)

    @pl.when(pl.program_id(0) == 0)
    def _():
        bc_o[...] = dot1(rbc_ref[:, :320], normed_ref[...], (((0,), (1,)), ((), ())))
        prev_o[...] = prev_ref[...]
        next_o[...] = next_ref[...]


def grads(round_all, mixed_all, normed, rbc, cot, prev_grad, next_act):
    shape = jax.ShapeDtypeStruct

    def fixed(*dims):
        return pl.BlockSpec(dims, lambda i: (0,) * len(dims))

    return pl.pallas_call(
        grads_kernel,
        grid=(8,),
        out_shape=(
            shape((512, 8192), F32),
            shape((4096, 512), F32),
            shape((320, 512), F32),
            shape((SEQ, 512), BF16),
            shape((SEQ, 512), BF16),
        ),
        in_specs=[
            pl.BlockSpec((2, SEQ, 512), lambda i: (i, 0, 0)),
            pl.BlockSpec((2, 256, SEQ), lambda i: (i, 0, 0)),
            fixed(512, SEQ),
            fixed(SEQ, 384),
            fixed(SEQ, 512),
            fixed(SEQ, 512),
            fixed(SEQ, 512),
        ],
        out_specs=(
            pl.BlockSpec((512, 1024), lambda i: (0, i)),
            pl.BlockSpec((512, 512), lambda i: (i, 0)),
            fixed(320, 512),
            fixed(SEQ, 512),
            fixed(SEQ, 512),
        ),
        compiler_params=pltpu.CompilerParams(vmem_limit_bytes=60 * 1024 * 1024),
        cost_estimate=pl.CostEstimate(
            flops=1_700_000_000, bytes_accessed=29_000_000, transcendentals=0
        ),
        name="grads",
    )(
        round_all.reshape(16, SEQ, 512),
        mixed_all.reshape(16, 256, SEQ),
        normed,
        rbc,
        cot,
        prev_grad,
        next_act,
    )


def per_device_four(
    act_in,
    saved_act,
    cotangent,
    weight_xz,
    weight_bcdt,
    weight_out,
    conv_x,
    conv_bc,
    dt_bias,
    a_log,
    d_skip,
    norm_gain,
):
    round_all, mixed_all, normed, rbc, prev_grad, next_act = chain(
        saved_act[0],
        act_in[0],
        cotangent[0],
        weight_xz[0],
        weight_bcdt[0],
        weight_out[0],
        conv_x[0],
        conv_bc[0],
        dt_bias,
        a_log,
        d_skip,
        norm_gain,
    )
    grad_xz, grad_out, grad_bcdt, prev_grad, next_act = grads(
        round_all, mixed_all, normed, rbc, cotangent[0], prev_grad, next_act
    )
    return (next_act[None], prev_grad[None], grad_xz[None], grad_bcdt[None], grad_out[None])


def solution(mesh):
    return jax.shard_map(
        per_device_four if mesh.shape["dp"] == 4 and mesh.shape["section"] > 1 else per_device,
        mesh=mesh,
        in_specs=(
            P("section", None, "dp"),
            P("section", None, "dp"),
            P("section", None, "dp"),
            P("section", "dp", None),
            P("section", None, "dp"),
            P("section", None, "dp"),
            P("section", None, "dp"),
            P("section", None, None),
            P("section", "dp"),
            P("section", "dp"),
            P("section", "dp"),
            P("section", "dp"),
        ),
        out_specs=(
            P("section", None, "dp"),
            P("section", None, "dp"),
            P("section", "dp", None),
            P("section", None, "dp"),
            P("section", None, "dp"),
        ),
        check_vma=False,
    )
```

```python
import functools

import jax
import jax.numpy as jnp
from jax import lax
from jax.experimental import pallas as pl
from jax.experimental.pallas import tpu as pltpu
from jax.sharding import PartitionSpec as P

D = 2048
HEAD_DIM = 64
NSTATE = 128
HEADS = 64
SEQ = 128
INNER = 4096
KCONV = 4
MAPS = 2 * NSTATE


def from_behind(x, axis, by):
    length = lax.axis_size(axis)
    return lax.ppermute(x, axis, [(i, (i + by) % length) for i in range(length)])


def swap(x, mask):
    length = lax.axis_size("dp")
    return lax.ppermute(x, "dp", [(i, i ^ mask) for i in range(length)])


def masks():
    length = lax.axis_size("dp")
    out = []
    bit = 1
    while bit < length:
        out.append(bit)
        bit *= 2
    return out


def sum_all(x):
    for bit in masks():
        x = x + swap(x, bit)
    return x


def tied(x, other):
    return lax.optimization_barrier((x, other))[0]


def sum_first(part):
    length = lax.axis_size("dp")
    came = {j - 1: swap(part(j).astype(jnp.bfloat16), 1) for j in range(1, length, 2)}
    return {j: part(j) + came[j].astype(jnp.float32) for j in sorted(came, reverse=True)}


def sum_rest(held, after=None):
    first = begun = None
    for bit in masks()[1:]:
        sent = {j: held[j].astype(jnp.bfloat16) for j in held if j & bit}
        if after is not None and first is None:
            sent = {j: tied(x, after) for j, x in sent.items()}
        came = {j ^ bit: swap(x, bit) for j, x in sent.items()}
        if first is None:
            first = came[0]
            begun = sent[bit]
        held = {j: held[j] + came[j].astype(jnp.float32) for j in came}
    return held[0], first, begun


def sum_both(x, after):
    me = lax.axis_index("dp")
    odd = (me & 1) != 0
    x = x + swap(x, 1)
    mine = tied(jnp.where(odd, x[SEQ:], x[:SEQ]), after)
    for bit in masks()[1:]:
        mine = mine + swap(mine, bit)
    other = swap(mine, 1)
    return jnp.where(odd, other, mine), jnp.where(odd, mine, other)


def gather_cols(block, after=None):
    me = lax.axis_index("dp")
    length = lax.axis_size("dp")
    if after is not None:
        block = tied(block, after)
    held = [block]
    order = [0]
    for bit in reversed(masks()):
        held = held + [swap(b, bit) for b in held]
        order = order + [j ^ bit for j in order]
    by_mask = {j: b for j, b in zip(order, held)}
    level = [by_mask[j] for j in range(length)]
    for bit in masks():
        flip = (me & bit) != 0
        level = [jnp.where(flip, level[j ^ bit], level[j]) for j in range(length)]
    return jnp.concatenate(level, axis=1), held[-1]


def causal_conv(values, kernel_taps):
    kernel = kernel_taps.shape[0]
    length = values.shape[0]
    padded = jnp.pad(values, ((kernel - 1, 0), (0, 0)))
    running = jnp.zeros_like(values)
    for offset in range(kernel):
        running = running + kernel_taps[offset] * padded[offset : offset + length]
    return running


def mixer(proj_x, proj_z, proj_dt, scores, conv_taps, dt_offset, log_rate, skip_gain):
    length, width = proj_x.shape
    nheads = dt_offset.shape[0]
    head_width = width // nheads
    xconv = jax.nn.silu(causal_conv(proj_x, conv_taps))
    steps = jax.nn.softplus(proj_dt + dt_offset)
    position = jnp.arange(length)
    causal = position[:, None] >= position[None, :]
    cumul = jnp.dot(
        causal.astype(jnp.float32), steps * -jnp.exp(log_rate), precision=lax.Precision.HIGHEST
    )
    heads_cum = cumul.T
    spread = heads_cum[:, :, None] - heads_cum[:, None, :]
    decay = jnp.where(causal[None], jnp.exp(jnp.where(causal[None], spread, 0.0)), 0.0)
    weights = decay * scores[None] * steps.T[:, None, :]
    heads_in = xconv.reshape(length, nheads, head_width)
    result = jnp.einsum("hts,shp->thp", weights, heads_in, precision=lax.Precision.HIGH)
    result = result + skip_gain[None, :, None] * heads_in
    gate_in = jax.nn.silu(proj_z.reshape(length, nheads, head_width))
    return (result * gate_in).reshape(length, width)


def times_transposed(left, right):
    return lax.dot_general(
        left, right, (((1,), (1,)), ((), ())), preferred_element_type=jnp.float32
    )


def transposed_times(left, right):
    return lax.dot_general(
        left, right, (((0,), (0,)), ((), ())), preferred_element_type=jnp.float32
    )


def per_device(
    act_in,
    saved_act,
    cotangent,
    weight_xz,
    weight_bcdt,
    weight_out,
    conv_x,
    conv_bc,
    dt_bias,
    a_log,
    d_skip,
    norm_gain,
):
    input_rows = act_in[0]
    saved_rows = saved_act[0]
    cot_rows = cotangent[0]
    local_xz = weight_xz[0]
    local_bcdt = weight_bcdt[0]
    local_out = weight_out[0]
    taps_x = conv_x[0]
    taps_bc = conv_bc[0]
    dt_offset = dt_bias[0]
    log_rate = a_log[0]
    skip_gain = d_skip[0]
    gain_local = norm_gain[0]
    own_heads = dt_offset.shape[0]
    me = lax.axis_index("dp")
    head_first = me * own_heads
    width = own_heads * HEAD_DIM

    def whole_act(pre_part):
        return jax.nn.silu(causal_conv(pre_part, taps_bc))

    both = jnp.concatenate([saved_rows, input_rows], axis=0)
    both_values = both.astype(jnp.float32)
    squares = jnp.sum(both_values * both_values, axis=1, keepdims=True)
    def xz_part(j):
        cols = lax.dynamic_slice_in_dim(local_xz, (me ^ j) * 2 * width, 2 * width, 1)
        return jnp.dot(both, cols, preferred_element_type=jnp.float32)

    held_xz = sum_first(xz_part)
    back_raw, back_first, back_begun = sum_rest({j: x[:SEQ] for j, x in held_xz.items()})
    back_small, forward_small = sum_both(
        jnp.concatenate([times_transposed(both, local_bcdt), squares], axis=1), back_begun
    )

    def mixed_part(j):
        taken = lax.dynamic_slice_in_dim(local_out, (me ^ j) * width, width, 0)
        return times_transposed(cot_rows, taken)

    d_mixed = sum_rest(sum_first(mixed_part), back_begun)[0]
    forward_raw = sum_rest({j: x[SEQ:] for j, x in held_xz.items()}, back_first)[0]

    def project(rows, small, raw_xz):
        raw_cols = small[:, : MAPS + HEADS]
        scales = lax.rsqrt(small[:, MAPS + HEADS :] / D + 1e-05)
        return (rows.astype(jnp.float32), scales, raw_xz, raw_cols)

    back_proj = project(saved_rows, back_small, back_raw)
    forward_proj = project(input_rows, forward_small, forward_raw)

    def gate_parts(projected):
        values, scales, raw_xz, raw_cols = projected
        own_xz = raw_xz * scales
        whole_cols = raw_cols * scales
        pre_part = whole_cols[:, :MAPS]
        maps = whole_act(pre_part).astype(jnp.bfloat16)
        own_dt = lax.dynamic_slice_in_dim(whole_cols[:, MAPS:], head_first, own_heads, 1)
        split_xz = own_xz.reshape(SEQ, own_heads, 2, HEAD_DIM)
        mix_x = split_xz[:, :, 0].reshape(SEQ, width)
        mix_z = split_xz[:, :, 1].reshape(SEQ, width)
        scores = times_transposed(maps[:, NSTATE:], maps[:, :NSTATE])

        def local_mix(in_x, in_z, in_dt, in_scores):
            return mixer(in_x, in_z, in_dt, in_scores, taps_x, dt_offset, log_rate, skip_gain)

        gated, mix_back = jax.vjp(local_mix, mix_x, mix_z, own_dt, scores)
        return (gated, mix_back, maps, pre_part)

    values, scales, raw_xz, raw_cols = back_proj
    gated, mix_back, maps, pre_part = gate_parts(back_proj)
    gained = gated * gain_local
    row_sums = sum_all(
        jnp.stack([jnp.sum(gated * gated, axis=1), jnp.sum(d_mixed * gained, axis=1)])
    )
    inverse = lax.rsqrt(row_sums[0] / INNER + 1e-05)[:, None]
    dots = row_sums[1][:, None]
    mixed_in = (gained * inverse).astype(jnp.bfloat16)
    d_gated = inverse * gain_local * d_mixed - gated * (inverse * inverse * inverse) * dots / INNER
    d_px, d_pz, d_pdt, d_scores = mix_back(d_gated)
    own_round = (
        jnp.stack(
            [
                d_px.reshape(SEQ, own_heads, HEAD_DIM),
                d_pz.reshape(SEQ, own_heads, HEAD_DIM),
            ],
            axis=2,
        )
        .reshape(SEQ, own_heads * 2 * HEAD_DIM)
        .astype(jnp.bfloat16)
    )
    round_xz, round_last = gather_cols(own_round)
    inner_own = jnp.sum(own_round.astype(jnp.float32) * raw_xz, axis=1, keepdims=True)
    wide_maps = maps.astype(jnp.float32)
    d_maps = jnp.concatenate(
        [
            jnp.dot(d_scores.T, wide_maps[:, NSTATE:], precision=lax.Precision.HIGH),
            jnp.dot(d_scores, wide_maps[:, :NSTATE], precision=lax.Precision.HIGH),
        ],
        axis=1,
    )
    d_dt_full = lax.dynamic_update_slice_in_dim(
        jnp.zeros((SEQ, HEADS), jnp.float32), d_pdt, head_first, 1
    )
    summed = sum_all(jnp.concatenate([d_maps, d_dt_full, inner_own], axis=1))
    conv_out, conv_back = jax.vjp(whole_act, pre_part)
    d_pre = conv_back(summed[:, :MAPS])[0]
    round_bcdt = jnp.concatenate([d_pre, summed[:, MAPS : MAPS + HEADS]], axis=1).astype(
        jnp.bfloat16
    )
    inner_sum = summed[:, MAPS + HEADS :] + jnp.sum(
        round_bcdt.astype(jnp.float32) * raw_cols, axis=1, keepdims=True
    )

    fwd_gated = gate_parts(forward_proj)[0]
    fwd_all, _ = gather_cols((fwd_gated * gain_local).astype(jnp.bfloat16), round_last)
    fwd_sum = sum_all(jnp.sum(fwd_gated * fwd_gated, axis=1)[None])
    fwd_inverse = lax.rsqrt(fwd_sum[0] / INNER + 1e-05)[:, None]
    mixed = jnp.dot(fwd_all, local_out, preferred_element_type=jnp.float32) * fwd_inverse
    section_out = (input_rows.astype(jnp.float32) + mixed).astype(jnp.bfloat16)
    next_act = from_behind(section_out, "section", 1)

    normed = (values * scales).astype(jnp.bfloat16)
    d_normed = times_transposed(round_xz, local_xz)
    d_normed = d_normed + jnp.dot(round_bcdt, local_bcdt, preferred_element_type=jnp.float32)
    d_norm_in = scales * d_normed - values * (scales * scales * scales) * inner_sum / D
    d_input = (cot_rows.astype(jnp.float32) + d_norm_in).astype(jnp.bfloat16)
    prev_grad = from_behind(d_input, "section", -1)

    grad_out = transposed_times(gather_cols(mixed_in, round_last)[0], cot_rows)
    grad_xz = transposed_times(normed, round_xz)
    grad_bcdt = transposed_times(round_bcdt, normed)
    return (next_act[None], prev_grad[None], grad_xz[None], grad_bcdt[None], grad_out[None])


BF16 = jnp.bfloat16
F32 = jnp.float32
MESH_ID = pl.DeviceIdType.MESH
NN = (((1,), (0,)), ((), ()))
NT = (((1,), (1,)), ((), ()))
TN = (((0,), (0,)), ((), ()))


def dot1(a, b, dims):
    return lax.dot_general(a, b, dims, preferred_element_type=F32)


def dot_full(a, b, dims):
    return lax.dot_general(
        a, b, dims, precision=lax.Precision.HIGHEST, preferred_element_type=F32
    )


def halves(x):
    high = x.astype(BF16)
    return high, (x - high.astype(F32)).astype(BF16)


def dot3(a, b, dims):
    a_high, a_low = halves(a)
    b_high, b_low = halves(b)
    return dot1(a_high, b_high, dims) + (dot1(a_high, b_low, dims) + dot1(a_low, b_high, dims))


def sigmoid(x):
    return 1.0 / (1.0 + jnp.exp(-x))


def d_silu(x, s):
    return s * (1.0 + x * (1.0 - s))


def rows_of(shape):
    return lax.broadcasted_iota(jnp.int32, shape, 0)


def lanes_of(shape):
    return lax.broadcasted_iota(jnp.int32, shape, 1)


def conv_rows(v, taps):
    row = rows_of(v.shape)
    out = taps[KCONV - 1 : KCONV] * v
    for s in range(1, KCONV):
        moved = jnp.where(row >= s, pltpu.roll(v, s, 0), 0.0)
        out = out + taps[KCONV - 1 - s : KCONV - s] * moved
    return out


def conv_rows_back(d, taps):
    row = rows_of(d.shape)
    out = taps[KCONV - 1 : KCONV] * d
    for s in range(1, KCONV):
        moved = jnp.where(row < SEQ - s, pltpu.roll(d, SEQ - s, 0), 0.0)
        out = out + taps[KCONV - 1 - s : KCONV - s] * moved
    return out


def as_column(row):
    return jnp.broadcast_to(row, (SEQ, SEQ)).T


def row_sums(values):
    return dot_full(jnp.ones((8, values.shape[1]), F32), values, NT)


def wide(col, n):
    return jnp.concatenate([col] * n, axis=1)


def scratch_table():
    dma = pltpu.SemaphoreType.DMA
    vm = pltpu.VMEM
    table = dict(
        w=vm((16, 512, 512), BF16),
        wo=vm((16, 256, 512), BF16),
        wbc=vm((384, 512), BF16),
        x2=vm((2, SEQ, 512), BF16),
        cot=vm((SEQ, 512), BF16),
        sec=vm((2, SEQ, 512), BF16),
        normed=vm((512, SEQ), BF16),
        xzd_s=vm((2, 2, 4, SEQ, 512), BF16),
        xzd_r=vm((2, 2, 4, SEQ, 512), BF16),
        xzy_s=vm((2, 4, SEQ, 512), BF16),
        xzy_r=vm((2, 4, SEQ, 512), BF16),
        md_s=vm((2, 4, SEQ, 256), BF16),
        md_r=vm((2, 4, SEQ, 256), BF16),
        my_s=vm((4, SEQ, 256), BF16),
        my_r=vm((4, SEQ, 256), BF16),
        smd_s=vm((SEQ, 384), F32),
        smd_r=vm((SEQ, 384), F32),
        smy_s=vm((SEQ, 384), BF16),
        smy_r=vm((SEQ, 384), BF16),
        sm=vm((2, SEQ, 384), F32),
        sq=vm((4, 8, SEQ), F32),
        rs=vm((4, 8, SEQ), F32),
        rf=vm((4, 8, SEQ), F32),
        tg=vm((4, 24, SEQ), F32),
        dsd_s=vm((64, SEQ), F32),
        dsd_r=vm((64, SEQ), F32),
        dsy_s=vm((64, SEQ), F32),
        dsy_r=vm((64, SEQ), F32),
        ds_tot=vm((2, 64, SEQ), F32),
        ds_acc=vm((2, 64, SEQ), F32),
        ga_round=vm((4, 4, SEQ, 512), BF16),
        ga_mix=vm((4, 4, 256, SEQ), BF16),
        ga_fwd=vm((4, 4, SEQ, 256), BF16),
        big_l=vm((16, SEQ, SEQ), F32),
        xc=vm((8, SEQ, SEQ), F32),
        ys=vm((8, SEQ, SEQ), F32),
        gz=vm((8, SEQ, SEQ), F32),
        dcv=vm((8, SEQ, SEQ), F32),
        dzs=vm((8, SEQ, SEQ), F32),
        dm=vm((8, SEQ, SEQ), F32),
        raw=vm((4, SEQ, 512), F32),
        acc0=vm((SEQ, SEQ), F32),
        acc1=vm((SEQ, SEQ), F32),
        dn=vm((SEQ, 512), F32),
        pdt=vm((SEQ, SEQ), F32),
        dtT=vm((2, 16, SEQ), F32),
        cumT=vm((2, 16, SEQ), F32),
        sgT=vm((16, SEQ), F32),
        negA=vm((16, SEQ), F32),
        dirT=vm((16, SEQ), F32),
        rowT=vm((16, SEQ), F32),
        scores=vm((2, SEQ, SEQ), F32),
        maps=vm((SEQ, 256), BF16),
        dcm=vm((SEQ, 256), F32),
        scale=vm((2, SEQ, SEQ), F32),
        cx=vm((8, KCONV, SEQ), F32),
        gain=vm((8, 1, SEQ), F32),
        dsk=vm((8, 1, SEQ), F32),
        rbc=vm((SEQ, 384), BF16),
        s_w=dma((16,)),
        s_wo=dma((16,)),
        s_in=dma((4,)),
        s_out=dma((10,)),
    )
    for name, shape in dict(
        xzd=(2, 2, 4), xzy=(2, 4), md=(2, 4), my=(4,), smd=(1,), smy=(1,), smt=(1,), sq=(3,), rs=(3,),
        rf=(3,), tg=(3,), dsd=(1,), dsy=(1,), dst=(1,), ry=(4,), rd=(4,), rw=(4,), my2=(4,), md2=(4,),
        mw=(4,), fy=(4,), fd=(4,), fw=(4,), sec=(2,),
    ).items():
        table["a_" + name] = dma(shape)
        table["b_" + name] = dma(shape)
    return table


class Names:
    pass


def chain_kernel(names, *refs):
    (saved_h, act_h, cot_h, wxz_h, wbc_h, wout_h, convx, convbc, dtb, alog, dskip, gain_in,
     round_o, mixed_o, normed_o, rbc_o, prev_o, next_o) = refs[:18]
    v = Names()
    for name, ref in zip(names, refs[18:]):
        setattr(v, name, ref)
    saved, act, cot = v.x2.at[0], v.x2.at[1], v.cot

    me = lax.axis_index("dp")
    core = lax.rem(me, 2)
    mate = me + 1 - 2 * core
    ypeer = me + 2 - 4 * (me // 2)
    diag = 3 - me
    peers = (mate, ypeer, diag)
    sections = lax.axis_size("section")
    place = lax.axis_index("section")
    ahead = lax.rem(place + 1, sections)
    behind = lax.rem(place + sections - 1, sections)

    def remote(src, dst, kind, index, dev):
        return pltpu.make_async_remote_copy(
            src_ref=src,
            dst_ref=dst,
            send_sem=getattr(v, "a_" + kind).at[index],
            recv_sem=getattr(v, "b_" + kind).at[index],
            device_id={"dp": dev},
            device_id_type=MESH_ID,
        )

    def xzd(mb, role, j):
        return remote(v.xzd_s.at[mb, role, j], v.xzd_r.at[mb, role, j], "xzd", (mb, role, j), mate)

    def xzy(mb, j):
        return remote(v.xzy_s.at[mb, j], v.xzy_r.at[mb, j], "xzy", (mb, j), ypeer)

    def md(role, j):
        return remote(v.md_s.at[role, j], v.md_r.at[role, j], "md", (role, j), mate)

    def my(j):
        return remote(v.my_s.at[j], v.my_r.at[j], "my", (j,), ypeer)

    def smd():
        return remote(v.smd_s, v.smd_r, "smd", (0,), mate)

    def smy():
        return remote(v.smy_s, v.smy_r, "smy", (0,), ypeer)

    def smt(mb):
        return remote(v.sm.at[mb], v.sm.at[mb], "smt", (0,), mate)

    def spread(buf, kind, i, slot):
        return remote(buf.at[slot], buf.at[slot], kind, (i,), peers[i])

    def spread_start(buf, kind):
        for i in range(3):
            spread(buf, kind, i, me).start()

    def spread_wait(buf, kind):
        for i in range(3):
            spread(buf, kind, i, peers[i]).wait_recv()

    def dsd():
        return remote(v.dsd_s, v.dsd_r, "dsd", (0,), mate)

    def dsy():
        return remote(v.dsy_s, v.dsy_r, "dsy", (0,), ypeer)

    def dst(half):
        return remote(v.ds_tot.at[half], v.ds_tot.at[half], "dst", (0,), mate)

    def gather(buf, kind, q, j, dev):
        return remote(buf.at[q, j], buf.at[q, j], kind, (j,), dev)

    def send_section(i):
        return pltpu.make_async_remote_copy(
            src_ref=v.sec.at[i],
            dst_ref=(prev_o, next_o)[i],
            send_sem=v.a_sec.at[i],
            recv_sem=v.b_sec.at[i],
            device_id={"section": (behind, ahead)[i]},
            device_id_type=MESH_ID,
        )

    def hand_out(kind, q):
        buf, out = ((v.ga_round, round_o), (v.ga_mix, mixed_o))[kind]
        return pltpu.make_async_copy(buf.at[q], out.at[q], v.s_out.at[4 * kind + q])

    def load_w(i):
        cols = pl.ds(pl.multiple_of(i * 512, 512), 512)
        return pltpu.make_async_copy(wxz_h.at[:, cols], v.w.at[i], v.s_w.at[i])

    def load_wo(i):
        return pltpu.make_async_copy(
            wout_h.at[pl.ds(pl.multiple_of(i * 256, 256), 256)], v.wo.at[i], v.s_wo.at[i]
        )

    def loop(fn, n=4):
        def step(j, carry):
            fn(j)
            return carry
        lax.fori_loop(0, n, step, 0)

    def follow(j, begin):
        @pl.when(j >= 1)
        def _():
            begin(j - 1)

        @pl.when(j == 3)
        def _():
            begin(3)

    barrier = pltpu.get_barrier_semaphore()
    for peer in peers:
        pl.semaphore_signal(barrier, 1, device_id={"dp": peer}, device_id_type=MESH_ID)
    for other in (ahead, behind):
        pl.semaphore_signal(barrier, 1, device_id={"section": other}, device_id_type=MESH_ID)

    loads = [
        pltpu.make_async_copy(src, dst, v.s_in.at[i])
        for i, (src, dst) in enumerate(
            ((saved_h, saved), (act_h, act), (wbc_h, v.wbc.at[0:320]), (cot_h, v.cot))
        )
    ]
    loads[0].start()
    for i in range(2):
        load_w(4 * diag + i).start()
    load_w(4 * ypeer).start()

    def xz_first(j, ready=None):
        load_w(4 * diag + j).wait()
        v.xzd_s[0, 0, j] = dot1(saved[...], v.w[4 * diag + j], NN).astype(BF16)
        if ready is not None:
            ready()
        xzd(0, 0, j).start()

    def xz_sum(mb, x_ref):
        def fn(j):
            part = dot1(x_ref[...], v.w[4 * ypeer + j], NN)
            xzd(mb, 0, j).wait_recv()
            v.xzy_s[mb, j] = (part + v.xzd_r[mb, 0, j].astype(F32)).astype(BF16)
        return fn

    def xz_back(j):
        load_w(4 * ypeer + j).wait()
        xz_sum(0, saved)(j)
        xzy(0, j).start()

    v.wbc[320:] = jnp.zeros((64, 512), BF16)
    loads[0].wait()
    xz_first(0, lambda: pl.semaphore_wait(barrier, 5))
    for load in loads[1:]:
        load.start()
    load_w(4 * diag + 2).start()
    load_w(4 * ypeer + 1).start()
    xz_first(1)
    load_w(4 * diag + 3).start()
    load_w(4 * ypeer + 2).start()
    load_w(4 * ypeer + 3).start()
    loads[1].wait()
    loads[2].wait()
    v.smd_s[...] = dot1(v.x2[1 - core], v.wbc[...], NT)
    smd().start()
    xz_back(0)
    for q in (diag, ypeer):
        loop(lambda j: load_wo(4 * q + j).start())
    for q in (mate, me):
        loop(lambda j: load_w(4 * q + j).start())
    for q in (mate, me):
        loop(lambda j: load_wo(4 * q + j).start())
    xz_first(2)
    xz_back(1)
    xz_first(3)
    own_small = dot1(v.x2[core], v.wbc[...], NT)
    smd().wait_recv()
    own_small = own_small + v.smd_r[...]
    v.smy_s[...] = own_small.astype(BF16)
    smy().start()
    v.sm[core] = own_small
    xz_back(2)
    squares = []
    for x_ref in (saved, act):
        wide_x = x_ref[...].astype(F32)
        squares.append(row_sums(wide_x * wide_x))
    v.sq[me] = jnp.where(rows_of((8, SEQ)) == 0, squares[0], squares[1])
    spread_start(v.sq, "sq")
    xz_back(3)
    loads[3].wait()

    def m_first(j):
        load_wo(4 * diag + j).wait()
        v.md_s[0, j] = dot1(cot[...], v.wo[4 * diag + j], NT).astype(BF16)
        md(0, j).start()

    loop(m_first)

    def m_sum(j):
        load_wo(4 * ypeer + j).wait()
        part = dot1(cot[...], v.wo[4 * ypeer + j], NT)
        md(0, j).wait_recv()
        v.my_s[j] = (part + v.md_r[0, j].astype(F32)).astype(BF16)

    loop(m_sum)

    def xz_mate(j):
        load_w(4 * mate + j).wait()
        v.xzd_s[0, 1, j] = dot1(saved[...], v.w[4 * mate + j], NN).astype(BF16)
        xzd(0, 1, j).start()

    loop(xz_mate)

    def m_mate(j):
        load_wo(4 * mate + j).wait()
        v.md_s[1, j] = dot1(cot[...], v.wo[4 * mate + j], NT).astype(BF16)
        md(1, j).start()

    loop(m_mate)

    def fwd_first(j):
        v.xzd_s[1, 0, j] = dot1(act[...], v.w[4 * diag + j], NN).astype(BF16)
        xzd(1, 0, j).start()

    loop(fwd_first)

    smy().wait_recv()
    v.sm[core] = v.sm[core] + v.smy_r[...].astype(F32)
    smt(core).start()

    expand = (lanes_of((16, 1024)) // HEAD_DIM == rows_of((16, 1024))).astype(F32)
    skip_wide = dot_full(dskip[...], expand, NN)
    for p in range(8):
        cols = slice(128 * p, 128 * p + 128)
        v.cx[p] = convx[:, cols]
        v.gain[p] = gain_in[:, cols]
        v.dsk[p] = skip_wide[:, cols]
    bias_col = jnp.broadcast_to(dtb[...], (SEQ, 16)).T
    v.negA[...] = -jnp.exp(jnp.broadcast_to(alog[...], (SEQ, 16)).T)
    row_id = rows_of((SEQ, SEQ))
    lane_id = lanes_of((SEQ, SEQ))
    causal = row_id >= lane_id
    low = lane_id < HEAD_DIM

    spread_wait(v.sq, "sq")
    total_sq = v.sq[0] + v.sq[1] + v.sq[2] + v.sq[3]
    for mb in range(2):
        v.scale[mb] = lax.rsqrt(as_column(total_sq[mb : mb + 1]) / D + 1e-05)

    smt(1 - core).wait_recv()

    def prepare(mb):
        scale = v.scale[mb]
        small = v.sm[mb] * wide(scale, 3)
        conv = conv_rows(small[:, :MAPS], convbc[...])
        sig = sigmoid(conv)
        maps = (conv * sig).astype(BF16)
        v.scores[mb] = dot1(maps[:, NSTATE:], maps[:, :NSTATE], NT)
        if mb == 0:
            v.maps[...] = maps
            v.dcm[...] = d_silu(conv, sig)
        v.pdt[...] = small[:, MAPS:].T
        logits = v.pdt[pl.ds(pl.multiple_of(16 * me, 16), 16)] + bias_col
        steps = jnp.maximum(logits, 0.0) + jnp.log1p(jnp.exp(-jnp.abs(logits)))
        if mb == 0:
            v.sgT[...] = sigmoid(logits)
        v.dtT[mb] = steps
        v.cumT[mb] = dot_full(
            steps * v.negA[...], (row_id <= lane_id).astype(F32), NN
        )

    prepare(0)

    def split_pair(first, second):
        head_x = jnp.where(low, first, pltpu.roll(second, 64, 1))
        head_z = jnp.where(low, pltpu.roll(first, 64, 1), second)
        return head_x, head_z

    def mix(mb, pair, block, save):
        scale = v.scale[mb]
        x, z = split_pair(block[:, :128] * scale, block[:, 128:] * scale)
        conv = conv_rows(x, v.cx[pair])
        sig = sigmoid(conv)
        xc = conv * sig
        sig_z = sigmoid(z)
        gate = z * sig_z
        weights = []
        for k in range(2):
            head = pl.ds(2 * pair + k, 1)
            row = v.cumT[mb, head]
            decay = jnp.exp(jnp.where(causal, as_column(row) - row, -1e30))
            if save:
                v.big_l[2 * pair + k] = decay
            weights.append(decay * v.scores[mb] * v.dtT[mb, head])
        stacked = jnp.concatenate([jnp.where(low, xc, 0.0), jnp.where(low, 0.0, xc)], axis=0)
        y = dot3(jnp.concatenate(weights, axis=1), stacked, NN)
        if save:
            v.xc[pair] = xc
            v.ys[pair] = y
            v.gz[pair] = gate
            v.dcv[pair] = d_silu(conv, sig)
            v.dzs[pair] = d_silu(z, sig_z)
        return (y + v.dsk[pair] * xc) * gate

    def raw_block(mb, x_ref, j):
        return (
            dot1(x_ref[...], v.w[4 * me + j], NN)
            + v.xzd_r[mb, 1, j].astype(F32)
            + v.xzy_r[mb, j].astype(F32)
        )

    v.acc0[...] = jnp.zeros((SEQ, SEQ), F32)

    def stage_a(j):
        load_w(4 * me + j).wait()
        xzd(0, 1, j).wait_recv()
        xzy(0, j).wait_recv()
        follow(j, lambda i: my(i).start())
        raw = raw_block(0, saved, j)
        v.raw[j] = raw
        for k in range(2):
            gated = mix(0, 2 * j + k, raw[:, 256 * k : 256 * k + 256], True)
            v.acc0[...] += gated * gated

    loop(stage_a)

    def fwd_mate(j):
        v.xzd_s[1, 1, j] = dot1(act[...], v.w[4 * mate + j], NN).astype(BF16)
        xzd(1, 1, j).start()

    loop(xz_sum(1, act))
    loop(fwd_mate)

    v.acc1[...] = jnp.zeros((SEQ, SEQ), F32)

    def stage_b(j):
        load_wo(4 * me + j).wait()
        md(1, j).wait_recv()
        my(j).wait_recv()

        @pl.when(j == 2)
        def _():
            xzy(1, 0).start()

        d_mixed = (
            dot1(cot[...], v.wo[4 * me + j], NT)
            + v.md_r[1, j].astype(F32)
            + v.my_r[j].astype(F32)
        )
        for k in range(2):
            pair = 2 * j + k
            part = d_mixed[:, 128 * k : 128 * k + 128]
            v.dm[pair] = part
            gated = (v.ys[pair] + v.dsk[pair] * v.xc[pair]) * v.gz[pair]
            v.acc1[...] += part * v.gain[pair] * gated

    loop(stage_b)

    v.rs[me] = jnp.where(
        rows_of((8, SEQ)) == 0, row_sums(v.acc0[...]), row_sums(v.acc1[...])
    )
    spread_start(v.rs, "rs")
    loop(lambda j: xzy(1, j + 1).start(), 3)
    prepare(1)
    for k in range(4):
        cols = slice(128 * k, 128 * k + 128)
        normed = (saved[:, cols].astype(F32) * v.scale[0]).astype(BF16)
        v.normed[cols] = normed.astype(F32).T.astype(BF16)
    normed_copy = pltpu.make_async_copy(v.normed, normed_o, v.s_out.at[8])
    normed_copy.start()
    spread_wait(v.rs, "rs")
    total_rs = v.rs[0] + v.rs[1] + v.rs[2] + v.rs[3]
    v.acc0[...] = lax.rsqrt(as_column(total_rs[0:1]) / INNER + 1e-05)
    v.acc1[...] = as_column(total_rs[1:2]) / INNER

    v.pdt[...] = jnp.zeros((SEQ, SEQ), F32)
    v.ds_acc[...] = jnp.zeros((2, 64, SEQ), F32)
    head_rows = (
        lanes_of((8, SEQ)) // HEAD_DIM == rows_of((8, SEQ))
    ).astype(F32)

    def stage_c(j):
        inverse = v.acc0[...]
        lower = inverse * inverse * inverse * v.acc1[...]
        for k in range(2):
            pair = 2 * j + k
            xc = v.xc[pair]
            y = v.ys[pair]
            gate = v.gz[pair]
            skip = v.dsk[pair]
            gained = inverse * v.gain[pair]
            y_full = y + skip * xc
            gated = y_full * gate
            v.ga_mix[me, j, 128 * k : 128 * k + 128] = (gated * gained).T.astype(BF16)
            d_gated = gained * v.dm[pair] - gated * lower
            d_y = d_gated * gate
            d_gate = d_gated * y_full
            d_ys = jnp.concatenate([jnp.where(low, d_y, 0.0), jnp.where(low, 0.0, d_y)], axis=0)
            d_w = dot3(d_ys, xc, NT)
            scores = v.scores[0]
            weights = []
            d_scores = None
            for h in range(2):
                head = pl.ds(2 * pair + h, 1)
                decay = v.big_l[2 * pair + h]
                steps = v.dtT[0, head]
                scored = decay * scores
                weights.append(scored * steps)
                d_head = d_w[SEQ * h : SEQ * h + SEQ]
                term = d_head * (decay * steps)
                d_scores = term if d_scores is None else d_scores + term
                v.dirT[head] = jnp.sum(d_head * scored, axis=0, keepdims=True)
            v.ds_acc[0] += d_scores[:64]
            v.ds_acc[1] += d_scores[64:]
            sums = dot_full(head_rows, d_y * y, NT)
            v.rowT[pl.ds(2 * pair, 1)] = sums[0:1]
            v.rowT[pl.ds(2 * pair + 1, 1)] = sums[1:2]
            d_xc = dot3(jnp.concatenate(weights, axis=0), d_ys, TN) + skip * d_y
            d_x = conv_rows_back(d_xc * v.dcv[pair], v.cx[pair])
            d_z = d_gate * v.dzs[pair]
            first, second = split_pair(d_x, d_z)
            first = first.astype(BF16)
            second = second.astype(BF16)
            v.ga_round[me, j, :, 256 * k : 256 * k + 128] = first
            v.ga_round[me, j, :, 256 * k + 128 : 256 * k + 256] = second
            v.pdt[...] += (
                first.astype(F32) * v.raw[j, :, 256 * k : 256 * k + 128]
                + second.astype(F32) * v.raw[j, :, 256 * k + 128 : 256 * k + 256]
            )
        gather(v.ga_round, "rd", me, j, mate).start()
        gather(v.ga_mix, "md2", me, j, mate).start()

    loop(stage_c)
    hand_out(0, me).start()
    hand_out(1, me).start()

    v.dsd_s[...] = v.ds_acc[1 - core]
    dsd().start()
    d_cum = v.rowT[...] - v.dtT[0] * v.dirT[...]
    d_a = dot_full(d_cum, (row_id >= lane_id).astype(F32), NN)
    v.tg[me, 0:16] = (v.dirT[...] + v.negA[...] * d_a) * v.sgT[...]
    v.tg[me, 16:24] = row_sums(v.pdt[...])
    spread_start(v.tg, "tg")
    dsd().wait_recv()
    v.dsy_s[...] = v.ds_acc[core] + v.dsd_r[...]
    dsy().start()

    v.acc0[...] = jnp.zeros((SEQ, SEQ), F32)

    def stage_e(j):
        xzd(1, 1, j).wait_recv()
        xzy(1, j).wait_recv()
        follow(j, lambda i: gather(v.ga_round, "ry", me, i, ypeer).start())
        raw = raw_block(1, act, j)
        for k in range(2):
            pair = 2 * j + k
            gated = mix(1, pair, raw[:, 256 * k : 256 * k + 256], False)
            v.acc0[...] += gated * gated
            v.ga_fwd[me, j, :, 128 * k : 128 * k + 128] = (gated * v.gain[pair]).astype(BF16)
        gather(v.ga_fwd, "fd", me, j, mate).start()

    loop(stage_e)
    v.rf[me] = row_sums(v.acc0[...])
    spread_start(v.rf, "rf")

    v.dn[...] = jnp.zeros((SEQ, 512), F32)

    def add_dn(q, j):
        v.dn[...] += dot1(v.ga_round[q, j], v.w[4 * q + j], NT)

    loop(lambda j: add_dn(me, j))

    dsy().wait_recv()
    v.ds_tot[core] = v.dsy_s[...] + v.dsy_r[...]
    dst(core).start()

    def add_mate(j):
        gather(v.ga_round, "rd", mate, j, mate).wait_recv()
        add_dn(mate, j)

    loop(add_mate)
    hand_out(0, mate).start()
    dst(1 - core).wait_recv()
    d_scores = jnp.concatenate([v.ds_tot[0], v.ds_tot[1]], axis=0)
    ds_high, ds_low = halves(d_scores)
    maps = v.maps[...]
    d_input_map = dot1(ds_high, maps[:, NSTATE:], TN) + dot1(ds_low, maps[:, NSTATE:], TN)
    d_output_map = dot1(ds_high, maps[:, :NSTATE], NN) + dot1(ds_low, maps[:, :NSTATE], NN)
    d_maps = jnp.concatenate([d_input_map, d_output_map], axis=1)
    d_pre = conv_rows_back(d_maps * v.dcm[...], convbc[...])
    v.rbc[:, :MAPS] = d_pre.astype(BF16)
    spread_wait(v.tg, "tg")
    v.pdt[...] = jnp.zeros((SEQ, SEQ), F32)
    for q in range(4):
        v.pdt[16 * q : 16 * q + 16] = v.tg[q, 0:16]
    v.rbc[:, MAPS:] = v.pdt[...].T.astype(BF16)
    rbc_copy = pltpu.make_async_copy(v.rbc, rbc_o, v.s_out.at[9])
    rbc_copy.start()
    product = v.rbc[...].astype(F32) * v.sm[0]
    inner = row_sums(product[:, :128] + product[:, 128:256] + product[:, 256:])
    inner = inner + v.tg[0, 16:24] + v.tg[1, 16:24] + v.tg[2, 16:24] + v.tg[3, 16:24]
    v.acc1[...] = as_column(inner[0:1]) / D
    v.dn[...] += dot1(v.rbc[...], v.wbc[...], NN)

    def pass_on(j):
        gather(v.ga_round, "ry", ypeer, j, ypeer).wait_recv()
        follow(j, lambda i: gather(v.ga_fwd, "fy", me, i, ypeer).start())
        gather(v.ga_round, "rw", ypeer, j, mate).start()
        add_dn(ypeer, j)

    loop(pass_on)
    hand_out(0, ypeer).start()

    def add_diag(j):
        gather(v.ga_round, "rw", diag, j, mate).wait_recv()
        add_dn(diag, j)

    loop(add_diag)
    hand_out(0, diag).start()
    for k in range(4):
        cols = slice(128 * k, 128 * k + 128)
        scale = v.scale[0]
        d_in = scale * v.dn[:, cols] - saved[:, cols].astype(F32) * (
            scale * scale * scale
        ) * v.acc1[...]
        v.sec[0, :, cols] = (cot[:, cols].astype(F32) + d_in).astype(BF16)
    send_section(0).start()

    v.dn[...] = jnp.zeros((SEQ, 512), F32)

    def add_out(q, j):
        v.dn[...] += dot1(v.ga_fwd[q, j], v.wo[4 * q + j], NN)

    loop(lambda j: add_out(me, j))

    def out_mate(j):
        gather(v.ga_fwd, "fd", mate, j, mate).wait_recv()
        add_out(mate, j)

    loop(out_mate)
    loop(lambda j: gather(v.ga_mix, "md2", mate, j, mate).wait_recv())
    hand_out(1, mate).start()
    spread_wait(v.rf, "rf")
    total_rf = v.rf[0] + v.rf[1] + v.rf[2] + v.rf[3]
    v.acc0[...] = lax.rsqrt(as_column(total_rf[0:1]) / INNER + 1e-05)

    def out_peer(j):
        gather(v.ga_fwd, "fy", ypeer, j, ypeer).wait_recv()
        follow(j, lambda i: gather(v.ga_mix, "my2", me, i, ypeer).start())
        gather(v.ga_fwd, "fw", ypeer, j, mate).start()
        add_out(ypeer, j)

    loop(out_peer)

    def out_diag(j):
        gather(v.ga_fwd, "fw", diag, j, mate).wait_recv()
        add_out(diag, j)

    loop(out_diag)
    for k in range(4):
        cols = slice(128 * k, 128 * k + 128)
        mixed = v.dn[:, cols] * v.acc0[...]
        v.sec[1, :, cols] = (act[:, cols].astype(F32) + mixed).astype(BF16)
    send_section(1).start()

    def pass_mix(j):
        gather(v.ga_mix, "my2", ypeer, j, ypeer).wait_recv()
        gather(v.ga_mix, "mw", ypeer, j, mate).start()

    loop(pass_mix)
    hand_out(1, ypeer).start()
    loop(lambda j: gather(v.ga_mix, "mw", diag, j, mate).wait_recv())
    hand_out(1, diag).start()

    smd().wait_send()
    smy().wait_send()
    smt(core).wait_send()
    dsd().wait_send()
    dsy().wait_send()
    dst(core).wait_send()
    for buf, kind in ((v.sq, "sq"), (v.rs, "rs"), (v.rf, "rf"), (v.tg, "tg")):
        for i in range(3):
            spread(buf, kind, i, me).wait_send()

    def drain(j):
        for mb in range(2):
            for role in range(2):
                xzd(mb, role, j).wait_send()
            xzy(mb, j).wait_send()
        md(0, j).wait_send()
        md(1, j).wait_send()
        my(j).wait_send()
        for buf, kinds in (
            (v.ga_round, ("ry", "rd", "rw")),
            (v.ga_mix, ("my2", "md2", "mw")),
            (v.ga_fwd, ("fy", "fd", "fw")),
        ):
            gather(buf, kinds[0], me, j, ypeer).wait_send()
            gather(buf, kinds[1], me, j, mate).wait_send()
            gather(buf, kinds[2], ypeer, j, mate).wait_send()

    loop(drain)
    for i in range(2):
        send_section(i).wait()
    normed_copy.wait()
    rbc_copy.wait()
    for q in range(4):
        hand_out(0, q).wait()
        hand_out(1, q).wait()


def chain(saved, act, cot, wxz, wbc, wout, convx, convbc, dtb, alog, dskip, gain):
    table = scratch_table()
    vm = pl.BlockSpec(memory_space=pltpu.VMEM)
    hbm = pl.BlockSpec(memory_space=pl.ANY)
    shape = jax.ShapeDtypeStruct
    return pl.pallas_call(
        functools.partial(chain_kernel, tuple(table)),
        out_shape=(
            shape((4, 4, SEQ, 512), BF16),
            shape((4, 4, 256, SEQ), BF16),
            shape((512, SEQ), BF16),
            shape((SEQ, 384), BF16),
            shape((SEQ, 512), BF16),
            shape((SEQ, 512), BF16),
        ),
        in_specs=[pl.BlockSpec(memory_space=pltpu.HBM)] * 6 + [vm] * 6,
        out_specs=(hbm,) * 6,
        scratch_shapes=list(table.values()),
        compiler_params=pltpu.CompilerParams(
            collective_id=0, has_side_effects=True, vmem_limit_bytes=60 * 1024 * 1024
        ),
        cost_estimate=pl.CostEstimate(
            flops=4_300_000_000, bytes_accessed=18_000_000, transcendentals=2_000_000
        ),
        name="chain",
    )(saved, act, cot, wxz, wbc, wout, convx, convbc, dtb, alog, dskip, gain)


def grads_kernel(
    round_h, mixed_h, normed_h, rbc_h, cot_h, prev_ref, next_ref,
    xz_o, out_o, bc_o, prev_o, next_o,
    round_ref, mixed_ref, normed_ref, rbc_ref, cot_ref,
    xz_s, out_s, bc_s, s_xz, s_out, s_rest, s_round, s_mixed, s_in,
):
    fixed = [
        pltpu.make_async_copy(src, dst, s_in.at[i])
        for i, (src, dst) in enumerate(
            ((cot_h, cot_ref), (normed_h, normed_ref), (rbc_h, rbc_ref))
        )
    ]

    def load_round(i):
        return pltpu.make_async_copy(round_h.at[i], round_ref.at[i], s_round.at[i])

    def load_mixed(i):
        return pltpu.make_async_copy(mixed_h.at[i], mixed_ref.at[i], s_mixed.at[i])

    def begin(i, carry):
        load_mixed(i).start()
        load_round(i).start()
        return carry

    fixed[0].start()
    fixed[1].start()
    lax.fori_loop(0, 16, begin, 0)
    fixed[2].start()
    small = [
        pltpu.make_async_copy(src, dst, s_rest.at[i])
        for i, (src, dst) in enumerate(((prev_ref, prev_o), (next_ref, next_o), (bc_s, bc_o)))
    ]
    small[0].start()
    small[1].start()
    fixed[0].wait()
    fixed[1].wait()

    def xz_copy(i):
        cols = pl.ds(pl.multiple_of(i * 512, 512), 512)
        return pltpu.make_async_copy(xz_s.at[i], xz_o.at[:, cols], s_xz.at[i])

    def out_copy(i):
        rows = pl.ds(pl.multiple_of(i * 256, 256), 256)
        return pltpu.make_async_copy(out_s.at[i], out_o.at[rows], s_out.at[i])

    def step(i, carry):
        load_mixed(i).wait()
        out_s[i] = dot1(mixed_ref[i], cot_ref[...], NN)
        out_copy(i).start()
        load_round(i).wait()
        xz_s[i] = dot1(normed_ref[...], round_ref[i], NN)
        xz_copy(i).start()
        return carry

    lax.fori_loop(0, 16, step, 0)
    fixed[2].wait()
    bc_s[...] = dot1(rbc_ref[:, :320], normed_ref[...], (((0,), (1,)), ((), ())))
    small[2].start()

    def finish(i, carry):
        out_copy(i).wait()
        xz_copy(i).wait()
        return carry

    lax.fori_loop(0, 16, finish, 0)
    for copy in small:
        copy.wait()


def grads(round_all, mixed_all, normed, rbc, cot, prev_grad, next_act):
    shape = jax.ShapeDtypeStruct
    hbm = pl.BlockSpec(memory_space=pl.ANY)
    dma = pltpu.SemaphoreType.DMA
    return pl.pallas_call(
        grads_kernel,
        out_shape=(
            shape((512, 8192), F32),
            shape((4096, 512), F32),
            shape((320, 512), F32),
            shape((SEQ, 512), BF16),
            shape((SEQ, 512), BF16),
        ),
        in_specs=[hbm] * 7,
        out_specs=(hbm,) * 5,
        scratch_shapes=[
            pltpu.VMEM((16, SEQ, 512), BF16),
            pltpu.VMEM((16, 256, SEQ), BF16),
            pltpu.VMEM((512, SEQ), BF16),
            pltpu.VMEM((SEQ, 384), BF16),
            pltpu.VMEM((SEQ, 512), BF16),
            pltpu.VMEM((16, 512, 512), F32),
            pltpu.VMEM((16, 256, 512), F32),
            pltpu.VMEM((320, 512), F32),
            dma((16,)),
            dma((16,)),
            dma((3,)),
            dma((16,)),
            dma((16,)),
            dma((3,)),
        ],
        compiler_params=pltpu.CompilerParams(vmem_limit_bytes=60 * 1024 * 1024),
        cost_estimate=pl.CostEstimate(
            flops=1_700_000_000, bytes_accessed=29_000_000, transcendentals=0
        ),
        name="grads",
    )(
        round_all.reshape(16, SEQ, 512),
        mixed_all.reshape(16, 256, SEQ),
        normed,
        rbc,
        cot,
        prev_grad,
        next_act,
    )


def per_device_four(
    act_in,
    saved_act,
    cotangent,
    weight_xz,
    weight_bcdt,
    weight_out,
    conv_x,
    conv_bc,
    dt_bias,
    a_log,
    d_skip,
    norm_gain,
):
    round_all, mixed_all, normed, rbc, prev_grad, next_act = chain(
        saved_act[0],
        act_in[0],
        cotangent[0],
        weight_xz[0],
        weight_bcdt[0],
        weight_out[0],
        conv_x[0],
        conv_bc[0],
        dt_bias,
        a_log,
        d_skip,
        norm_gain,
    )
    grad_xz, grad_out, grad_bcdt, prev_grad, next_act = grads(
        round_all, mixed_all, normed, rbc, cotangent[0], prev_grad, next_act
    )
    return (next_act[None], prev_grad[None], grad_xz[None], grad_bcdt[None], grad_out[None])


def solution(mesh):
    return jax.shard_map(
        per_device_four if mesh.shape["dp"] == 4 and mesh.shape["section"] > 1 else per_device,
        mesh=mesh,
        in_specs=(
            P("section", None, "dp"),
            P("section", None, "dp"),
            P("section", None, "dp"),
            P("section", "dp", None),
            P("section", None, "dp"),
            P("section", None, "dp"),
            P("section", None, "dp"),
            P("section", None, None),
            P("section", "dp"),
            P("section", "dp"),
            P("section", "dp"),
            P("section", "dp"),
        ),
        out_specs=(
            P("section", None, "dp"),
            P("section", None, "dp"),
            P("section", "dp", None),
            P("section", None, "dp"),
            P("section", None, "dp"),
        ),
        check_vma=False,
    )
```

```python
import functools

import jax
import jax.numpy as jnp
from jax import lax
from jax.experimental import pallas as pl
from jax.experimental.pallas import tpu as pltpu
from jax.sharding import PartitionSpec as P

D = 2048
HEAD_DIM = 64
NSTATE = 128
HEADS = 64
SEQ = 128
INNER = 4096
KCONV = 4
MAPS = 2 * NSTATE


def from_behind(x, axis, by):
    length = lax.axis_size(axis)
    return lax.ppermute(x, axis, [(i, (i + by) % length) for i in range(length)])


def swap(x, mask):
    length = lax.axis_size("dp")
    return lax.ppermute(x, "dp", [(i, i ^ mask) for i in range(length)])


def masks():
    length = lax.axis_size("dp")
    out = []
    bit = 1
    while bit < length:
        out.append(bit)
        bit *= 2
    return out


def sum_all(x):
    for bit in masks():
        x = x + swap(x, bit)
    return x


def tied(x, other):
    return lax.optimization_barrier((x, other))[0]


def sum_first(part):
    length = lax.axis_size("dp")
    came = {j - 1: swap(part(j).astype(jnp.bfloat16), 1) for j in range(1, length, 2)}
    return {j: part(j) + came[j].astype(jnp.float32) for j in sorted(came, reverse=True)}


def sum_rest(held, after=None):
    first = begun = None
    for bit in masks()[1:]:
        sent = {j: held[j].astype(jnp.bfloat16) for j in held if j & bit}
        if after is not None and first is None:
            sent = {j: tied(x, after) for j, x in sent.items()}
        came = {j ^ bit: swap(x, bit) for j, x in sent.items()}
        if first is None:
            first = came[0]
            begun = sent[bit]
        held = {j: held[j] + came[j].astype(jnp.float32) for j in came}
    return held[0], first, begun


def sum_both(x, after):
    me = lax.axis_index("dp")
    odd = (me & 1) != 0
    x = x + swap(x, 1)
    mine = tied(jnp.where(odd, x[SEQ:], x[:SEQ]), after)
    for bit in masks()[1:]:
        mine = mine + swap(mine, bit)
    other = swap(mine, 1)
    return jnp.where(odd, other, mine), jnp.where(odd, mine, other)


def gather_cols(block, after=None):
    me = lax.axis_index("dp")
    length = lax.axis_size("dp")
    if after is not None:
        block = tied(block, after)
    held = [block]
    order = [0]
    for bit in reversed(masks()):
        held = held + [swap(b, bit) for b in held]
        order = order + [j ^ bit for j in order]
    by_mask = {j: b for j, b in zip(order, held)}
    level = [by_mask[j] for j in range(length)]
    for bit in masks():
        flip = (me & bit) != 0
        level = [jnp.where(flip, level[j ^ bit], level[j]) for j in range(length)]
    return jnp.concatenate(level, axis=1), held[-1]


def causal_conv(values, kernel_taps):
    kernel = kernel_taps.shape[0]
    length = values.shape[0]
    padded = jnp.pad(values, ((kernel - 1, 0), (0, 0)))
    running = jnp.zeros_like(values)
    for offset in range(kernel):
        running = running + kernel_taps[offset] * padded[offset : offset + length]
    return running


def mixer(proj_x, proj_z, proj_dt, scores, conv_taps, dt_offset, log_rate, skip_gain):
    length, width = proj_x.shape
    nheads = dt_offset.shape[0]
    head_width = width // nheads
    xconv = jax.nn.silu(causal_conv(proj_x, conv_taps))
    steps = jax.nn.softplus(proj_dt + dt_offset)
    position = jnp.arange(length)
    causal = position[:, None] >= position[None, :]
    cumul = jnp.dot(
        causal.astype(jnp.float32), steps * -jnp.exp(log_rate), precision=lax.Precision.HIGHEST
    )
    heads_cum = cumul.T
    spread = heads_cum[:, :, None] - heads_cum[:, None, :]
    decay = jnp.where(causal[None], jnp.exp(jnp.where(causal[None], spread, 0.0)), 0.0)
    weights = decay * scores[None] * steps.T[:, None, :]
    heads_in = xconv.reshape(length, nheads, head_width)
    result = jnp.einsum("hts,shp->thp", weights, heads_in, precision=lax.Precision.HIGH)
    result = result + skip_gain[None, :, None] * heads_in
    gate_in = jax.nn.silu(proj_z.reshape(length, nheads, head_width))
    return (result * gate_in).reshape(length, width)


def times_transposed(left, right):
    return lax.dot_general(
        left, right, (((1,), (1,)), ((), ())), preferred_element_type=jnp.float32
    )


def transposed_times(left, right):
    return lax.dot_general(
        left, right, (((0,), (0,)), ((), ())), preferred_element_type=jnp.float32
    )


def per_device(
    act_in,
    saved_act,
    cotangent,
    weight_xz,
    weight_bcdt,
    weight_out,
    conv_x,
    conv_bc,
    dt_bias,
    a_log,
    d_skip,
    norm_gain,
):
    input_rows = act_in[0]
    saved_rows = saved_act[0]
    cot_rows = cotangent[0]
    local_xz = weight_xz[0]
    local_bcdt = weight_bcdt[0]
    local_out = weight_out[0]
    taps_x = conv_x[0]
    taps_bc = conv_bc[0]
    dt_offset = dt_bias[0]
    log_rate = a_log[0]
    skip_gain = d_skip[0]
    gain_local = norm_gain[0]
    own_heads = dt_offset.shape[0]
    me = lax.axis_index("dp")
    head_first = me * own_heads
    width = own_heads * HEAD_DIM

    def whole_act(pre_part):
        return jax.nn.silu(causal_conv(pre_part, taps_bc))

    both = jnp.concatenate([saved_rows, input_rows], axis=0)
    both_values = both.astype(jnp.float32)
    squares = jnp.sum(both_values * both_values, axis=1, keepdims=True)
    def xz_part(j):
        cols = lax.dynamic_slice_in_dim(local_xz, (me ^ j) * 2 * width, 2 * width, 1)
        return jnp.dot(both, cols, preferred_element_type=jnp.float32)

    held_xz = sum_first(xz_part)
    back_raw, back_first, back_begun = sum_rest({j: x[:SEQ] for j, x in held_xz.items()})
    back_small, forward_small = sum_both(
        jnp.concatenate([times_transposed(both, local_bcdt), squares], axis=1), back_begun
    )

    def mixed_part(j):
        taken = lax.dynamic_slice_in_dim(local_out, (me ^ j) * width, width, 0)
        return times_transposed(cot_rows, taken)

    d_mixed = sum_rest(sum_first(mixed_part), back_begun)[0]
    forward_raw = sum_rest({j: x[SEQ:] for j, x in held_xz.items()}, back_first)[0]

    def project(rows, small, raw_xz):
        raw_cols = small[:, : MAPS + HEADS]
        scales = lax.rsqrt(small[:, MAPS + HEADS :] / D + 1e-05)
        return (rows.astype(jnp.float32), scales, raw_xz, raw_cols)

    back_proj = project(saved_rows, back_small, back_raw)
    forward_proj = project(input_rows, forward_small, forward_raw)

    def gate_parts(projected):
        values, scales, raw_xz, raw_cols = projected
        own_xz = raw_xz * scales
        whole_cols = raw_cols * scales
        pre_part = whole_cols[:, :MAPS]
        maps = whole_act(pre_part).astype(jnp.bfloat16)
        own_dt = lax.dynamic_slice_in_dim(whole_cols[:, MAPS:], head_first, own_heads, 1)
        split_xz = own_xz.reshape(SEQ, own_heads, 2, HEAD_DIM)
        mix_x = split_xz[:, :, 0].reshape(SEQ, width)
        mix_z = split_xz[:, :, 1].reshape(SEQ, width)
        scores = times_transposed(maps[:, NSTATE:], maps[:, :NSTATE])

        def local_mix(in_x, in_z, in_dt, in_scores):
            return mixer(in_x, in_z, in_dt, in_scores, taps_x, dt_offset, log_rate, skip_gain)

        gated, mix_back = jax.vjp(local_mix, mix_x, mix_z, own_dt, scores)
        return (gated, mix_back, maps, pre_part)

    values, scales, raw_xz, raw_cols = back_proj
    gated, mix_back, maps, pre_part = gate_parts(back_proj)
    gained = gated * gain_local
    row_sums = sum_all(
        jnp.stack([jnp.sum(gated * gated, axis=1), jnp.sum(d_mixed * gained, axis=1)])
    )
    inverse = lax.rsqrt(row_sums[0] / INNER + 1e-05)[:, None]
    dots = row_sums[1][:, None]
    mixed_in = (gained * inverse).astype(jnp.bfloat16)
    d_gated = inverse * gain_local * d_mixed - gated * (inverse * inverse * inverse) * dots / INNER
    d_px, d_pz, d_pdt, d_scores = mix_back(d_gated)
    own_round = (
        jnp.stack(
            [
                d_px.reshape(SEQ, own_heads, HEAD_DIM),
                d_pz.reshape(SEQ, own_heads, HEAD_DIM),
            ],
            axis=2,
        )
        .reshape(SEQ, own_heads * 2 * HEAD_DIM)
        .astype(jnp.bfloat16)
    )
    round_xz, round_last = gather_cols(own_round)
    inner_own = jnp.sum(own_round.astype(jnp.float32) * raw_xz, axis=1, keepdims=True)
    wide_maps = maps.astype(jnp.float32)
    d_maps = jnp.concatenate(
        [
            jnp.dot(d_scores.T, wide_maps[:, NSTATE:], precision=lax.Precision.HIGH),
            jnp.dot(d_scores, wide_maps[:, :NSTATE], precision=lax.Precision.HIGH),
        ],
        axis=1,
    )
    d_dt_full = lax.dynamic_update_slice_in_dim(
        jnp.zeros((SEQ, HEADS), jnp.float32), d_pdt, head_first, 1
    )
    summed = sum_all(jnp.concatenate([d_maps, d_dt_full, inner_own], axis=1))
    conv_out, conv_back = jax.vjp(whole_act, pre_part)
    d_pre = conv_back(summed[:, :MAPS])[0]
    round_bcdt = jnp.concatenate([d_pre, summed[:, MAPS : MAPS + HEADS]], axis=1).astype(
        jnp.bfloat16
    )
    inner_sum = summed[:, MAPS + HEADS :] + jnp.sum(
        round_bcdt.astype(jnp.float32) * raw_cols, axis=1, keepdims=True
    )

    fwd_gated = gate_parts(forward_proj)[0]
    fwd_all, _ = gather_cols((fwd_gated * gain_local).astype(jnp.bfloat16), round_last)
    fwd_sum = sum_all(jnp.sum(fwd_gated * fwd_gated, axis=1)[None])
    fwd_inverse = lax.rsqrt(fwd_sum[0] / INNER + 1e-05)[:, None]
    mixed = jnp.dot(fwd_all, local_out, preferred_element_type=jnp.float32) * fwd_inverse
    section_out = (input_rows.astype(jnp.float32) + mixed).astype(jnp.bfloat16)
    next_act = from_behind(section_out, "section", 1)

    normed = (values * scales).astype(jnp.bfloat16)
    d_normed = times_transposed(round_xz, local_xz)
    d_normed = d_normed + jnp.dot(round_bcdt, local_bcdt, preferred_element_type=jnp.float32)
    d_norm_in = scales * d_normed - values * (scales * scales * scales) * inner_sum / D
    d_input = (cot_rows.astype(jnp.float32) + d_norm_in).astype(jnp.bfloat16)
    prev_grad = from_behind(d_input, "section", -1)

    grad_out = transposed_times(gather_cols(mixed_in, round_last)[0], cot_rows)
    grad_xz = transposed_times(normed, round_xz)
    grad_bcdt = transposed_times(round_bcdt, normed)
    return (next_act[None], prev_grad[None], grad_xz[None], grad_bcdt[None], grad_out[None])


BF16 = jnp.bfloat16
F32 = jnp.float32
MESH_ID = pl.DeviceIdType.MESH
NN = (((1,), (0,)), ((), ()))
NT = (((1,), (1,)), ((), ()))
TN = (((0,), (0,)), ((), ()))


def dot1(a, b, dims):
    return lax.dot_general(a, b, dims, preferred_element_type=F32)


def dot_full(a, b, dims):
    return lax.dot_general(
        a, b, dims, precision=lax.Precision.HIGHEST, preferred_element_type=F32
    )


def halves(x):
    high = x.astype(BF16)
    return high, (x - high.astype(F32)).astype(BF16)


def dot3(a, b, dims):
    a_high, a_low = halves(a)
    b_high, b_low = halves(b)
    return dot1(a_high, b_high, dims) + (dot1(a_high, b_low, dims) + dot1(a_low, b_high, dims))


def sigmoid(x):
    return 1.0 / (1.0 + jnp.exp(-x))


def d_silu(x, s):
    return s * (1.0 + x * (1.0 - s))


def rows_of(shape):
    return lax.broadcasted_iota(jnp.int32, shape, 0)


def lanes_of(shape):
    return lax.broadcasted_iota(jnp.int32, shape, 1)


def conv_rows(v, taps):
    row = rows_of(v.shape)
    out = taps[KCONV - 1 : KCONV] * v
    for s in range(1, KCONV):
        moved = jnp.where(row >= s, pltpu.roll(v, s, 0), 0.0)
        out = out + taps[KCONV - 1 - s : KCONV - s] * moved
    return out


def conv_rows_back(d, taps):
    row = rows_of(d.shape)
    out = taps[KCONV - 1 : KCONV] * d
    for s in range(1, KCONV):
        moved = jnp.where(row < SEQ - s, pltpu.roll(d, SEQ - s, 0), 0.0)
        out = out + taps[KCONV - 1 - s : KCONV - s] * moved
    return out


def as_column(row):
    return jnp.broadcast_to(row, (SEQ, SEQ)).T


def row_sums(values):
    return dot_full(jnp.ones((8, values.shape[1]), F32), values, NT)


def wide(col, n):
    return jnp.concatenate([col] * n, axis=1)


def scratch_table():
    dma = pltpu.SemaphoreType.DMA
    vm = pltpu.VMEM
    table = dict(
        w=vm((16, 512, 512), BF16),
        wo=vm((16, 256, 512), BF16),
        wbc=vm((384, 512), BF16),
        x2=vm((2, SEQ, 512), BF16),
        cot=vm((SEQ, 512), BF16),
        sec=vm((2, SEQ, 512), BF16),
        normed=vm((512, SEQ), BF16),
        xzd_s=vm((2, 2, 4, SEQ, 512), BF16),
        xzd_r=vm((2, 2, 4, SEQ, 512), BF16),
        xzy_s=vm((2, 4, SEQ, 512), BF16),
        xzy_r=vm((2, 4, SEQ, 512), BF16),
        md_s=vm((2, 4, SEQ, 256), BF16),
        md_r=vm((2, 4, SEQ, 256), BF16),
        my_s=vm((4, SEQ, 256), BF16),
        my_r=vm((4, SEQ, 256), BF16),
        smd_s=vm((SEQ, 384), F32),
        smd_r=vm((SEQ, 384), F32),
        smy_s=vm((SEQ, 384), BF16),
        smy_r=vm((SEQ, 384), BF16),
        sm=vm((2, SEQ, 384), F32),
        sq=vm((4, 8, SEQ), F32),
        rs=vm((4, 8, SEQ), F32),
        rf=vm((4, 8, SEQ), F32),
        tg=vm((4, 24, SEQ), F32),
        dsd_s=vm((64, SEQ), F32),
        dsd_r=vm((64, SEQ), F32),
        dsy_s=vm((64, SEQ), F32),
        dsy_r=vm((64, SEQ), F32),
        ds_tot=vm((2, 64, SEQ), F32),
        ds_acc=vm((2, 64, SEQ), F32),
        ga_round=vm((4, 4, SEQ, 512), BF16),
        ga_mix=vm((4, 4, 256, SEQ), BF16),
        ga_fwd=vm((4, 4, SEQ, 256), BF16),
        big_l=vm((16, SEQ, SEQ), F32),
        xc=vm((8, SEQ, SEQ), F32),
        ys=vm((8, SEQ, SEQ), F32),
        gz=vm((8, SEQ, SEQ), F32),
        dcv=vm((8, SEQ, SEQ), F32),
        dzs=vm((8, SEQ, SEQ), F32),
        dm=vm((8, SEQ, SEQ), F32),
        raw=vm((4, SEQ, 512), F32),
        acc0=vm((SEQ, SEQ), F32),
        acc1=vm((SEQ, SEQ), F32),
        dn=vm((SEQ, 512), F32),
        pdt=vm((SEQ, SEQ), F32),
        dtT=vm((2, 16, SEQ), F32),
        cumT=vm((2, 16, SEQ), F32),
        sgT=vm((16, SEQ), F32),
        negA=vm((16, SEQ), F32),
        dirT=vm((16, SEQ), F32),
        rowT=vm((16, SEQ), F32),
        scores=vm((2, SEQ, SEQ), F32),
        maps=vm((SEQ, 256), BF16),
        dcm=vm((SEQ, 256), F32),
        scale=vm((2, SEQ, SEQ), F32),
        cx=vm((8, KCONV, SEQ), F32),
        gain=vm((8, 1, SEQ), F32),
        dsk=vm((8, 1, SEQ), F32),
        rbc=vm((SEQ, 384), BF16),
        s_w=dma((16,)),
        s_wo=dma((16,)),
        s_in=dma((4,)),
        s_out=dma((10,)),
    )
    for name, shape in dict(
        xzd=(2, 2, 4), xzy=(2, 4), md=(2, 4), my=(4,), smd=(1,), smy=(1,), smt=(1,), sq=(3,), rs=(3,),
        rf=(3,), tg=(3,), dsd=(1,), dsy=(1,), dst=(1,), ry=(4,), rd=(4,), rw=(4,), my2=(4,), md2=(4,),
        mw=(4,), fy=(4,), fd=(4,), fw=(4,), sec=(2,),
    ).items():
        table["a_" + name] = dma(shape)
        table["b_" + name] = dma(shape)
    return table


class Names:
    pass


def chain_kernel(names, *refs):
    (saved_h, act_h, cot_h, wxz_h, wbc_h, wout_h, convx, convbc, dtb, alog, dskip, gain_in,
     round_o, mixed_o, normed_o, rbc_o, prev_o, next_o) = refs[:18]
    v = Names()
    for name, ref in zip(names, refs[18:]):
        setattr(v, name, ref)
    saved, act, cot = v.x2.at[0], v.x2.at[1], v.cot

    me = lax.axis_index("dp")
    core = lax.rem(me, 2)
    mate = me + 1 - 2 * core
    ypeer = me + 2 - 4 * (me // 2)
    diag = 3 - me
    peers = (mate, ypeer, diag)
    sections = lax.axis_size("section")
    place = lax.axis_index("section")
    ahead = lax.rem(place + 1, sections)
    behind = lax.rem(place + sections - 1, sections)

    def remote(src, dst, kind, index, dev):
        return pltpu.make_async_remote_copy(
            src_ref=src,
            dst_ref=dst,
            send_sem=getattr(v, "a_" + kind).at[index],
            recv_sem=getattr(v, "b_" + kind).at[index],
            device_id={"dp": dev},
            device_id_type=MESH_ID,
        )

    def xzd(mb, role, j):
        return remote(v.xzd_s.at[mb, role, j], v.xzd_r.at[mb, role, j], "xzd", (mb, role, j), mate)

    def xzy(mb, j):
        return remote(v.xzy_s.at[mb, j], v.xzy_r.at[mb, j], "xzy", (mb, j), ypeer)

    def md(role, j):
        return remote(v.md_s.at[role, j], v.md_r.at[role, j], "md", (role, j), mate)

    def my(j):
        return remote(v.my_s.at[j], v.my_r.at[j], "my", (j,), ypeer)

    def smd():
        return remote(v.smd_s, v.smd_r, "smd", (0,), mate)

    def smy():
        return remote(v.smy_s, v.smy_r, "smy", (0,), ypeer)

    def smt(mb):
        return remote(v.sm.at[mb], v.sm.at[mb], "smt", (0,), mate)

    def spread(buf, kind, i, slot):
        return remote(buf.at[slot], buf.at[slot], kind, (i,), peers[i])

    def spread_start(buf, kind):
        for i in range(3):
            spread(buf, kind, i, me).start()

    def spread_wait(buf, kind):
        for i in range(3):
            spread(buf, kind, i, peers[i]).wait_recv()

    def dsd():
        return remote(v.dsd_s, v.dsd_r, "dsd", (0,), mate)

    def dsy():
        return remote(v.dsy_s, v.dsy_r, "dsy", (0,), ypeer)

    def dst(half):
        return remote(v.ds_tot.at[half], v.ds_tot.at[half], "dst", (0,), mate)

    def gather(buf, kind, q, j, dev):
        return remote(buf.at[q, j], buf.at[q, j], kind, (j,), dev)

    def send_section(i):
        return pltpu.make_async_remote_copy(
            src_ref=v.sec.at[i],
            dst_ref=(prev_o, next_o)[i],
            send_sem=v.a_sec.at[i],
            recv_sem=v.b_sec.at[i],
            device_id={"section": (behind, ahead)[i]},
            device_id_type=MESH_ID,
        )

    def hand_out(kind, q):
        buf, out = ((v.ga_round, round_o), (v.ga_mix, mixed_o))[kind]
        return pltpu.make_async_copy(buf.at[q], out.at[q], v.s_out.at[4 * kind + q])

    def load_w(i):
        cols = pl.ds(pl.multiple_of(i * 512, 512), 512)
        return pltpu.make_async_copy(wxz_h.at[:, cols], v.w.at[i], v.s_w.at[i])

    def load_wo(i):
        return pltpu.make_async_copy(
            wout_h.at[pl.ds(pl.multiple_of(i * 256, 256), 256)], v.wo.at[i], v.s_wo.at[i]
        )

    def loop(fn, n=4):
        def step(j, carry):
            fn(j)
            return carry
        lax.fori_loop(0, n, step, 0)

    def follow(j, begin):
        @pl.when(j >= 1)
        def _():
            begin(j - 1)

        @pl.when(j == 3)
        def _():
            begin(3)

    barrier = pltpu.get_barrier_semaphore()
    for peer in peers:
        pl.semaphore_signal(barrier, 1, device_id={"dp": peer}, device_id_type=MESH_ID)
    for other in (ahead, behind):
        pl.semaphore_signal(barrier, 1, device_id={"section": other}, device_id_type=MESH_ID)

    loads = [
        pltpu.make_async_copy(src, dst, v.s_in.at[i])
        for i, (src, dst) in enumerate(
            ((saved_h, saved), (act_h, act), (wbc_h, v.wbc.at[0:320]), (cot_h, v.cot))
        )
    ]
    loads[0].start()
    for i in range(2):
        load_w(4 * diag + i).start()
    load_w(4 * ypeer).start()

    def xz_first(j, ready=None):
        load_w(4 * diag + j).wait()
        v.xzd_s[0, 0, j] = dot1(saved[...], v.w[4 * diag + j], NN).astype(BF16)
        if ready is not None:
            ready()
        xzd(0, 0, j).start()

    def xz_sum(mb, x_ref):
        def fn(j):
            part = dot1(x_ref[...], v.w[4 * ypeer + j], NN)
            xzd(mb, 0, j).wait_recv()
            v.xzy_s[mb, j] = (part + v.xzd_r[mb, 0, j].astype(F32)).astype(BF16)
        return fn

    def xz_back(j):
        load_w(4 * ypeer + j).wait()
        xz_sum(0, saved)(j)
        xzy(0, j).start()

    v.wbc[320:] = jnp.zeros((64, 512), BF16)
    loads[0].wait()
    xz_first(0, lambda: pl.semaphore_wait(barrier, 5))
    for load in loads[1:]:
        load.start()
    load_w(4 * diag + 2).start()
    load_w(4 * ypeer + 1).start()
    xz_first(1)
    load_w(4 * diag + 3).start()
    load_w(4 * ypeer + 2).start()
    load_w(4 * ypeer + 3).start()
    loads[1].wait()
    loads[2].wait()
    v.smd_s[...] = dot1(v.x2[1 - core], v.wbc[...], NT)
    smd().start()
    xz_back(0)
    for q in (diag, ypeer):
        loop(lambda j: load_wo(4 * q + j).start())
    for q in (mate, me):
        loop(lambda j: load_w(4 * q + j).start())
    for q in (mate, me):
        loop(lambda j: load_wo(4 * q + j).start())
    xz_first(2)
    xz_back(1)
    xz_first(3)
    own_small = dot1(v.x2[core], v.wbc[...], NT)
    smd().wait_recv()
    own_small = own_small + v.smd_r[...]
    v.smy_s[...] = own_small.astype(BF16)
    smy().start()
    v.sm[core] = own_small
    xz_back(2)
    squares = []
    for x_ref in (saved, act):
        wide_x = x_ref[...].astype(F32)
        squares.append(row_sums(wide_x * wide_x))
    v.sq[me] = jnp.where(rows_of((8, SEQ)) == 0, squares[0], squares[1])
    spread_start(v.sq, "sq")
    xz_back(3)
    loads[3].wait()

    def m_first(j):
        load_wo(4 * diag + j).wait()
        v.md_s[0, j] = dot1(cot[...], v.wo[4 * diag + j], NT).astype(BF16)
        md(0, j).start()

    loop(m_first)

    def m_sum(j):
        load_wo(4 * ypeer + j).wait()
        part = dot1(cot[...], v.wo[4 * ypeer + j], NT)
        md(0, j).wait_recv()
        v.my_s[j] = (part + v.md_r[0, j].astype(F32)).astype(BF16)

    loop(m_sum)

    def xz_mate(j):
        load_w(4 * mate + j).wait()
        v.xzd_s[0, 1, j] = dot1(saved[...], v.w[4 * mate + j], NN).astype(BF16)
        xzd(0, 1, j).start()

    loop(xz_mate)

    def m_mate(j):
        load_wo(4 * mate + j).wait()
        v.md_s[1, j] = dot1(cot[...], v.wo[4 * mate + j], NT).astype(BF16)
        md(1, j).start()

    loop(m_mate)

    def fwd_first(j):
        v.xzd_s[1, 0, j] = dot1(act[...], v.w[4 * diag + j], NN).astype(BF16)
        xzd(1, 0, j).start()

    loop(fwd_first)

    smy().wait_recv()
    v.sm[core] = v.sm[core] + v.smy_r[...].astype(F32)
    smt(core).start()

    expand = (lanes_of((16, 1024)) // HEAD_DIM == rows_of((16, 1024))).astype(F32)
    skip_wide = dot_full(dskip[...], expand, NN)
    for p in range(8):
        cols = slice(128 * p, 128 * p + 128)
        v.cx[p] = convx[:, cols]
        v.gain[p] = gain_in[:, cols]
        v.dsk[p] = skip_wide[:, cols]
    bias_col = jnp.broadcast_to(dtb[...], (SEQ, 16)).T
    v.negA[...] = -jnp.exp(jnp.broadcast_to(alog[...], (SEQ, 16)).T)
    row_id = rows_of((SEQ, SEQ))
    lane_id = lanes_of((SEQ, SEQ))
    causal = row_id >= lane_id
    low = lane_id < HEAD_DIM

    spread_wait(v.sq, "sq")
    total_sq = v.sq[0] + v.sq[1] + v.sq[2] + v.sq[3]
    for mb in range(2):
        v.scale[mb] = lax.rsqrt(as_column(total_sq[mb : mb + 1]) / D + 1e-05)

    smt(1 - core).wait_recv()

    def prepare(mb):
        scale = v.scale[mb]
        small = v.sm[mb] * wide(scale, 3)
        conv = conv_rows(small[:, :MAPS], convbc[...])
        sig = sigmoid(conv)
        maps = (conv * sig).astype(BF16)
        v.scores[mb] = dot1(maps[:, NSTATE:], maps[:, :NSTATE], NT)
        if mb == 0:
            v.maps[...] = maps
            v.dcm[...] = d_silu(conv, sig)
        v.pdt[...] = small[:, MAPS:].T
        logits = v.pdt[pl.ds(pl.multiple_of(16 * me, 16), 16)] + bias_col
        steps = jnp.maximum(logits, 0.0) + jnp.log1p(jnp.exp(-jnp.abs(logits)))
        if mb == 0:
            v.sgT[...] = sigmoid(logits)
        v.dtT[mb] = steps
        v.cumT[mb] = dot_full(
            steps * v.negA[...], (row_id <= lane_id).astype(F32), NN
        )

    prepare(0)

    def split_pair(first, second):
        head_x = jnp.where(low, first, pltpu.roll(second, 64, 1))
        head_z = jnp.where(low, pltpu.roll(first, 64, 1), second)
        return head_x, head_z

    def mix(mb, pair, block, save):
        scale = v.scale[mb]
        x, z = split_pair(block[:, :128] * scale, block[:, 128:] * scale)
        conv = conv_rows(x, v.cx[pair])
        sig = sigmoid(conv)
        xc = conv * sig
        sig_z = sigmoid(z)
        gate = z * sig_z
        weights = []
        for k in range(2):
            head = pl.ds(2 * pair + k, 1)
            row = v.cumT[mb, head]
            decay = jnp.exp(jnp.where(causal, as_column(row) - row, -1e30))
            if save:
                v.big_l[2 * pair + k] = decay
            weights.append(decay * v.scores[mb] * v.dtT[mb, head])
        stacked = jnp.concatenate([jnp.where(low, xc, 0.0), jnp.where(low, 0.0, xc)], axis=0)
        y = dot3(jnp.concatenate(weights, axis=1), stacked, NN)
        if save:
            v.xc[pair] = xc
            v.ys[pair] = y
            v.gz[pair] = gate
            v.dcv[pair] = d_silu(conv, sig)
            v.dzs[pair] = d_silu(z, sig_z)
        return (y + v.dsk[pair] * xc) * gate

    def raw_block(mb, x_ref, j):
        return (
            dot1(x_ref[...], v.w[4 * me + j], NN)
            + v.xzd_r[mb, 1, j].astype(F32)
            + v.xzy_r[mb, j].astype(F32)
        )

    v.acc0[...] = jnp.zeros((SEQ, SEQ), F32)

    def stage_a(j):
        load_w(4 * me + j).wait()
        xzd(0, 1, j).wait_recv()
        xzy(0, j).wait_recv()
        follow(j, lambda i: my(i).start())
        raw = raw_block(0, saved, j)
        v.raw[j] = raw
        for k in range(2):
            gated = mix(0, 2 * j + k, raw[:, 256 * k : 256 * k + 256], True)
            v.acc0[...] += gated * gated

    loop(stage_a)

    def fwd_mate(j):
        v.xzd_s[1, 1, j] = dot1(act[...], v.w[4 * mate + j], NN).astype(BF16)
        xzd(1, 1, j).start()

    loop(xz_sum(1, act))
    loop(fwd_mate)

    v.acc1[...] = jnp.zeros((SEQ, SEQ), F32)

    def stage_b(j):
        load_wo(4 * me + j).wait()
        md(1, j).wait_recv()
        my(j).wait_recv()

        @pl.when(j == 2)
        def _():
            xzy(1, 0).start()

        d_mixed = (
            dot1(cot[...], v.wo[4 * me + j], NT)
            + v.md_r[1, j].astype(F32)
            + v.my_r[j].astype(F32)
        )
        for k in range(2):
            pair = 2 * j + k
            part = d_mixed[:, 128 * k : 128 * k + 128]
            v.dm[pair] = part
            gated = (v.ys[pair] + v.dsk[pair] * v.xc[pair]) * v.gz[pair]
            v.acc1[...] += part * v.gain[pair] * gated

    loop(stage_b)

    v.rs[me] = jnp.where(
        rows_of((8, SEQ)) == 0, row_sums(v.acc0[...]), row_sums(v.acc1[...])
    )
    spread_start(v.rs, "rs")
    loop(lambda j: xzy(1, j + 1).start(), 3)
    prepare(1)
    for k in range(4):
        cols = slice(128 * k, 128 * k + 128)
        normed = (saved[:, cols].astype(F32) * v.scale[0]).astype(BF16)
        v.normed[cols] = normed.astype(F32).T.astype(BF16)
    normed_copy = pltpu.make_async_copy(v.normed, normed_o, v.s_out.at[8])
    normed_copy.start()
    spread_wait(v.rs, "rs")
    total_rs = v.rs[0] + v.rs[1] + v.rs[2] + v.rs[3]
    v.acc0[...] = lax.rsqrt(as_column(total_rs[0:1]) / INNER + 1e-05)
    v.acc1[...] = as_column(total_rs[1:2]) / INNER

    v.pdt[...] = jnp.zeros((SEQ, SEQ), F32)
    v.ds_acc[...] = jnp.zeros((2, 64, SEQ), F32)
    head_rows = (
        lanes_of((8, SEQ)) // HEAD_DIM == rows_of((8, SEQ))
    ).astype(F32)

    def stage_c(j):
        inverse = v.acc0[...]
        lower = inverse * inverse * inverse * v.acc1[...]
        for k in range(2):
            pair = 2 * j + k
            xc = v.xc[pair]
            y = v.ys[pair]
            gate = v.gz[pair]
            skip = v.dsk[pair]
            gained = inverse * v.gain[pair]
            y_full = y + skip * xc
            gated = y_full * gate
            v.ga_mix[me, j, 128 * k : 128 * k + 128] = (gated * gained).T.astype(BF16)
            d_gated = gained * v.dm[pair] - gated * lower
            d_y = d_gated * gate
            d_gate = d_gated * y_full
            d_ys = jnp.concatenate([jnp.where(low, d_y, 0.0), jnp.where(low, 0.0, d_y)], axis=0)
            d_w = dot3(d_ys, xc, NT)
            scores = v.scores[0]
            weights = []
            d_scores = None
            for h in range(2):
                head = pl.ds(2 * pair + h, 1)
                decay = v.big_l[2 * pair + h]
                steps = v.dtT[0, head]
                scored = decay * scores
                weights.append(scored * steps)
                d_head = d_w[SEQ * h : SEQ * h + SEQ]
                term = d_head * (decay * steps)
                d_scores = term if d_scores is None else d_scores + term
                v.dirT[head] = jnp.sum(d_head * scored, axis=0, keepdims=True)
            v.ds_acc[0] += d_scores[:64]
            v.ds_acc[1] += d_scores[64:]
            sums = dot_full(head_rows, d_y * y, NT)
            v.rowT[pl.ds(2 * pair, 1)] = sums[0:1]
            v.rowT[pl.ds(2 * pair + 1, 1)] = sums[1:2]
            d_xc = dot3(jnp.concatenate(weights, axis=0), d_ys, TN) + skip * d_y
            d_x = conv_rows_back(d_xc * v.dcv[pair], v.cx[pair])
            d_z = d_gate * v.dzs[pair]
            first, second = split_pair(d_x, d_z)
            first = first.astype(BF16)
            second = second.astype(BF16)
            v.ga_round[me, j, :, 256 * k : 256 * k + 128] = first
            v.ga_round[me, j, :, 256 * k + 128 : 256 * k + 256] = second
            v.pdt[...] += (
                first.astype(F32) * v.raw[j, :, 256 * k : 256 * k + 128]
                + second.astype(F32) * v.raw[j, :, 256 * k + 128 : 256 * k + 256]
            )
        gather(v.ga_round, "rd", me, j, mate).start()
        gather(v.ga_mix, "md2", me, j, mate).start()

    loop(stage_c)
    hand_out(0, me).start()
    hand_out(1, me).start()

    v.dsd_s[...] = v.ds_acc[1 - core]
    dsd().start()
    d_cum = v.rowT[...] - v.dtT[0] * v.dirT[...]
    d_a = dot_full(d_cum, (row_id >= lane_id).astype(F32), NN)
    v.tg[me, 0:16] = (v.dirT[...] + v.negA[...] * d_a) * v.sgT[...]
    v.tg[me, 16:24] = row_sums(v.pdt[...])
    spread_start(v.tg, "tg")
    dsd().wait_recv()
    v.dsy_s[...] = v.ds_acc[core] + v.dsd_r[...]
    dsy().start()

    v.acc0[...] = jnp.zeros((SEQ, SEQ), F32)

    def stage_e(j):
        xzd(1, 1, j).wait_recv()
        xzy(1, j).wait_recv()
        follow(j, lambda i: gather(v.ga_round, "ry", me, i, ypeer).start())
        raw = raw_block(1, act, j)
        for k in range(2):
            pair = 2 * j + k
            gated = mix(1, pair, raw[:, 256 * k : 256 * k + 256], False)
            v.acc0[...] += gated * gated
            v.ga_fwd[me, j, :, 128 * k : 128 * k + 128] = (gated * v.gain[pair]).astype(BF16)
        gather(v.ga_fwd, "fd", me, j, mate).start()

    loop(stage_e)
    v.rf[me] = row_sums(v.acc0[...])
    spread_start(v.rf, "rf")

    v.dn[...] = jnp.zeros((SEQ, 512), F32)

    def add_dn(q, j):
        v.dn[...] += dot1(v.ga_round[q, j], v.w[4 * q + j], NT)

    loop(lambda j: add_dn(me, j))

    dsy().wait_recv()
    v.ds_tot[core] = v.dsy_s[...] + v.dsy_r[...]
    dst(core).start()

    def add_mate(j):
        gather(v.ga_round, "rd", mate, j, mate).wait_recv()
        add_dn(mate, j)

    loop(add_mate)
    hand_out(0, mate).start()
    dst(1 - core).wait_recv()
    d_scores = jnp.concatenate([v.ds_tot[0], v.ds_tot[1]], axis=0)
    ds_high, ds_low = halves(d_scores)
    maps = v.maps[...]
    d_input_map = dot1(ds_high, maps[:, NSTATE:], TN) + dot1(ds_low, maps[:, NSTATE:], TN)
    d_output_map = dot1(ds_high, maps[:, :NSTATE], NN) + dot1(ds_low, maps[:, :NSTATE], NN)
    d_maps = jnp.concatenate([d_input_map, d_output_map], axis=1)
    d_pre = conv_rows_back(d_maps * v.dcm[...], convbc[...])
    v.rbc[:, :MAPS] = d_pre.astype(BF16)
    spread_wait(v.tg, "tg")
    v.pdt[...] = jnp.zeros((SEQ, SEQ), F32)
    for q in range(4):
        v.pdt[16 * q : 16 * q + 16] = v.tg[q, 0:16]
    v.rbc[:, MAPS:] = v.pdt[...].T.astype(BF16)
    rbc_copy = pltpu.make_async_copy(v.rbc, rbc_o, v.s_out.at[9])
    rbc_copy.start()
    product = v.rbc[...].astype(F32) * v.sm[0]
    inner = row_sums(product[:, :128] + product[:, 128:256] + product[:, 256:])
    inner = inner + v.tg[0, 16:24] + v.tg[1, 16:24] + v.tg[2, 16:24] + v.tg[3, 16:24]
    v.acc1[...] = as_column(inner[0:1]) / D
    v.dn[...] += dot1(v.rbc[...], v.wbc[...], NN)

    def pass_on(j):
        gather(v.ga_round, "ry", ypeer, j, ypeer).wait_recv()
        follow(j, lambda i: gather(v.ga_fwd, "fy", me, i, ypeer).start())
        gather(v.ga_round, "rw", ypeer, j, mate).start()
        add_dn(ypeer, j)

    loop(pass_on)
    hand_out(0, ypeer).start()

    def add_diag(j):
        gather(v.ga_round, "rw", diag, j, mate).wait_recv()
        add_dn(diag, j)

    loop(add_diag)
    hand_out(0, diag).start()
    for k in range(4):
        cols = slice(128 * k, 128 * k + 128)
        scale = v.scale[0]
        d_in = scale * v.dn[:, cols] - saved[:, cols].astype(F32) * (
            scale * scale * scale
        ) * v.acc1[...]
        v.sec[0, :, cols] = (cot[:, cols].astype(F32) + d_in).astype(BF16)
    send_section(0).start()

    v.dn[...] = jnp.zeros((SEQ, 512), F32)

    def add_out(q, j):
        v.dn[...] += dot1(v.ga_fwd[q, j], v.wo[4 * q + j], NN)

    loop(lambda j: add_out(me, j))

    def out_mate(j):
        gather(v.ga_fwd, "fd", mate, j, mate).wait_recv()
        add_out(mate, j)

    loop(out_mate)
    loop(lambda j: gather(v.ga_mix, "md2", mate, j, mate).wait_recv())
    hand_out(1, mate).start()
    spread_wait(v.rf, "rf")
    total_rf = v.rf[0] + v.rf[1] + v.rf[2] + v.rf[3]
    v.acc0[...] = lax.rsqrt(as_column(total_rf[0:1]) / INNER + 1e-05)

    def out_peer(j):
        gather(v.ga_fwd, "fy", ypeer, j, ypeer).wait_recv()
        follow(j, lambda i: gather(v.ga_mix, "my2", me, i, ypeer).start())
        gather(v.ga_fwd, "fw", ypeer, j, mate).start()
        add_out(ypeer, j)

    loop(out_peer)

    def out_diag(j):
        gather(v.ga_fwd, "fw", diag, j, mate).wait_recv()
        add_out(diag, j)

    loop(out_diag)
    for k in range(4):
        cols = slice(128 * k, 128 * k + 128)
        mixed = v.dn[:, cols] * v.acc0[...]
        v.sec[1, :, cols] = (act[:, cols].astype(F32) + mixed).astype(BF16)
    send_section(1).start()

    def pass_mix(j):
        gather(v.ga_mix, "my2", ypeer, j, ypeer).wait_recv()
        gather(v.ga_mix, "mw", ypeer, j, mate).start()

    loop(pass_mix)
    hand_out(1, ypeer).start()
    loop(lambda j: gather(v.ga_mix, "mw", diag, j, mate).wait_recv())
    hand_out(1, diag).start()

    smd().wait_send()
    smy().wait_send()
    smt(core).wait_send()
    dsd().wait_send()
    dsy().wait_send()
    dst(core).wait_send()
    for buf, kind in ((v.sq, "sq"), (v.rs, "rs"), (v.rf, "rf"), (v.tg, "tg")):
        for i in range(3):
            spread(buf, kind, i, me).wait_send()

    def drain(j):
        for mb in range(2):
            for role in range(2):
                xzd(mb, role, j).wait_send()
            xzy(mb, j).wait_send()
        md(0, j).wait_send()
        md(1, j).wait_send()
        my(j).wait_send()
        for buf, kinds in (
            (v.ga_round, ("ry", "rd", "rw")),
            (v.ga_mix, ("my2", "md2", "mw")),
            (v.ga_fwd, ("fy", "fd", "fw")),
        ):
            gather(buf, kinds[0], me, j, ypeer).wait_send()
            gather(buf, kinds[1], me, j, mate).wait_send()
            gather(buf, kinds[2], ypeer, j, mate).wait_send()

    loop(drain)
    for i in range(2):
        send_section(i).wait()
    normed_copy.wait()
    rbc_copy.wait()
    for q in range(4):
        hand_out(0, q).wait()
        hand_out(1, q).wait()


def chain(saved, act, cot, wxz, wbc, wout, convx, convbc, dtb, alog, dskip, gain):
    table = scratch_table()
    vm = pl.BlockSpec(memory_space=pltpu.VMEM)
    hbm = pl.BlockSpec(memory_space=pl.ANY)
    shape = jax.ShapeDtypeStruct
    return pl.pallas_call(
        functools.partial(chain_kernel, tuple(table)),
        out_shape=(
            shape((4, 4, SEQ, 512), BF16),
            shape((4, 4, 256, SEQ), BF16),
            shape((512, SEQ), BF16),
            shape((SEQ, 384), BF16),
            shape((SEQ, 512), BF16),
            shape((SEQ, 512), BF16),
        ),
        in_specs=[pl.BlockSpec(memory_space=pltpu.HBM)] * 6 + [vm] * 6,
        out_specs=(hbm,) * 6,
        scratch_shapes=list(table.values()),
        compiler_params=pltpu.CompilerParams(
            collective_id=0, has_side_effects=True, vmem_limit_bytes=36 * 1024 * 1024
        ),
        cost_estimate=pl.CostEstimate(
            flops=4_300_000_000, bytes_accessed=18_000_000, transcendentals=2_000_000
        ),
        name="chain",
    )(*(
        pltpu.with_memory_space_constraint(x, pltpu.HBM)
        for x in (saved, act, cot, wxz, wbc, wout, convx, convbc, dtb, alog, dskip, gain)
    ))


def grads_kernel(
    round_ref, mixed_ref, normed_ref, rbc_ref, cot_ref, prev_ref, next_ref,
    xz_o, out_o, bc_o, prev_o, next_o,
    xz_s, out_s, bc_s, s_xz, s_out, s_rest,
):
    small = [
        pltpu.make_async_copy(src, dst, s_rest.at[i])
        for i, (src, dst) in enumerate(((prev_ref, prev_o), (next_ref, next_o), (bc_s, bc_o)))
    ]
    small[0].start()
    small[1].start()

    def xz_copy(i):
        cols = pl.ds(pl.multiple_of(i * 512, 512), 512)
        return pltpu.make_async_copy(xz_s.at[i], xz_o.at[:, cols], s_xz.at[i])

    def out_copy(i):
        rows = pl.ds(pl.multiple_of(i * 256, 256), 256)
        return pltpu.make_async_copy(out_s.at[i], out_o.at[rows], s_out.at[i])

    def step(i, carry):
        out_s[i] = dot1(mixed_ref[i], cot_ref[...], NN)
        out_copy(i).start()
        xz_s[i] = dot1(normed_ref[...], round_ref[i], NN)
        xz_copy(i).start()
        return carry

    lax.fori_loop(0, 16, step, 0)
    bc_s[...] = dot1(rbc_ref[:, :320], normed_ref[...], (((0,), (1,)), ((), ())))
    small[2].start()

    def finish(i, carry):
        out_copy(i).wait()
        xz_copy(i).wait()
        return carry

    lax.fori_loop(0, 16, finish, 0)
    for copy in small:
        copy.wait()


def grads(round_all, mixed_all, normed, rbc, cot, prev_grad, next_act):
    shape = jax.ShapeDtypeStruct
    vm = pl.BlockSpec(memory_space=pltpu.VMEM)
    hbm = pl.BlockSpec(memory_space=pl.ANY)
    dma = pltpu.SemaphoreType.DMA
    return pl.pallas_call(
        grads_kernel,
        out_shape=(
            shape((512, 8192), F32),
            shape((4096, 512), F32),
            shape((320, 512), F32),
            shape((SEQ, 512), BF16),
            shape((SEQ, 512), BF16),
        ),
        in_specs=[vm] * 5 + [hbm] * 2,
        out_specs=(hbm,) * 5,
        scratch_shapes=[
            pltpu.VMEM((16, 512, 512), F32),
            pltpu.VMEM((16, 256, 512), F32),
            pltpu.VMEM((320, 512), F32),
            dma((16,)),
            dma((16,)),
            dma((3,)),
        ],
        compiler_params=pltpu.CompilerParams(vmem_limit_bytes=34 * 1024 * 1024),
        cost_estimate=pl.CostEstimate(
            flops=1_700_000_000, bytes_accessed=29_000_000, transcendentals=0
        ),
        name="grads",
    )(
        round_all.reshape(16, SEQ, 512),
        mixed_all.reshape(16, 256, SEQ),
        normed,
        rbc,
        cot,
        prev_grad,
        next_act,
    )


def per_device_four(
    act_in,
    saved_act,
    cotangent,
    weight_xz,
    weight_bcdt,
    weight_out,
    conv_x,
    conv_bc,
    dt_bias,
    a_log,
    d_skip,
    norm_gain,
):
    round_all, mixed_all, normed, rbc, prev_grad, next_act = chain(
        saved_act[0],
        act_in[0],
        cotangent[0],
        weight_xz[0],
        weight_bcdt[0],
        weight_out[0],
        conv_x[0],
        conv_bc[0],
        dt_bias,
        a_log,
        d_skip,
        norm_gain,
    )
    grad_xz, grad_out, grad_bcdt, prev_grad, next_act = grads(
        round_all, mixed_all, normed, rbc, cotangent[0], prev_grad, next_act
    )
    return (next_act[None], prev_grad[None], grad_xz[None], grad_bcdt[None], grad_out[None])


def solution(mesh):
    return jax.shard_map(
        per_device_four if mesh.shape["dp"] == 4 and mesh.shape["section"] > 1 else per_device,
        mesh=mesh,
        in_specs=(
            P("section", None, "dp"),
            P("section", None, "dp"),
            P("section", None, "dp"),
            P("section", "dp", None),
            P("section", None, "dp"),
            P("section", None, "dp"),
            P("section", None, "dp"),
            P("section", None, None),
            P("section", "dp"),
            P("section", "dp"),
            P("section", "dp"),
            P("section", "dp"),
        ),
        out_specs=(
            P("section", None, "dp"),
            P("section", None, "dp"),
            P("section", "dp", None),
            P("section", None, "dp"),
            P("section", None, "dp"),
        ),
        check_vma=False,
    )
```

```python
import functools

import jax
import jax.numpy as jnp
from jax import lax
from jax.experimental import pallas as pl
from jax.experimental.pallas import tpu as pltpu
from jax.sharding import PartitionSpec as P

D = 2048
HEAD_DIM = 64
NSTATE = 128
HEADS = 64
SEQ = 128
INNER = 4096
KCONV = 4
MAPS = 2 * NSTATE


def from_behind(x, axis, by):
    length = lax.axis_size(axis)
    return lax.ppermute(x, axis, [(i, (i + by) % length) for i in range(length)])


def swap(x, mask):
    length = lax.axis_size("dp")
    return lax.ppermute(x, "dp", [(i, i ^ mask) for i in range(length)])


def masks():
    length = lax.axis_size("dp")
    out = []
    bit = 1
    while bit < length:
        out.append(bit)
        bit *= 2
    return out


def sum_all(x):
    for bit in masks():
        x = x + swap(x, bit)
    return x


def tied(x, other):
    return lax.optimization_barrier((x, other))[0]


def sum_first(part):
    length = lax.axis_size("dp")
    came = {j - 1: swap(part(j).astype(jnp.bfloat16), 1) for j in range(1, length, 2)}
    return {j: part(j) + came[j].astype(jnp.float32) for j in sorted(came, reverse=True)}


def sum_rest(held, after=None):
    first = begun = None
    for bit in masks()[1:]:
        sent = {j: held[j].astype(jnp.bfloat16) for j in held if j & bit}
        if after is not None and first is None:
            sent = {j: tied(x, after) for j, x in sent.items()}
        came = {j ^ bit: swap(x, bit) for j, x in sent.items()}
        if first is None:
            first = came[0]
            begun = sent[bit]
        held = {j: held[j] + came[j].astype(jnp.float32) for j in came}
    return held[0], first, begun


def sum_both(x, after):
    me = lax.axis_index("dp")
    odd = (me & 1) != 0
    x = x + swap(x, 1)
    mine = tied(jnp.where(odd, x[SEQ:], x[:SEQ]), after)
    for bit in masks()[1:]:
        mine = mine + swap(mine, bit)
    other = swap(mine, 1)
    return jnp.where(odd, other, mine), jnp.where(odd, mine, other)


def gather_cols(block, after=None):
    me = lax.axis_index("dp")
    length = lax.axis_size("dp")
    if after is not None:
        block = tied(block, after)
    held = [block]
    order = [0]
    for bit in reversed(masks()):
        held = held + [swap(b, bit) for b in held]
        order = order + [j ^ bit for j in order]
    by_mask = {j: b for j, b in zip(order, held)}
    level = [by_mask[j] for j in range(length)]
    for bit in masks():
        flip = (me & bit) != 0
        level = [jnp.where(flip, level[j ^ bit], level[j]) for j in range(length)]
    return jnp.concatenate(level, axis=1), held[-1]


def causal_conv(values, kernel_taps):
    kernel = kernel_taps.shape[0]
    length = values.shape[0]
    padded = jnp.pad(values, ((kernel - 1, 0), (0, 0)))
    running = jnp.zeros_like(values)
    for offset in range(kernel):
        running = running + kernel_taps[offset] * padded[offset : offset + length]
    return running


def mixer(proj_x, proj_z, proj_dt, scores, conv_taps, dt_offset, log_rate, skip_gain):
    length, width = proj_x.shape
    nheads = dt_offset.shape[0]
    head_width = width // nheads
    xconv = jax.nn.silu(causal_conv(proj_x, conv_taps))
    steps = jax.nn.softplus(proj_dt + dt_offset)
    position = jnp.arange(length)
    causal = position[:, None] >= position[None, :]
    cumul = jnp.dot(
        causal.astype(jnp.float32), steps * -jnp.exp(log_rate), precision=lax.Precision.HIGHEST
    )
    heads_cum = cumul.T
    spread = heads_cum[:, :, None] - heads_cum[:, None, :]
    decay = jnp.where(causal[None], jnp.exp(jnp.where(causal[None], spread, 0.0)), 0.0)
    weights = decay * scores[None] * steps.T[:, None, :]
    heads_in = xconv.reshape(length, nheads, head_width)
    result = jnp.einsum("hts,shp->thp", weights, heads_in, precision=lax.Precision.HIGH)
    result = result + skip_gain[None, :, None] * heads_in
    gate_in = jax.nn.silu(proj_z.reshape(length, nheads, head_width))
    return (result * gate_in).reshape(length, width)


def times_transposed(left, right):
    return lax.dot_general(
        left, right, (((1,), (1,)), ((), ())), preferred_element_type=jnp.float32
    )


def transposed_times(left, right):
    return lax.dot_general(
        left, right, (((0,), (0,)), ((), ())), preferred_element_type=jnp.float32
    )


def per_device(
    act_in,
    saved_act,
    cotangent,
    weight_xz,
    weight_bcdt,
    weight_out,
    conv_x,
    conv_bc,
    dt_bias,
    a_log,
    d_skip,
    norm_gain,
):
    input_rows = act_in[0]
    saved_rows = saved_act[0]
    cot_rows = cotangent[0]
    local_xz = weight_xz[0]
    local_bcdt = weight_bcdt[0]
    local_out = weight_out[0]
    taps_x = conv_x[0]
    taps_bc = conv_bc[0]
    dt_offset = dt_bias[0]
    log_rate = a_log[0]
    skip_gain = d_skip[0]
    gain_local = norm_gain[0]
    own_heads = dt_offset.shape[0]
    me = lax.axis_index("dp")
    head_first = me * own_heads
    width = own_heads * HEAD_DIM

    def whole_act(pre_part):
        return jax.nn.silu(causal_conv(pre_part, taps_bc))

    both = jnp.concatenate([saved_rows, input_rows], axis=0)
    both_values = both.astype(jnp.float32)
    squares = jnp.sum(both_values * both_values, axis=1, keepdims=True)
    def xz_part(j):
        cols = lax.dynamic_slice_in_dim(local_xz, (me ^ j) * 2 * width, 2 * width, 1)
        return jnp.dot(both, cols, preferred_element_type=jnp.float32)

    held_xz = sum_first(xz_part)
    back_raw, back_first, back_begun = sum_rest({j: x[:SEQ] for j, x in held_xz.items()})
    back_small, forward_small = sum_both(
        jnp.concatenate([times_transposed(both, local_bcdt), squares], axis=1), back_begun
    )

    def mixed_part(j):
        taken = lax.dynamic_slice_in_dim(local_out, (me ^ j) * width, width, 0)
        return times_transposed(cot_rows, taken)

    d_mixed = sum_rest(sum_first(mixed_part), back_begun)[0]
    forward_raw = sum_rest({j: x[SEQ:] for j, x in held_xz.items()}, back_first)[0]

    def project(rows, small, raw_xz):
        raw_cols = small[:, : MAPS + HEADS]
        scales = lax.rsqrt(small[:, MAPS + HEADS :] / D + 1e-05)
        return (rows.astype(jnp.float32), scales, raw_xz, raw_cols)

    back_proj = project(saved_rows, back_small, back_raw)
    forward_proj = project(input_rows, forward_small, forward_raw)

    def gate_parts(projected):
        values, scales, raw_xz, raw_cols = projected
        own_xz = raw_xz * scales
        whole_cols = raw_cols * scales
        pre_part = whole_cols[:, :MAPS]
        maps = whole_act(pre_part).astype(jnp.bfloat16)
        own_dt = lax.dynamic_slice_in_dim(whole_cols[:, MAPS:], head_first, own_heads, 1)
        split_xz = own_xz.reshape(SEQ, own_heads, 2, HEAD_DIM)
        mix_x = split_xz[:, :, 0].reshape(SEQ, width)
        mix_z = split_xz[:, :, 1].reshape(SEQ, width)
        scores = times_transposed(maps[:, NSTATE:], maps[:, :NSTATE])

        def local_mix(in_x, in_z, in_dt, in_scores):
            return mixer(in_x, in_z, in_dt, in_scores, taps_x, dt_offset, log_rate, skip_gain)

        gated, mix_back = jax.vjp(local_mix, mix_x, mix_z, own_dt, scores)
        return (gated, mix_back, maps, pre_part)

    values, scales, raw_xz, raw_cols = back_proj
    gated, mix_back, maps, pre_part = gate_parts(back_proj)
    gained = gated * gain_local
    row_sums = sum_all(
        jnp.stack([jnp.sum(gated * gated, axis=1), jnp.sum(d_mixed * gained, axis=1)])
    )
    inverse = lax.rsqrt(row_sums[0] / INNER + 1e-05)[:, None]
    dots = row_sums[1][:, None]
    mixed_in = (gained * inverse).astype(jnp.bfloat16)
    d_gated = inverse * gain_local * d_mixed - gated * (inverse * inverse * inverse) * dots / INNER
    d_px, d_pz, d_pdt, d_scores = mix_back(d_gated)
    own_round = (
        jnp.stack(
            [
                d_px.reshape(SEQ, own_heads, HEAD_DIM),
                d_pz.reshape(SEQ, own_heads, HEAD_DIM),
            ],
            axis=2,
        )
        .reshape(SEQ, own_heads * 2 * HEAD_DIM)
        .astype(jnp.bfloat16)
    )
    round_xz, round_last = gather_cols(own_round)
    inner_own = jnp.sum(own_round.astype(jnp.float32) * raw_xz, axis=1, keepdims=True)
    wide_maps = maps.astype(jnp.float32)
    d_maps = jnp.concatenate(
        [
            jnp.dot(d_scores.T, wide_maps[:, NSTATE:], precision=lax.Precision.HIGH),
            jnp.dot(d_scores, wide_maps[:, :NSTATE], precision=lax.Precision.HIGH),
        ],
        axis=1,
    )
    d_dt_full = lax.dynamic_update_slice_in_dim(
        jnp.zeros((SEQ, HEADS), jnp.float32), d_pdt, head_first, 1
    )
    summed = sum_all(jnp.concatenate([d_maps, d_dt_full, inner_own], axis=1))
    conv_out, conv_back = jax.vjp(whole_act, pre_part)
    d_pre = conv_back(summed[:, :MAPS])[0]
    round_bcdt = jnp.concatenate([d_pre, summed[:, MAPS : MAPS + HEADS]], axis=1).astype(
        jnp.bfloat16
    )
    inner_sum = summed[:, MAPS + HEADS :] + jnp.sum(
        round_bcdt.astype(jnp.float32) * raw_cols, axis=1, keepdims=True
    )

    fwd_gated = gate_parts(forward_proj)[0]
    fwd_all, _ = gather_cols((fwd_gated * gain_local).astype(jnp.bfloat16), round_last)
    fwd_sum = sum_all(jnp.sum(fwd_gated * fwd_gated, axis=1)[None])
    fwd_inverse = lax.rsqrt(fwd_sum[0] / INNER + 1e-05)[:, None]
    mixed = jnp.dot(fwd_all, local_out, preferred_element_type=jnp.float32) * fwd_inverse
    section_out = (input_rows.astype(jnp.float32) + mixed).astype(jnp.bfloat16)
    next_act = from_behind(section_out, "section", 1)

    normed = (values * scales).astype(jnp.bfloat16)
    d_normed = times_transposed(round_xz, local_xz)
    d_normed = d_normed + jnp.dot(round_bcdt, local_bcdt, preferred_element_type=jnp.float32)
    d_norm_in = scales * d_normed - values * (scales * scales * scales) * inner_sum / D
    d_input = (cot_rows.astype(jnp.float32) + d_norm_in).astype(jnp.bfloat16)
    prev_grad = from_behind(d_input, "section", -1)

    grad_out = transposed_times(gather_cols(mixed_in, round_last)[0], cot_rows)
    grad_xz = transposed_times(normed, round_xz)
    grad_bcdt = transposed_times(round_bcdt, normed)
    return (next_act[None], prev_grad[None], grad_xz[None], grad_bcdt[None], grad_out[None])


BF16 = jnp.bfloat16
F32 = jnp.float32
MESH_ID = pl.DeviceIdType.MESH
NN = (((1,), (0,)), ((), ()))
NT = (((1,), (1,)), ((), ()))
TN = (((0,), (0,)), ((), ()))


def dot1(a, b, dims):
    return lax.dot_general(a, b, dims, preferred_element_type=F32)


def dot_full(a, b, dims):
    return lax.dot_general(
        a, b, dims, precision=lax.Precision.HIGHEST, preferred_element_type=F32
    )


def halves(x):
    high = x.astype(BF16)
    return high, (x - high.astype(F32)).astype(BF16)


def dot3(a, b, dims):
    a_high, a_low = halves(a)
    b_high, b_low = halves(b)
    return dot1(a_high, b_high, dims) + (dot1(a_high, b_low, dims) + dot1(a_low, b_high, dims))


def sigmoid(x):
    return 1.0 / (1.0 + jnp.exp(-x))


def d_silu(x, s):
    return s * (1.0 + x * (1.0 - s))


def rows_of(shape):
    return lax.broadcasted_iota(jnp.int32, shape, 0)


def lanes_of(shape):
    return lax.broadcasted_iota(jnp.int32, shape, 1)


def conv_rows(v, taps):
    row = rows_of(v.shape)
    out = taps[KCONV - 1 : KCONV] * v
    for s in range(1, KCONV):
        moved = jnp.where(row >= s, pltpu.roll(v, s, 0), 0.0)
        out = out + taps[KCONV - 1 - s : KCONV - s] * moved
    return out


def conv_rows_back(d, taps):
    row = rows_of(d.shape)
    out = taps[KCONV - 1 : KCONV] * d
    for s in range(1, KCONV):
        moved = jnp.where(row < SEQ - s, pltpu.roll(d, SEQ - s, 0), 0.0)
        out = out + taps[KCONV - 1 - s : KCONV - s] * moved
    return out


def as_column(row):
    return jnp.broadcast_to(row, (SEQ, SEQ)).T


def row_sums(values):
    return dot_full(jnp.ones((8, values.shape[1]), F32), values, NT)


def wide(col, n):
    return jnp.concatenate([col] * n, axis=1)


def scratch_table():
    dma = pltpu.SemaphoreType.DMA
    vm = pltpu.VMEM
    table = dict(
        w=vm((16, 512, 512), BF16),
        wo=vm((16, 256, 512), BF16),
        wbc=vm((384, 512), BF16),
        x2=vm((2, SEQ, 512), BF16),
        cot=vm((SEQ, 512), BF16),
        sec=vm((2, SEQ, 512), BF16),
        normed=vm((512, SEQ), BF16),
        xzd_s=vm((2, 2, 4, SEQ, 512), BF16),
        xzd_r=vm((2, 2, 4, SEQ, 512), BF16),
        xzy_s=vm((2, 4, SEQ, 512), BF16),
        xzy_r=vm((2, 4, SEQ, 512), BF16),
        md_s=vm((2, 4, SEQ, 256), BF16),
        md_r=vm((2, 4, SEQ, 256), BF16),
        my_s=vm((4, SEQ, 256), BF16),
        my_r=vm((4, SEQ, 256), BF16),
        smd_s=vm((SEQ, 384), F32),
        smd_r=vm((SEQ, 384), F32),
        smy_s=vm((SEQ, 384), BF16),
        smy_r=vm((SEQ, 384), BF16),
        sm=vm((2, SEQ, 384), F32),
        sq=vm((4, 8, SEQ), F32),
        rs=vm((4, 8, SEQ), F32),
        rf=vm((4, 8, SEQ), F32),
        tg=vm((4, 24, SEQ), F32),
        dsd_s=vm((64, SEQ), F32),
        dsd_r=vm((64, SEQ), F32),
        dsy_s=vm((64, SEQ), F32),
        dsy_r=vm((64, SEQ), F32),
        ds_tot=vm((2, 64, SEQ), F32),
        ds_acc=vm((2, 64, SEQ), F32),
        ga_round=vm((4, 4, SEQ, 512), BF16),
        ga_mix=vm((4, 4, 256, SEQ), BF16),
        ga_fwd=vm((4, 4, SEQ, 256), BF16),
        big_l=vm((16, SEQ, SEQ), F32),
        xc=vm((8, SEQ, SEQ), F32),
        ys=vm((8, SEQ, SEQ), F32),
        gz=vm((8, SEQ, SEQ), F32),
        dcv=vm((8, SEQ, SEQ), F32),
        dzs=vm((8, SEQ, SEQ), F32),
        dm=vm((8, SEQ, SEQ), F32),
        raw=vm((4, SEQ, 512), F32),
        acc0=vm((SEQ, SEQ), F32),
        acc1=vm((SEQ, SEQ), F32),
        dn=vm((SEQ, 512), F32),
        pdt=vm((SEQ, SEQ), F32),
        dtT=vm((2, 16, SEQ), F32),
        cumT=vm((2, 16, SEQ), F32),
        sgT=vm((16, SEQ), F32),
        negA=vm((16, SEQ), F32),
        dirT=vm((16, SEQ), F32),
        rowT=vm((16, SEQ), F32),
        scores=vm((2, SEQ, SEQ), F32),
        maps=vm((SEQ, 256), BF16),
        dcm=vm((SEQ, 256), F32),
        scale=vm((2, SEQ, SEQ), F32),
        cx=vm((8, KCONV, SEQ), F32),
        gain=vm((8, 1, SEQ), F32),
        dsk=vm((8, 1, SEQ), F32),
        rbc=vm((SEQ, 384), BF16),
        s_w=dma((16,)),
        s_wo=dma((16,)),
        s_in=dma((4,)),
        s_out=dma((10,)),
    )
    for name, shape in dict(
        xzd=(2, 2, 4), xzy=(2, 4), md=(2, 4), my=(4,), smd=(1,), smy=(1,), smt=(1,), sq=(3,), rs=(3,),
        rf=(3,), tg=(3,), dsd=(1,), dsy=(1,), dst=(1,), ry=(4,), rd=(4,), rw=(4,), my2=(4,), md2=(4,),
        mw=(4,), fy=(4,), fd=(4,), fw=(4,), sec=(2,),
    ).items():
        table["a_" + name] = dma(shape)
        table["b_" + name] = dma(shape)
    return table


class Names:
    pass


def chain_kernel(names, *refs):
    (saved_h, act_h, cot_h, wxz_h, wbc_h, wout_h, convx, convbc, dtb, alog, dskip, gain_in,
     round_o, mixed_o, normed_o, rbc_o, prev_o, next_o) = refs[:18]
    v = Names()
    for name, ref in zip(names, refs[18:]):
        setattr(v, name, ref)
    saved, act, cot = v.x2.at[0], v.x2.at[1], v.cot

    me = lax.axis_index("dp")
    core = lax.rem(me, 2)
    mate = me + 1 - 2 * core
    ypeer = me + 2 - 4 * (me // 2)
    diag = 3 - me
    peers = (mate, ypeer, diag)
    sections = lax.axis_size("section")
    place = lax.axis_index("section")
    ahead = lax.rem(place + 1, sections)
    behind = lax.rem(place + sections - 1, sections)

    def remote(src, dst, kind, index, dev):
        return pltpu.make_async_remote_copy(
            src_ref=src,
            dst_ref=dst,
            send_sem=getattr(v, "a_" + kind).at[index],
            recv_sem=getattr(v, "b_" + kind).at[index],
            device_id={"dp": dev},
            device_id_type=MESH_ID,
        )

    def xzd(mb, role, j):
        return remote(v.xzd_s.at[mb, role, j], v.xzd_r.at[mb, role, j], "xzd", (mb, role, j), mate)

    def xzy(mb, j):
        return remote(v.xzy_s.at[mb, j], v.xzy_r.at[mb, j], "xzy", (mb, j), ypeer)

    def md(role, j):
        return remote(v.md_s.at[role, j], v.md_r.at[role, j], "md", (role, j), mate)

    def my(j):
        return remote(v.my_s.at[j], v.my_r.at[j], "my", (j,), ypeer)

    def smd():
        return remote(v.smd_s, v.smd_r, "smd", (0,), mate)

    def smy():
        return remote(v.smy_s, v.smy_r, "smy", (0,), ypeer)

    def smt(mb):
        return remote(v.sm.at[mb], v.sm.at[mb], "smt", (0,), mate)

    def spread(buf, kind, i, slot):
        return remote(buf.at[slot], buf.at[slot], kind, (i,), peers[i])

    def spread_start(buf, kind):
        for i in range(3):
            spread(buf, kind, i, me).start()

    def spread_wait(buf, kind):
        for i in range(3):
            spread(buf, kind, i, peers[i]).wait_recv()

    def dsd():
        return remote(v.dsd_s, v.dsd_r, "dsd", (0,), mate)

    def dsy():
        return remote(v.dsy_s, v.dsy_r, "dsy", (0,), ypeer)

    def dst(half):
        return remote(v.ds_tot.at[half], v.ds_tot.at[half], "dst", (0,), mate)

    def gather(buf, kind, q, j, dev):
        return remote(buf.at[q, j], buf.at[q, j], kind, (j,), dev)

    def send_section(i):
        return pltpu.make_async_remote_copy(
            src_ref=v.sec.at[i],
            dst_ref=(prev_o, next_o)[i],
            send_sem=v.a_sec.at[i],
            recv_sem=v.b_sec.at[i],
            device_id={"section": (behind, ahead)[i]},
            device_id_type=MESH_ID,
        )

    def hand_out(kind, q):
        buf, out = ((v.ga_round, round_o), (v.ga_mix, mixed_o))[kind]
        return pltpu.make_async_copy(buf.at[q], out.at[q], v.s_out.at[4 * kind + q])

    def load_w(i):
        cols = pl.ds(pl.multiple_of(i * 512, 512), 512)
        return pltpu.make_async_copy(wxz_h.at[:, cols], v.w.at[i], v.s_w.at[i])

    def load_wo(i):
        return pltpu.make_async_copy(
            wout_h.at[pl.ds(pl.multiple_of(i * 256, 256), 256)], v.wo.at[i], v.s_wo.at[i]
        )

    def loop(fn, n=4):
        def step(j, carry):
            fn(j)
            return carry
        lax.fori_loop(0, n, step, 0)

    def follow(j, begin):
        @pl.when(j >= 1)
        def _():
            begin(j - 1)

        @pl.when(j == 3)
        def _():
            begin(3)

    barrier = pltpu.get_barrier_semaphore()
    for peer in peers:
        pl.semaphore_signal(barrier, 1, device_id={"dp": peer}, device_id_type=MESH_ID)
    for other in (ahead, behind):
        pl.semaphore_signal(barrier, 1, device_id={"section": other}, device_id_type=MESH_ID)

    loads = [
        pltpu.make_async_copy(src, dst, v.s_in.at[i])
        for i, (src, dst) in enumerate(
            ((saved_h, saved), (act_h, act), (wbc_h, v.wbc.at[0:320]), (cot_h, v.cot))
        )
    ]
    loads[0].start()
    load_w(4 * diag).start()
    load_w(4 * ypeer).start()
    load_w(4 * diag + 1).start()
    for load in loads[1:]:
        load.start()
    load_w(4 * ypeer + 1).start()
    load_w(4 * diag + 2).start()

    def xz_first(j, ready=None):
        load_w(4 * diag + j).wait()
        v.xzd_s[0, 0, j] = dot1(saved[...], v.w[4 * diag + j], NN).astype(BF16)
        if ready is not None:
            ready()
        xzd(0, 0, j).start()

    def xz_sum(mb, x_ref):
        def fn(j):
            part = dot1(x_ref[...], v.w[4 * ypeer + j], NN)
            xzd(mb, 0, j).wait_recv()
            v.xzy_s[mb, j] = (part + v.xzd_r[mb, 0, j].astype(F32)).astype(BF16)
        return fn

    def xz_back(j):
        load_w(4 * ypeer + j).wait()
        xz_sum(0, saved)(j)
        xzy(0, j).start()

    v.wbc[320:] = jnp.zeros((64, 512), BF16)
    loads[0].wait()
    xz_first(0, lambda: pl.semaphore_wait(barrier, 5))
    load_w(4 * ypeer + 2).start()
    load_w(4 * diag + 3).start()
    load_w(4 * ypeer + 3).start()
    xz_first(1)
    xz_back(0)
    for q in (diag, ypeer):
        loop(lambda j: load_wo(4 * q + j).start())
    for q in (mate, me):
        loop(lambda j: load_w(4 * q + j).start())
    for q in (mate, me):
        loop(lambda j: load_wo(4 * q + j).start())
    loads[1].wait()
    loads[2].wait()
    v.smd_s[...] = dot1(v.x2[1 - core], v.wbc[...], NT)
    smd().start()
    xz_first(2)
    xz_back(1)
    xz_first(3)
    own_small = dot1(v.x2[core], v.wbc[...], NT)
    smd().wait_recv()
    own_small = own_small + v.smd_r[...]
    v.smy_s[...] = own_small.astype(BF16)
    smy().start()
    v.sm[core] = own_small
    xz_back(2)
    squares = []
    for x_ref in (saved, act):
        wide_x = x_ref[...].astype(F32)
        squares.append(row_sums(wide_x * wide_x))
    v.sq[me] = jnp.where(rows_of((8, SEQ)) == 0, squares[0], squares[1])
    spread_start(v.sq, "sq")
    xz_back(3)
    loads[3].wait()

    def m_first(j):
        load_wo(4 * diag + j).wait()
        v.md_s[0, j] = dot1(cot[...], v.wo[4 * diag + j], NT).astype(BF16)
        md(0, j).start()

    loop(m_first)

    def m_sum(j):
        load_wo(4 * ypeer + j).wait()
        part = dot1(cot[...], v.wo[4 * ypeer + j], NT)
        md(0, j).wait_recv()
        v.my_s[j] = (part + v.md_r[0, j].astype(F32)).astype(BF16)

    loop(m_sum)

    def xz_mate(j):
        load_w(4 * mate + j).wait()
        v.xzd_s[0, 1, j] = dot1(saved[...], v.w[4 * mate + j], NN).astype(BF16)
        xzd(0, 1, j).start()

    loop(xz_mate)

    def m_mate(j):
        load_wo(4 * mate + j).wait()
        v.md_s[1, j] = dot1(cot[...], v.wo[4 * mate + j], NT).astype(BF16)
        md(1, j).start()

    loop(m_mate)

    def fwd_first(j):
        v.xzd_s[1, 0, j] = dot1(act[...], v.w[4 * diag + j], NN).astype(BF16)
        xzd(1, 0, j).start()

    loop(fwd_first)

    smy().wait_recv()
    v.sm[core] = v.sm[core] + v.smy_r[...].astype(F32)
    smt(core).start()

    expand = (lanes_of((16, 1024)) // HEAD_DIM == rows_of((16, 1024))).astype(F32)
    skip_wide = dot_full(dskip[...], expand, NN)
    for p in range(8):
        cols = slice(128 * p, 128 * p + 128)
        v.cx[p] = convx[:, cols]
        v.gain[p] = gain_in[:, cols]
        v.dsk[p] = skip_wide[:, cols]
    bias_col = jnp.broadcast_to(dtb[...], (SEQ, 16)).T
    v.negA[...] = -jnp.exp(jnp.broadcast_to(alog[...], (SEQ, 16)).T)
    row_id = rows_of((SEQ, SEQ))
    lane_id = lanes_of((SEQ, SEQ))
    causal = row_id >= lane_id
    low = lane_id < HEAD_DIM

    spread_wait(v.sq, "sq")
    total_sq = v.sq[0] + v.sq[1] + v.sq[2] + v.sq[3]
    for mb in range(2):
        v.scale[mb] = lax.rsqrt(as_column(total_sq[mb : mb + 1]) / D + 1e-05)

    smt(1 - core).wait_recv()

    def prepare(mb):
        scale = v.scale[mb]
        small = v.sm[mb] * wide(scale, 3)
        conv = conv_rows(small[:, :MAPS], convbc[...])
        sig = sigmoid(conv)
        maps = (conv * sig).astype(BF16)
        v.scores[mb] = dot1(maps[:, NSTATE:], maps[:, :NSTATE], NT)
        if mb == 0:
            v.maps[...] = maps
            v.dcm[...] = d_silu(conv, sig)
        v.pdt[...] = small[:, MAPS:].T
        logits = v.pdt[pl.ds(pl.multiple_of(16 * me, 16), 16)] + bias_col
        steps = jnp.maximum(logits, 0.0) + jnp.log1p(jnp.exp(-jnp.abs(logits)))
        if mb == 0:
            v.sgT[...] = sigmoid(logits)
        v.dtT[mb] = steps
        v.cumT[mb] = dot_full(
            steps * v.negA[...], (row_id <= lane_id).astype(F32), NN
        )

    prepare(0)

    def split_pair(first, second):
        head_x = jnp.where(low, first, pltpu.roll(second, 64, 1))
        head_z = jnp.where(low, pltpu.roll(first, 64, 1), second)
        return head_x, head_z

    def mix(mb, pair, block, save):
        scale = v.scale[mb]
        x, z = split_pair(block[:, :128] * scale, block[:, 128:] * scale)
        conv = conv_rows(x, v.cx[pair])
        sig = sigmoid(conv)
        xc = conv * sig
        sig_z = sigmoid(z)
        gate = z * sig_z
        weights = []
        for k in range(2):
            head = pl.ds(2 * pair + k, 1)
            row = v.cumT[mb, head]
            decay = jnp.exp(jnp.where(causal, as_column(row) - row, -1e30))
            if save:
                v.big_l[2 * pair + k] = decay
            weights.append(decay * v.scores[mb] * v.dtT[mb, head])
        stacked = jnp.concatenate([jnp.where(low, xc, 0.0), jnp.where(low, 0.0, xc)], axis=0)
        y = dot3(jnp.concatenate(weights, axis=1), stacked, NN)
        if save:
            v.xc[pair] = xc
            v.ys[pair] = y
            v.gz[pair] = gate
            v.dcv[pair] = d_silu(conv, sig)
            v.dzs[pair] = d_silu(z, sig_z)
        return (y + v.dsk[pair] * xc) * gate

    def raw_block(mb, x_ref, j):
        return (
            dot1(x_ref[...], v.w[4 * me + j], NN)
            + v.xzd_r[mb, 1, j].astype(F32)
            + v.xzy_r[mb, j].astype(F32)
        )

    v.acc0[...] = jnp.zeros((SEQ, SEQ), F32)

    def stage_a(j):
        load_w(4 * me + j).wait()
        xzd(0, 1, j).wait_recv()
        xzy(0, j).wait_recv()
        follow(j, lambda i: my(i).start())
        raw = raw_block(0, saved, j)
        v.raw[j] = raw
        for k in range(2):
            gated = mix(0, 2 * j + k, raw[:, 256 * k : 256 * k + 256], True)
            v.acc0[...] += gated * gated

    loop(stage_a)

    def fwd_mate(j):
        v.xzd_s[1, 1, j] = dot1(act[...], v.w[4 * mate + j], NN).astype(BF16)
        xzd(1, 1, j).start()

    loop(xz_sum(1, act))
    loop(fwd_mate)

    v.acc1[...] = jnp.zeros((SEQ, SEQ), F32)

    def stage_b(j):
        load_wo(4 * me + j).wait()
        md(1, j).wait_recv()
        my(j).wait_recv()

        @pl.when(j == 2)
        def _():
            xzy(1, 0).start()

        d_mixed = (
            dot1(cot[...], v.wo[4 * me + j], NT)
            + v.md_r[1, j].astype(F32)
            + v.my_r[j].astype(F32)
        )
        for k in range(2):
            pair = 2 * j + k
            part = d_mixed[:, 128 * k : 128 * k + 128]
            v.dm[pair] = part
            gated = (v.ys[pair] + v.dsk[pair] * v.xc[pair]) * v.gz[pair]
            v.acc1[...] += part * v.gain[pair] * gated

    loop(stage_b)

    v.rs[me] = jnp.where(
        rows_of((8, SEQ)) == 0, row_sums(v.acc0[...]), row_sums(v.acc1[...])
    )
    spread_start(v.rs, "rs")
    loop(lambda j: xzy(1, j + 1).start(), 3)
    prepare(1)
    for k in range(4):
        cols = slice(128 * k, 128 * k + 128)
        normed = (saved[:, cols].astype(F32) * v.scale[0]).astype(BF16)
        v.normed[cols] = normed.astype(F32).T.astype(BF16)
    normed_copy = pltpu.make_async_copy(v.normed, normed_o, v.s_out.at[8])
    normed_copy.start()
    spread_wait(v.rs, "rs")
    total_rs = v.rs[0] + v.rs[1] + v.rs[2] + v.rs[3]
    v.acc0[...] = lax.rsqrt(as_column(total_rs[0:1]) / INNER + 1e-05)
    v.acc1[...] = as_column(total_rs[1:2]) / INNER

    v.pdt[...] = jnp.zeros((SEQ, SEQ), F32)
    v.ds_acc[...] = jnp.zeros((2, 64, SEQ), F32)
    head_rows = (
        lanes_of((8, SEQ)) // HEAD_DIM == rows_of((8, SEQ))
    ).astype(F32)

    def stage_c(j):
        inverse = v.acc0[...]
        lower = inverse * inverse * inverse * v.acc1[...]
        for k in range(2):
            pair = 2 * j + k
            xc = v.xc[pair]
            y = v.ys[pair]
            gate = v.gz[pair]
            skip = v.dsk[pair]
            gained = inverse * v.gain[pair]
            y_full = y + skip * xc
            gated = y_full * gate
            v.ga_mix[me, j, 128 * k : 128 * k + 128] = (gated * gained).T.astype(BF16)
            d_gated = gained * v.dm[pair] - gated * lower
            d_y = d_gated * gate
            d_gate = d_gated * y_full
            d_ys = jnp.concatenate([jnp.where(low, d_y, 0.0), jnp.where(low, 0.0, d_y)], axis=0)
            d_w = dot3(d_ys, xc, NT)
            scores = v.scores[0]
            weights = []
            d_scores = None
            for h in range(2):
                head = pl.ds(2 * pair + h, 1)
                decay = v.big_l[2 * pair + h]
                steps = v.dtT[0, head]
                scored = decay * scores
                weights.append(scored * steps)
                d_head = d_w[SEQ * h : SEQ * h + SEQ]
                term = d_head * (decay * steps)
                d_scores = term if d_scores is None else d_scores + term
                v.dirT[head] = jnp.sum(d_head * scored, axis=0, keepdims=True)
            v.ds_acc[0] += d_scores[:64]
            v.ds_acc[1] += d_scores[64:]
            sums = dot_full(head_rows, d_y * y, NT)
            v.rowT[pl.ds(2 * pair, 1)] = sums[0:1]
            v.rowT[pl.ds(2 * pair + 1, 1)] = sums[1:2]
            d_xc = dot3(jnp.concatenate(weights, axis=0), d_ys, TN) + skip * d_y
            d_x = conv_rows_back(d_xc * v.dcv[pair], v.cx[pair])
            d_z = d_gate * v.dzs[pair]
            first, second = split_pair(d_x, d_z)
            first = first.astype(BF16)
            second = second.astype(BF16)
            v.ga_round[me, j, :, 256 * k : 256 * k + 128] = first
            v.ga_round[me, j, :, 256 * k + 128 : 256 * k + 256] = second
            v.pdt[...] += (
                first.astype(F32) * v.raw[j, :, 256 * k : 256 * k + 128]
                + second.astype(F32) * v.raw[j, :, 256 * k + 128 : 256 * k + 256]
            )
        gather(v.ga_round, "rd", me, j, mate).start()
        gather(v.ga_mix, "md2", me, j, mate).start()

    loop(stage_c)
    hand_out(0, me).start()
    hand_out(1, me).start()

    v.dsd_s[...] = v.ds_acc[1 - core]
    dsd().start()
    d_cum = v.rowT[...] - v.dtT[0] * v.dirT[...]
    d_a = dot_full(d_cum, (row_id >= lane_id).astype(F32), NN)
    v.tg[me, 0:16] = (v.dirT[...] + v.negA[...] * d_a) * v.sgT[...]
    v.tg[me, 16:24] = row_sums(v.pdt[...])
    spread_start(v.tg, "tg")
    dsd().wait_recv()
    v.dsy_s[...] = v.ds_acc[core] + v.dsd_r[...]
    dsy().start()

    v.acc0[...] = jnp.zeros((SEQ, SEQ), F32)

    def stage_e(j):
        xzd(1, 1, j).wait_recv()
        xzy(1, j).wait_recv()
        follow(j, lambda i: gather(v.ga_round, "ry", me, i, ypeer).start())
        raw = raw_block(1, act, j)
        for k in range(2):
            pair = 2 * j + k
            gated = mix(1, pair, raw[:, 256 * k : 256 * k + 256], False)
            v.acc0[...] += gated * gated
            v.ga_fwd[me, j, :, 128 * k : 128 * k + 128] = (gated * v.gain[pair]).astype(BF16)
        gather(v.ga_fwd, "fd", me, j, mate).start()

    loop(stage_e)
    v.rf[me] = row_sums(v.acc0[...])
    spread_start(v.rf, "rf")

    v.dn[...] = jnp.zeros((SEQ, 512), F32)

    def add_dn(q, j):
        v.dn[...] += dot1(v.ga_round[q, j], v.w[4 * q + j], NT)

    loop(lambda j: add_dn(me, j))

    dsy().wait_recv()
    v.ds_tot[core] = v.dsy_s[...] + v.dsy_r[...]
    dst(core).start()

    def add_mate(j):
        gather(v.ga_round, "rd", mate, j, mate).wait_recv()
        add_dn(mate, j)

    loop(add_mate)
    hand_out(0, mate).start()
    dst(1 - core).wait_recv()
    d_scores = jnp.concatenate([v.ds_tot[0], v.ds_tot[1]], axis=0)
    ds_high, ds_low = halves(d_scores)
    maps = v.maps[...]
    d_input_map = dot1(ds_high, maps[:, NSTATE:], TN) + dot1(ds_low, maps[:, NSTATE:], TN)
    d_output_map = dot1(ds_high, maps[:, :NSTATE], NN) + dot1(ds_low, maps[:, :NSTATE], NN)
    d_maps = jnp.concatenate([d_input_map, d_output_map], axis=1)
    d_pre = conv_rows_back(d_maps * v.dcm[...], convbc[...])
    v.rbc[:, :MAPS] = d_pre.astype(BF16)
    spread_wait(v.tg, "tg")
    v.pdt[...] = jnp.zeros((SEQ, SEQ), F32)
    for q in range(4):
        v.pdt[16 * q : 16 * q + 16] = v.tg[q, 0:16]
    v.rbc[:, MAPS:] = v.pdt[...].T.astype(BF16)
    rbc_copy = pltpu.make_async_copy(v.rbc, rbc_o, v.s_out.at[9])
    rbc_copy.start()
    product = v.rbc[...].astype(F32) * v.sm[0]
    inner = row_sums(product[:, :128] + product[:, 128:256] + product[:, 256:])
    inner = inner + v.tg[0, 16:24] + v.tg[1, 16:24] + v.tg[2, 16:24] + v.tg[3, 16:24]
    v.acc1[...] = as_column(inner[0:1]) / D
    v.dn[...] += dot1(v.rbc[...], v.wbc[...], NN)

    def pass_on(j):
        gather(v.ga_round, "ry", ypeer, j, ypeer).wait_recv()
        follow(j, lambda i: gather(v.ga_fwd, "fy", me, i, ypeer).start())
        gather(v.ga_round, "rw", ypeer, j, mate).start()
        add_dn(ypeer, j)

    loop(pass_on)
    hand_out(0, ypeer).start()

    def add_diag(j):
        gather(v.ga_round, "rw", diag, j, mate).wait_recv()
        add_dn(diag, j)

    loop(add_diag)
    hand_out(0, diag).start()
    for k in range(4):
        cols = slice(128 * k, 128 * k + 128)
        scale = v.scale[0]
        d_in = scale * v.dn[:, cols] - saved[:, cols].astype(F32) * (
            scale * scale * scale
        ) * v.acc1[...]
        v.sec[0, :, cols] = (cot[:, cols].astype(F32) + d_in).astype(BF16)
    send_section(0).start()

    v.dn[...] = jnp.zeros((SEQ, 512), F32)

    def add_out(q, j):
        v.dn[...] += dot1(v.ga_fwd[q, j], v.wo[4 * q + j], NN)

    loop(lambda j: add_out(me, j))

    def out_mate(j):
        gather(v.ga_fwd, "fd", mate, j, mate).wait_recv()
        add_out(mate, j)

    loop(out_mate)
    loop(lambda j: gather(v.ga_mix, "md2", mate, j, mate).wait_recv())
    hand_out(1, mate).start()
    spread_wait(v.rf, "rf")
    total_rf = v.rf[0] + v.rf[1] + v.rf[2] + v.rf[3]
    v.acc0[...] = lax.rsqrt(as_column(total_rf[0:1]) / INNER + 1e-05)

    def out_peer(j):
        gather(v.ga_fwd, "fy", ypeer, j, ypeer).wait_recv()
        follow(j, lambda i: gather(v.ga_mix, "my2", me, i, ypeer).start())
        gather(v.ga_fwd, "fw", ypeer, j, mate).start()
        add_out(ypeer, j)

    loop(out_peer)

    def out_diag(j):
        gather(v.ga_fwd, "fw", diag, j, mate).wait_recv()
        add_out(diag, j)

    loop(out_diag)
    for k in range(4):
        cols = slice(128 * k, 128 * k + 128)
        mixed = v.dn[:, cols] * v.acc0[...]
        v.sec[1, :, cols] = (act[:, cols].astype(F32) + mixed).astype(BF16)
    send_section(1).start()

    smd().wait_send()
    smy().wait_send()
    smt(core).wait_send()
    dsd().wait_send()
    dsy().wait_send()
    dst(core).wait_send()
    for buf, kind in ((v.sq, "sq"), (v.rs, "rs"), (v.rf, "rf"), (v.tg, "tg")):
        for i in range(3):
            spread(buf, kind, i, me).wait_send()

    def drain(j):
        for mb in range(2):
            for role in range(2):
                xzd(mb, role, j).wait_send()
            xzy(mb, j).wait_send()
        md(0, j).wait_send()
        md(1, j).wait_send()
        my(j).wait_send()
        for buf, kinds in (
            (v.ga_round, ("ry", "rd", "rw")),
            (v.ga_fwd, ("fy", "fd", "fw")),
        ):
            gather(buf, kinds[0], me, j, ypeer).wait_send()
            gather(buf, kinds[1], me, j, mate).wait_send()
            gather(buf, kinds[2], ypeer, j, mate).wait_send()

    loop(drain)
    for q in range(4):
        hand_out(0, q).wait()

    def pass_mix(j):
        gather(v.ga_mix, "my2", ypeer, j, ypeer).wait_recv()
        gather(v.ga_mix, "mw", ypeer, j, mate).start()

    loop(pass_mix)
    hand_out(1, ypeer).start()
    loop(lambda j: gather(v.ga_mix, "mw", diag, j, mate).wait_recv())
    hand_out(1, diag).start()
    for i in range(2):
        send_section(i).wait()
    normed_copy.wait()
    rbc_copy.wait()

    def drain_mix(j):
        gather(v.ga_mix, "my2", me, j, ypeer).wait_send()
        gather(v.ga_mix, "md2", me, j, mate).wait_send()
        gather(v.ga_mix, "mw", ypeer, j, mate).wait_send()

    loop(drain_mix)
    for q in range(4):
        hand_out(1, q).wait()

def chain(saved, act, cot, wxz, wbc, wout, convx, convbc, dtb, alog, dskip, gain):
    table = scratch_table()
    vm = pl.BlockSpec(memory_space=pltpu.VMEM)
    hbm = pl.BlockSpec(memory_space=pl.ANY)
    shape = jax.ShapeDtypeStruct
    return pl.pallas_call(
        functools.partial(chain_kernel, tuple(table)),
        out_shape=(
            shape((4, 4, SEQ, 512), BF16),
            shape((4, 4, 256, SEQ), BF16),
            shape((512, SEQ), BF16),
            shape((SEQ, 384), BF16),
            shape((SEQ, 512), BF16),
            shape((SEQ, 512), BF16),
        ),
        in_specs=[pl.BlockSpec(memory_space=pltpu.HBM)] * 6 + [vm] * 6,
        out_specs=(hbm,) * 6,
        scratch_shapes=list(table.values()),
        compiler_params=pltpu.CompilerParams(
            collective_id=0, has_side_effects=True, vmem_limit_bytes=36 * 1024 * 1024
        ),
        cost_estimate=pl.CostEstimate(
            flops=4_300_000_000, bytes_accessed=18_000_000, transcendentals=2_000_000
        ),
        name="chain",
    )(*(
        pltpu.with_memory_space_constraint(x, pltpu.HBM)
        for x in (saved, act, cot, wxz, wbc, wout, convx, convbc, dtb, alog, dskip, gain)
    ))


def grads_kernel(
    round_ref, mixed_ref, normed_ref, rbc_ref, cot_ref, prev_ref, next_ref,
    xz_o, out_o, bc_o, prev_o, next_o,
    xz_s, out_s, bc_s, s_xz, s_out, s_rest,
):
    small = [
        pltpu.make_async_copy(src, dst, s_rest.at[i])
        for i, (src, dst) in enumerate(((prev_ref, prev_o), (next_ref, next_o), (bc_s, bc_o)))
    ]
    small[0].start()
    small[1].start()

    def xz_copy(i):
        cols = pl.ds(pl.multiple_of(i * 512, 512), 512)
        return pltpu.make_async_copy(xz_s.at[i], xz_o.at[:, cols], s_xz.at[i])

    def out_copy(i):
        rows = pl.ds(pl.multiple_of(i * 256, 256), 256)
        return pltpu.make_async_copy(out_s.at[i], out_o.at[rows], s_out.at[i])

    def step(i, carry):
        out_s[i] = dot1(mixed_ref[i], cot_ref[...], NN)
        out_copy(i).start()
        xz_s[i] = dot1(normed_ref[...], round_ref[i], NN)
        xz_copy(i).start()
        return carry

    lax.fori_loop(0, 16, step, 0)
    bc_s[...] = dot1(rbc_ref[:, :320], normed_ref[...], (((0,), (1,)), ((), ())))
    small[2].start()

    def finish(i, carry):
        out_copy(i).wait()
        xz_copy(i).wait()
        return carry

    lax.fori_loop(0, 16, finish, 0)
    for copy in small:
        copy.wait()


def grads(round_all, mixed_all, normed, rbc, cot, prev_grad, next_act):
    shape = jax.ShapeDtypeStruct
    vm = pl.BlockSpec(memory_space=pltpu.VMEM)
    hbm = pl.BlockSpec(memory_space=pl.ANY)
    dma = pltpu.SemaphoreType.DMA
    return pl.pallas_call(
        grads_kernel,
        out_shape=(
            shape((512, 8192), F32),
            shape((4096, 512), F32),
            shape((320, 512), F32),
            shape((SEQ, 512), BF16),
            shape((SEQ, 512), BF16),
        ),
        in_specs=[vm] * 5 + [hbm] * 2,
        out_specs=(hbm,) * 5,
        scratch_shapes=[
            pltpu.VMEM((16, 512, 512), F32),
            pltpu.VMEM((16, 256, 512), F32),
            pltpu.VMEM((320, 512), F32),
            dma((16,)),
            dma((16,)),
            dma((3,)),
        ],
        compiler_params=pltpu.CompilerParams(vmem_limit_bytes=34 * 1024 * 1024),
        cost_estimate=pl.CostEstimate(
            flops=1_700_000_000, bytes_accessed=29_000_000, transcendentals=0
        ),
        name="grads",
    )(
        round_all.reshape(16, SEQ, 512),
        mixed_all.reshape(16, 256, SEQ),
        normed,
        rbc,
        cot,
        prev_grad,
        next_act,
    )


def per_device_four(
    act_in,
    saved_act,
    cotangent,
    weight_xz,
    weight_bcdt,
    weight_out,
    conv_x,
    conv_bc,
    dt_bias,
    a_log,
    d_skip,
    norm_gain,
):
    round_all, mixed_all, normed, rbc, prev_grad, next_act = chain(
        saved_act[0],
        act_in[0],
        cotangent[0],
        weight_xz[0],
        weight_bcdt[0],
        weight_out[0],
        conv_x[0],
        conv_bc[0],
        dt_bias,
        a_log,
        d_skip,
        norm_gain,
    )
    grad_xz, grad_out, grad_bcdt, prev_grad, next_act = grads(
        round_all, mixed_all, normed, rbc, cotangent[0], prev_grad, next_act
    )
    return (next_act[None], prev_grad[None], grad_xz[None], grad_bcdt[None], grad_out[None])


def solution(mesh):
    return jax.shard_map(
        per_device_four if mesh.shape["dp"] == 4 and mesh.shape["section"] > 1 else per_device,
        mesh=mesh,
        in_specs=(
            P("section", None, "dp"),
            P("section", None, "dp"),
            P("section", None, "dp"),
            P("section", "dp", None),
            P("section", None, "dp"),
            P("section", None, "dp"),
            P("section", None, "dp"),
            P("section", None, None),
            P("section", "dp"),
            P("section", "dp"),
            P("section", "dp"),
            P("section", "dp"),
        ),
        out_specs=(
            P("section", None, "dp"),
            P("section", None, "dp"),
            P("section", "dp", None),
            P("section", None, "dp"),
            P("section", None, "dp"),
        ),
        check_vma=False,
    )
```

```python
import functools

import jax
import jax.numpy as jnp
from jax import lax
from jax.experimental import pallas as pl
from jax.experimental.pallas import tpu as pltpu
from jax.sharding import PartitionSpec as P

D = 2048
HEAD_DIM = 64
NSTATE = 128
HEADS = 64
SEQ = 128
INNER = 4096
KCONV = 4
MAPS = 2 * NSTATE


def from_behind(x, axis, by):
    length = lax.axis_size(axis)
    return lax.ppermute(x, axis, [(i, (i + by) % length) for i in range(length)])


def swap(x, mask):
    length = lax.axis_size("dp")
    return lax.ppermute(x, "dp", [(i, i ^ mask) for i in range(length)])


def masks():
    length = lax.axis_size("dp")
    out = []
    bit = 1
    while bit < length:
        out.append(bit)
        bit *= 2
    return out


def sum_all(x):
    for bit in masks():
        x = x + swap(x, bit)
    return x


def tied(x, other):
    return lax.optimization_barrier((x, other))[0]


def sum_first(part):
    length = lax.axis_size("dp")
    came = {j - 1: swap(part(j).astype(jnp.bfloat16), 1) for j in range(1, length, 2)}
    return {j: part(j) + came[j].astype(jnp.float32) for j in sorted(came, reverse=True)}


def sum_rest(held, after=None):
    first = begun = None
    for bit in masks()[1:]:
        sent = {j: held[j].astype(jnp.bfloat16) for j in held if j & bit}
        if after is not None and first is None:
            sent = {j: tied(x, after) for j, x in sent.items()}
        came = {j ^ bit: swap(x, bit) for j, x in sent.items()}
        if first is None:
            first = came[0]
            begun = sent[bit]
        held = {j: held[j] + came[j].astype(jnp.float32) for j in came}
    return held[0], first, begun


def sum_both(x, after):
    me = lax.axis_index("dp")
    odd = (me & 1) != 0
    x = x + swap(x, 1)
    mine = tied(jnp.where(odd, x[SEQ:], x[:SEQ]), after)
    for bit in masks()[1:]:
        mine = mine + swap(mine, bit)
    other = swap(mine, 1)
    return jnp.where(odd, other, mine), jnp.where(odd, mine, other)


def gather_cols(block, after=None):
    me = lax.axis_index("dp")
    length = lax.axis_size("dp")
    if after is not None:
        block = tied(block, after)
    held = [block]
    order = [0]
    for bit in reversed(masks()):
        held = held + [swap(b, bit) for b in held]
        order = order + [j ^ bit for j in order]
    by_mask = {j: b for j, b in zip(order, held)}
    level = [by_mask[j] for j in range(length)]
    for bit in masks():
        flip = (me & bit) != 0
        level = [jnp.where(flip, level[j ^ bit], level[j]) for j in range(length)]
    return jnp.concatenate(level, axis=1), held[-1]


def causal_conv(values, kernel_taps):
    kernel = kernel_taps.shape[0]
    length = values.shape[0]
    padded = jnp.pad(values, ((kernel - 1, 0), (0, 0)))
    running = jnp.zeros_like(values)
    for offset in range(kernel):
        running = running + kernel_taps[offset] * padded[offset : offset + length]
    return running


def mixer(proj_x, proj_z, proj_dt, scores, conv_taps, dt_offset, log_rate, skip_gain):
    length, width = proj_x.shape
    nheads = dt_offset.shape[0]
    head_width = width // nheads
    xconv = jax.nn.silu(causal_conv(proj_x, conv_taps))
    steps = jax.nn.softplus(proj_dt + dt_offset)
    position = jnp.arange(length)
    causal = position[:, None] >= position[None, :]
    cumul = jnp.dot(
        causal.astype(jnp.float32), steps * -jnp.exp(log_rate), precision=lax.Precision.HIGHEST
    )
    heads_cum = cumul.T
    spread = heads_cum[:, :, None] - heads_cum[:, None, :]
    decay = jnp.where(causal[None], jnp.exp(jnp.where(causal[None], spread, 0.0)), 0.0)
    weights = decay * scores[None] * steps.T[:, None, :]
    heads_in = xconv.reshape(length, nheads, head_width)
    result = jnp.einsum("hts,shp->thp", weights, heads_in, precision=lax.Precision.HIGH)
    result = result + skip_gain[None, :, None] * heads_in
    gate_in = jax.nn.silu(proj_z.reshape(length, nheads, head_width))
    return (result * gate_in).reshape(length, width)


def times_transposed(left, right):
    return lax.dot_general(
        left, right, (((1,), (1,)), ((), ())), preferred_element_type=jnp.float32
    )


def transposed_times(left, right):
    return lax.dot_general(
        left, right, (((0,), (0,)), ((), ())), preferred_element_type=jnp.float32
    )


def per_device(
    act_in,
    saved_act,
    cotangent,
    weight_xz,
    weight_bcdt,
    weight_out,
    conv_x,
    conv_bc,
    dt_bias,
    a_log,
    d_skip,
    norm_gain,
):
    input_rows = act_in[0]
    saved_rows = saved_act[0]
    cot_rows = cotangent[0]
    local_xz = weight_xz[0]
    local_bcdt = weight_bcdt[0]
    local_out = weight_out[0]
    taps_x = conv_x[0]
    taps_bc = conv_bc[0]
    dt_offset = dt_bias[0]
    log_rate = a_log[0]
    skip_gain = d_skip[0]
    gain_local = norm_gain[0]
    own_heads = dt_offset.shape[0]
    me = lax.axis_index("dp")
    head_first = me * own_heads
    width = own_heads * HEAD_DIM

    def whole_act(pre_part):
        return jax.nn.silu(causal_conv(pre_part, taps_bc))

    both = jnp.concatenate([saved_rows, input_rows], axis=0)
    both_values = both.astype(jnp.float32)
    squares = jnp.sum(both_values * both_values, axis=1, keepdims=True)
    def xz_part(j):
        cols = lax.dynamic_slice_in_dim(local_xz, (me ^ j) * 2 * width, 2 * width, 1)
        return jnp.dot(both, cols, preferred_element_type=jnp.float32)

    held_xz = sum_first(xz_part)
    back_raw, back_first, back_begun = sum_rest({j: x[:SEQ] for j, x in held_xz.items()})
    back_small, forward_small = sum_both(
        jnp.concatenate([times_transposed(both, local_bcdt), squares], axis=1), back_begun
    )

    def mixed_part(j):
        taken = lax.dynamic_slice_in_dim(local_out, (me ^ j) * width, width, 0)
        return times_transposed(cot_rows, taken)

    d_mixed = sum_rest(sum_first(mixed_part), back_begun)[0]
    forward_raw = sum_rest({j: x[SEQ:] for j, x in held_xz.items()}, back_first)[0]

    def project(rows, small, raw_xz):
        raw_cols = small[:, : MAPS + HEADS]
        scales = lax.rsqrt(small[:, MAPS + HEADS :] / D + 1e-05)
        return (rows.astype(jnp.float32), scales, raw_xz, raw_cols)

    back_proj = project(saved_rows, back_small, back_raw)
    forward_proj = project(input_rows, forward_small, forward_raw)

    def gate_parts(projected):
        values, scales, raw_xz, raw_cols = projected
        own_xz = raw_xz * scales
        whole_cols = raw_cols * scales
        pre_part = whole_cols[:, :MAPS]
        maps = whole_act(pre_part).astype(jnp.bfloat16)
        own_dt = lax.dynamic_slice_in_dim(whole_cols[:, MAPS:], head_first, own_heads, 1)
        split_xz = own_xz.reshape(SEQ, own_heads, 2, HEAD_DIM)
        mix_x = split_xz[:, :, 0].reshape(SEQ, width)
        mix_z = split_xz[:, :, 1].reshape(SEQ, width)
        scores = times_transposed(maps[:, NSTATE:], maps[:, :NSTATE])

        def local_mix(in_x, in_z, in_dt, in_scores):
            return mixer(in_x, in_z, in_dt, in_scores, taps_x, dt_offset, log_rate, skip_gain)

        gated, mix_back = jax.vjp(local_mix, mix_x, mix_z, own_dt, scores)
        return (gated, mix_back, maps, pre_part)

    values, scales, raw_xz, raw_cols = back_proj
    gated, mix_back, maps, pre_part = gate_parts(back_proj)
    gained = gated * gain_local
    row_sums = sum_all(
        jnp.stack([jnp.sum(gated * gated, axis=1), jnp.sum(d_mixed * gained, axis=1)])
    )
    inverse = lax.rsqrt(row_sums[0] / INNER + 1e-05)[:, None]
    dots = row_sums[1][:, None]
    mixed_in = (gained * inverse).astype(jnp.bfloat16)
    d_gated = inverse * gain_local * d_mixed - gated * (inverse * inverse * inverse) * dots / INNER
    d_px, d_pz, d_pdt, d_scores = mix_back(d_gated)
    own_round = (
        jnp.stack(
            [
                d_px.reshape(SEQ, own_heads, HEAD_DIM),
                d_pz.reshape(SEQ, own_heads, HEAD_DIM),
            ],
            axis=2,
        )
        .reshape(SEQ, own_heads * 2 * HEAD_DIM)
        .astype(jnp.bfloat16)
    )
    round_xz, round_last = gather_cols(own_round)
    inner_own = jnp.sum(own_round.astype(jnp.float32) * raw_xz, axis=1, keepdims=True)
    wide_maps = maps.astype(jnp.float32)
    d_maps = jnp.concatenate(
        [
            jnp.dot(d_scores.T, wide_maps[:, NSTATE:], precision=lax.Precision.HIGH),
            jnp.dot(d_scores, wide_maps[:, :NSTATE], precision=lax.Precision.HIGH),
        ],
        axis=1,
    )
    d_dt_full = lax.dynamic_update_slice_in_dim(
        jnp.zeros((SEQ, HEADS), jnp.float32), d_pdt, head_first, 1
    )
    summed = sum_all(jnp.concatenate([d_maps, d_dt_full, inner_own], axis=1))
    conv_out, conv_back = jax.vjp(whole_act, pre_part)
    d_pre = conv_back(summed[:, :MAPS])[0]
    round_bcdt = jnp.concatenate([d_pre, summed[:, MAPS : MAPS + HEADS]], axis=1).astype(
        jnp.bfloat16
    )
    inner_sum = summed[:, MAPS + HEADS :] + jnp.sum(
        round_bcdt.astype(jnp.float32) * raw_cols, axis=1, keepdims=True
    )

    fwd_gated = gate_parts(forward_proj)[0]
    fwd_all, _ = gather_cols((fwd_gated * gain_local).astype(jnp.bfloat16), round_last)
    fwd_sum = sum_all(jnp.sum(fwd_gated * fwd_gated, axis=1)[None])
    fwd_inverse = lax.rsqrt(fwd_sum[0] / INNER + 1e-05)[:, None]
    mixed = jnp.dot(fwd_all, local_out, preferred_element_type=jnp.float32) * fwd_inverse
    section_out = (input_rows.astype(jnp.float32) + mixed).astype(jnp.bfloat16)
    next_act = from_behind(section_out, "section", 1)

    normed = (values * scales).astype(jnp.bfloat16)
    d_normed = times_transposed(round_xz, local_xz)
    d_normed = d_normed + jnp.dot(round_bcdt, local_bcdt, preferred_element_type=jnp.float32)
    d_norm_in = scales * d_normed - values * (scales * scales * scales) * inner_sum / D
    d_input = (cot_rows.astype(jnp.float32) + d_norm_in).astype(jnp.bfloat16)
    prev_grad = from_behind(d_input, "section", -1)

    grad_out = transposed_times(gather_cols(mixed_in, round_last)[0], cot_rows)
    grad_xz = transposed_times(normed, round_xz)
    grad_bcdt = transposed_times(round_bcdt, normed)
    return (next_act[None], prev_grad[None], grad_xz[None], grad_bcdt[None], grad_out[None])


BF16 = jnp.bfloat16
F32 = jnp.float32
MESH_ID = pl.DeviceIdType.MESH
NN = (((1,), (0,)), ((), ()))
NT = (((1,), (1,)), ((), ()))
TN = (((0,), (0,)), ((), ()))


def dot1(a, b, dims):
    return lax.dot_general(a, b, dims, preferred_element_type=F32)


def dot_full(a, b, dims):
    return lax.dot_general(
        a, b, dims, precision=lax.Precision.HIGHEST, preferred_element_type=F32
    )


def halves(x):
    high = x.astype(BF16)
    return high, (x - high.astype(F32)).astype(BF16)


def dot3(a, b, dims):
    a_high, a_low = halves(a)
    b_high, b_low = halves(b)
    return dot1(a_high, b_high, dims) + (dot1(a_high, b_low, dims) + dot1(a_low, b_high, dims))


def sigmoid(x):
    return 1.0 / (1.0 + jnp.exp(-x))


def d_silu(x, s):
    return s * (1.0 + x * (1.0 - s))


def rows_of(shape):
    return lax.broadcasted_iota(jnp.int32, shape, 0)


def lanes_of(shape):
    return lax.broadcasted_iota(jnp.int32, shape, 1)


def conv_rows(v, taps):
    row = rows_of(v.shape)
    out = taps[KCONV - 1 : KCONV] * v
    for s in range(1, KCONV):
        moved = jnp.where(row >= s, pltpu.roll(v, s, 0), 0.0)
        out = out + taps[KCONV - 1 - s : KCONV - s] * moved
    return out


def conv_rows_back(d, taps):
    row = rows_of(d.shape)
    out = taps[KCONV - 1 : KCONV] * d
    for s in range(1, KCONV):
        moved = jnp.where(row < SEQ - s, pltpu.roll(d, SEQ - s, 0), 0.0)
        out = out + taps[KCONV - 1 - s : KCONV - s] * moved
    return out


def as_column(row):
    return jnp.broadcast_to(row, (SEQ, SEQ)).T


def row_sums(values):
    return dot_full(jnp.ones((8, values.shape[1]), F32), values, NT)


def wide(col, n):
    return jnp.concatenate([col] * n, axis=1)


def scratch_table():
    dma = pltpu.SemaphoreType.DMA
    vm = pltpu.VMEM
    table = dict(
        w=vm((16, 512, 512), BF16),
        wo=vm((16, 256, 512), BF16),
        wbc=vm((384, 512), BF16),
        x2=vm((2, SEQ, 512), BF16),
        cot=vm((SEQ, 512), BF16),
        sec=vm((2, SEQ, 512), BF16),
        normed=vm((512, SEQ), BF16),
        xzd_s=vm((2, 2, 4, SEQ, 512), BF16),
        xzd_r=vm((2, 2, 4, SEQ, 512), BF16),
        xzy_s=vm((2, 4, SEQ, 512), BF16),
        xzy_r=vm((2, 4, SEQ, 512), BF16),
        md_s=vm((2, 4, SEQ, 256), BF16),
        md_r=vm((2, 4, SEQ, 256), BF16),
        my_s=vm((4, SEQ, 256), BF16),
        my_r=vm((4, SEQ, 256), BF16),
        smd_s=vm((SEQ, 384), F32),
        smd_r=vm((SEQ, 384), F32),
        smy_s=vm((320, SEQ), BF16),
        smy_r=vm((320, SEQ), BF16),
        sm=vm((2, SEQ, 384), F32),
        sq=vm((4, 8, SEQ), F32),
        rs=vm((4, 8, SEQ), F32),
        rf=vm((4, 8, SEQ), F32),
        tg=vm((4, 24, SEQ), F32),
        dsd_s=vm((64, SEQ), F32),
        dsd_r=vm((64, SEQ), F32),
        dsy_s=vm((64, SEQ), BF16),
        dsy_r=vm((64, SEQ), BF16),
        ds_tot=vm((2, 64, SEQ), F32),
        ds_acc=vm((2, 64, SEQ), F32),
        ga_round=vm((4, 4, SEQ, 512), BF16),
        ga_mix=vm((4, 256, SEQ), BF16),
        ga_fwd=vm((4, 4, SEQ, 256), BF16),
        big_l=vm((16, SEQ, SEQ), F32),
        xc=vm((8, SEQ, SEQ), F32),
        ys=vm((8, SEQ, SEQ), F32),
        gz=vm((8, SEQ, SEQ), F32),
        dcv=vm((8, SEQ, SEQ), F32),
        dzs=vm((8, SEQ, SEQ), F32),
        dm=vm((8, SEQ, SEQ), F32),
        raw=vm((4, SEQ, 512), F32),
        acc0=vm((SEQ, SEQ), F32),
        acc1=vm((SEQ, SEQ), F32),
        dn=vm((SEQ, 512), F32),
        pdt=vm((SEQ, SEQ), F32),
        dtT=vm((2, 16, SEQ), F32),
        cumT=vm((2, 16, SEQ), F32),
        sgT=vm((16, SEQ), F32),
        negA=vm((16, SEQ), F32),
        dirT=vm((16, SEQ), F32),
        rowT=vm((16, SEQ), F32),
        scores=vm((2, SEQ, SEQ), F32),
        maps=vm((SEQ, 256), BF16),
        dcm=vm((SEQ, 256), F32),
        scale=vm((2, SEQ, SEQ), F32),
        cx=vm((8, KCONV, SEQ), F32),
        gain=vm((8, 1, SEQ), F32),
        dsk=vm((8, 1, SEQ), F32),
        rbc=vm((SEQ, 384), BF16),
        s_w=dma((16,)),
        s_wo=dma((16,)),
        s_in=dma((4,)),
        s_out=dma((10,)),
    )
    for name, shape in dict(
        xzd=(2, 2, 4), xzy=(2, 4), md=(2, 4), my=(4,), smd=(1,), smy=(1,), smt=(1,), sq=(3,), rs=(3,),
        rf=(3,), tg=(3,), dsd=(1,), dsy=(1,), dst=(1,), ry=(4,), rd=(4,), rw=(4,), my2=(4,), md2=(4,),
        mw=(4,), fy=(4,), fd=(4,), fw=(4,), sec=(2,),
    ).items():
        table["a_" + name] = dma(shape)
        table["b_" + name] = dma(shape)
    return table


class Names:
    pass


def chain_kernel(names, *refs):
    (saved_h, act_h, cot_h, wxz_h, wbc_h, wout_h, convx, convbc, dtb, alog, dskip, gain_in,
     round_o, mixed_o, normed_o, rbc_o, prev_o, next_o) = refs[:18]
    v = Names()
    for name, ref in zip(names, refs[18:]):
        setattr(v, name, ref)
    saved, act, cot = v.x2.at[0], v.x2.at[1], v.cot

    me = lax.axis_index("dp")
    core = lax.rem(me, 2)
    mate = me + 1 - 2 * core
    ypeer = me + 2 - 4 * (me // 2)
    diag = 3 - me
    peers = (mate, ypeer, diag)
    sections = lax.axis_size("section")
    place = lax.axis_index("section")
    ahead = lax.rem(place + 1, sections)
    behind = lax.rem(place + sections - 1, sections)

    def remote(src, dst, kind, index, dev):
        return pltpu.make_async_remote_copy(
            src_ref=src,
            dst_ref=dst,
            send_sem=getattr(v, "a_" + kind).at[index],
            recv_sem=getattr(v, "b_" + kind).at[index],
            device_id={"dp": dev},
            device_id_type=MESH_ID,
        )

    def xzd(mb, role, j):
        return remote(v.xzd_s.at[mb, role, j], v.xzd_r.at[mb, role, j], "xzd", (mb, role, j), mate)

    def xzy(mb, j):
        return remote(v.xzy_s.at[mb, j], v.xzy_r.at[mb, j], "xzy", (mb, j), ypeer)

    def md(role, j):
        return remote(v.md_s.at[role, j], v.md_r.at[role, j], "md", (role, j), mate)

    def my(j):
        return remote(v.my_s.at[j], v.my_r.at[j], "my", (j,), ypeer)

    def smd():
        return remote(v.smd_s, v.smd_r, "smd", (0,), mate)

    def smy():
        return remote(v.smy_s, v.smy_r, "smy", (0,), ypeer)

    def smt(mb):
        return remote(v.sm.at[mb], v.sm.at[mb], "smt", (0,), mate)

    def spread(buf, kind, i, slot):
        return remote(buf.at[slot], buf.at[slot], kind, (i,), peers[i])

    def spread_start(buf, kind):
        for i in range(3):
            spread(buf, kind, i, me).start()

    def spread_wait(buf, kind):
        for i in range(3):
            spread(buf, kind, i, peers[i]).wait_recv()

    def dsd():
        return remote(v.dsd_s, v.dsd_r, "dsd", (0,), mate)

    def dsy():
        return remote(v.dsy_s, v.dsy_r, "dsy", (0,), ypeer)

    def dst(half):
        return remote(v.ds_tot.at[half], v.ds_tot.at[half], "dst", (0,), mate)

    def gather(buf, kind, q, j, dev):
        return remote(buf.at[q, j], buf.at[q, j], kind, (j,), dev)

    def send_section(i):
        return pltpu.make_async_remote_copy(
            src_ref=v.sec.at[i],
            dst_ref=(prev_o, next_o)[i],
            send_sem=v.a_sec.at[i],
            recv_sem=v.b_sec.at[i],
            device_id={"section": (behind, ahead)[i]},
            device_id_type=MESH_ID,
        )

    def hand_out(q):
        return pltpu.make_async_copy(v.ga_round.at[q], round_o.at[q], v.s_out.at[q])

    def keep_mix():
        return pltpu.make_async_copy(v.ga_mix, mixed_o.at[me], v.s_out.at[4])

    def send_mix(kind, j, dev):
        return remote(v.ga_mix.at[j], mixed_o.at[me, j], kind, (j,), dev)

    def take_mix(kind, q, j):
        return remote(mixed_o.at[q, j], mixed_o.at[q, j], kind, (j,), mate)

    def load_w(i):
        cols = pl.ds(pl.multiple_of(i * 512, 512), 512)
        return pltpu.make_async_copy(wxz_h.at[:, cols], v.w.at[i], v.s_w.at[i])

    def load_wo(i):
        return pltpu.make_async_copy(
            wout_h.at[pl.ds(pl.multiple_of(i * 256, 256), 256)], v.wo.at[i], v.s_wo.at[i]
        )

    def loop(fn, n=4):
        def step(j, carry):
            fn(j)
            return carry
        lax.fori_loop(0, n, step, 0)

    def follow(j, begin):
        @pl.when(j >= 1)
        def _():
            begin(j - 1)

        @pl.when(j == 3)
        def _():
            begin(3)

    barrier = pltpu.get_barrier_semaphore()
    for peer in peers:
        pl.semaphore_signal(barrier, 1, device_id={"dp": peer}, device_id_type=MESH_ID)
    for other in (ahead, behind):
        pl.semaphore_signal(barrier, 1, device_id={"section": other}, device_id_type=MESH_ID)

    loads = [
        pltpu.make_async_copy(src, dst, v.s_in.at[i])
        for i, (src, dst) in enumerate(
            ((saved_h, saved), (act_h, act), (wbc_h, v.wbc.at[0:320]), (cot_h, v.cot))
        )
    ]
    loads[0].start()
    load_w(4 * diag).start()
    load_w(4 * ypeer).start()
    load_w(4 * diag + 1).start()
    for load in loads[1:]:
        load.start()
    load_w(4 * ypeer + 1).start()
    load_w(4 * diag + 2).start()

    def xz_first(j, ready=None):
        load_w(4 * diag + j).wait()
        v.xzd_s[0, 0, j] = dot1(saved[...], v.w[4 * diag + j], NN).astype(BF16)
        if ready is not None:
            ready()
        xzd(0, 0, j).start()

    def xz_sum(mb, x_ref):
        def fn(j):
            part = dot1(x_ref[...], v.w[4 * ypeer + j], NN)
            xzd(mb, 0, j).wait_recv()
            v.xzy_s[mb, j] = (part + v.xzd_r[mb, 0, j].astype(F32)).astype(BF16)
        return fn

    def xz_back(j):
        load_w(4 * ypeer + j).wait()
        xz_sum(0, saved)(j)
        xzy(0, j).start()

    v.wbc[320:] = jnp.zeros((64, 512), BF16)
    loads[0].wait()
    xz_first(0, lambda: pl.semaphore_wait(barrier, 5))
    load_w(4 * ypeer + 2).start()
    load_w(4 * diag + 3).start()
    load_w(4 * ypeer + 3).start()
    xz_first(1)
    xz_back(0)
    for q in (diag, ypeer):
        loop(lambda j: load_wo(4 * q + j).start())
    for q in (mate, me):
        loop(lambda j: load_w(4 * q + j).start())
    for q in (mate, me):
        loop(lambda j: load_wo(4 * q + j).start())
    loads[1].wait()
    loads[2].wait()
    v.smd_s[...] = dot1(v.x2[1 - core], v.wbc[...], NT)
    smd().start()
    xz_first(2)
    xz_back(1)
    xz_first(3)
    own_small = dot1(v.x2[core], v.wbc[...], NT)
    smd().wait_recv()
    own_small = own_small + v.smd_r[...]
    v.smy_s[0:128] = own_small[:, 0:128].astype(BF16)
    v.smy_s[128:256] = own_small[:, 128:256].astype(BF16)
    v.smy_s[256:320] = own_small[:, 256:384].T[:64].astype(BF16)
    smy().start()
    v.sm[core] = own_small
    xz_back(2)
    squares = []
    for x_ref in (saved, act):
        wide_x = x_ref[...].astype(F32)
        squares.append(row_sums(wide_x * wide_x))
    v.sq[me] = jnp.where(rows_of((8, SEQ)) == 0, squares[0], squares[1])
    spread_start(v.sq, "sq")
    xz_back(3)
    loads[3].wait()

    def m_first(j):
        load_wo(4 * diag + j).wait()
        v.md_s[0, j] = dot1(cot[...], v.wo[4 * diag + j], NT).astype(BF16)
        md(0, j).start()

    loop(m_first)

    def m_sum(j):
        load_wo(4 * ypeer + j).wait()
        part = dot1(cot[...], v.wo[4 * ypeer + j], NT)
        md(0, j).wait_recv()
        v.my_s[j] = (part + v.md_r[0, j].astype(F32)).astype(BF16)

    loop(m_sum)

    def xz_mate(j):
        load_w(4 * mate + j).wait()
        v.xzd_s[0, 1, j] = dot1(saved[...], v.w[4 * mate + j], NN).astype(BF16)
        xzd(0, 1, j).start()

    loop(xz_mate)

    def m_mate(j):
        load_wo(4 * mate + j).wait()
        v.md_s[1, j] = dot1(cot[...], v.wo[4 * mate + j], NT).astype(BF16)
        md(1, j).start()

    loop(m_mate)

    def fwd_first(j):
        v.xzd_s[1, 0, j] = dot1(act[...], v.w[4 * diag + j], NN).astype(BF16)
        xzd(1, 0, j).start()

    loop(fwd_first)

    smy().wait_recv()
    steps_there = jnp.concatenate(
        [v.smy_r[256:320].astype(F32), jnp.zeros((64, SEQ), F32)], axis=0
    ).T
    v.sm[core] = v.sm[core] + jnp.concatenate(
        [v.smy_r[0:128].astype(F32), v.smy_r[128:256].astype(F32), steps_there], axis=1
    )
    smt(core).start()

    expand = (lanes_of((16, 1024)) // HEAD_DIM == rows_of((16, 1024))).astype(F32)
    skip_wide = dot_full(dskip[...], expand, NN)
    for p in range(8):
        cols = slice(128 * p, 128 * p + 128)
        v.cx[p] = convx[:, cols]
        v.gain[p] = gain_in[:, cols]
        v.dsk[p] = skip_wide[:, cols]
    bias_col = jnp.broadcast_to(dtb[...], (SEQ, 16)).T
    v.negA[...] = -jnp.exp(jnp.broadcast_to(alog[...], (SEQ, 16)).T)
    row_id = rows_of((SEQ, SEQ))
    lane_id = lanes_of((SEQ, SEQ))
    causal = row_id >= lane_id
    low = lane_id < HEAD_DIM

    spread_wait(v.sq, "sq")
    total_sq = v.sq[0] + v.sq[1] + v.sq[2] + v.sq[3]
    for mb in range(2):
        v.scale[mb] = lax.rsqrt(as_column(total_sq[mb : mb + 1]) / D + 1e-05)

    smt(1 - core).wait_recv()

    def prepare(mb):
        scale = v.scale[mb]
        small = v.sm[mb] * wide(scale, 3)
        conv = conv_rows(small[:, :MAPS], convbc[...])
        sig = sigmoid(conv)
        maps = (conv * sig).astype(BF16)
        v.scores[mb] = dot1(maps[:, NSTATE:], maps[:, :NSTATE], NT)
        if mb == 0:
            v.maps[...] = maps
            v.dcm[...] = d_silu(conv, sig)
        v.pdt[...] = small[:, MAPS:].T
        logits = v.pdt[pl.ds(pl.multiple_of(16 * me, 16), 16)] + bias_col
        steps = jnp.maximum(logits, 0.0) + jnp.log1p(jnp.exp(-jnp.abs(logits)))
        if mb == 0:
            v.sgT[...] = sigmoid(logits)
        v.dtT[mb] = steps
        v.cumT[mb] = dot_full(
            steps * v.negA[...], (row_id <= lane_id).astype(F32), NN
        )

    prepare(0)

    def split_pair(first, second):
        head_x = jnp.where(low, first, pltpu.roll(second, 64, 1))
        head_z = jnp.where(low, pltpu.roll(first, 64, 1), second)
        return head_x, head_z

    def mix(mb, pair, block, save):
        scale = v.scale[mb]
        x, z = split_pair(block[:, :128] * scale, block[:, 128:] * scale)
        conv = conv_rows(x, v.cx[pair])
        sig = sigmoid(conv)
        xc = conv * sig
        sig_z = sigmoid(z)
        gate = z * sig_z
        weights = []
        for k in range(2):
            head = pl.ds(2 * pair + k, 1)
            row = v.cumT[mb, head]
            decay = jnp.exp(jnp.where(causal, as_column(row) - row, -1e30))
            if save:
                v.big_l[2 * pair + k] = decay
            weights.append(decay * v.scores[mb] * v.dtT[mb, head])
        stacked = jnp.concatenate([jnp.where(low, xc, 0.0), jnp.where(low, 0.0, xc)], axis=0)
        y = dot3(jnp.concatenate(weights, axis=1), stacked, NN)
        if save:
            v.xc[pair] = xc
            v.ys[pair] = y
            v.gz[pair] = gate
            v.dcv[pair] = d_silu(conv, sig)
            v.dzs[pair] = d_silu(z, sig_z)
        return (y + v.dsk[pair] * xc) * gate

    def raw_block(mb, x_ref, j):
        return (
            dot1(x_ref[...], v.w[4 * me + j], NN)
            + v.xzd_r[mb, 1, j].astype(F32)
            + v.xzy_r[mb, j].astype(F32)
        )

    v.acc0[...] = jnp.zeros((SEQ, SEQ), F32)

    def stage_a(j):
        load_w(4 * me + j).wait()
        xzd(0, 1, j).wait_recv()
        xzy(0, j).wait_recv()
        follow(j, lambda i: my(i).start())
        raw = raw_block(0, saved, j)
        v.raw[j] = raw
        for k in range(2):
            gated = mix(0, 2 * j + k, raw[:, 256 * k : 256 * k + 256], True)
            v.acc0[...] += gated * gated

    loop(stage_a)

    def fwd_mate(j):
        v.xzd_s[1, 1, j] = dot1(act[...], v.w[4 * mate + j], NN).astype(BF16)
        xzd(1, 1, j).start()

    loop(xz_sum(1, act))
    loop(fwd_mate)

    v.acc1[...] = jnp.zeros((SEQ, SEQ), F32)

    def stage_b(j):
        load_wo(4 * me + j).wait()
        md(1, j).wait_recv()
        my(j).wait_recv()

        @pl.when(j == 2)
        def _():
            xzy(1, 0).start()

        d_mixed = (
            dot1(cot[...], v.wo[4 * me + j], NT)
            + v.md_r[1, j].astype(F32)
            + v.my_r[j].astype(F32)
        )
        for k in range(2):
            pair = 2 * j + k
            part = d_mixed[:, 128 * k : 128 * k + 128]
            v.dm[pair] = part
            gated = (v.ys[pair] + v.dsk[pair] * v.xc[pair]) * v.gz[pair]
            v.acc1[...] += part * v.gain[pair] * gated

    loop(stage_b)

    v.rs[me] = jnp.where(
        rows_of((8, SEQ)) == 0, row_sums(v.acc0[...]), row_sums(v.acc1[...])
    )
    spread_start(v.rs, "rs")
    loop(lambda j: xzy(1, j + 1).start(), 3)
    prepare(1)
    for k in range(4):
        cols = slice(128 * k, 128 * k + 128)
        normed = (saved[:, cols].astype(F32) * v.scale[0]).astype(BF16)
        v.normed[cols] = normed.astype(F32).T.astype(BF16)
    normed_copy = pltpu.make_async_copy(v.normed, normed_o, v.s_out.at[8])
    normed_copy.start()
    spread_wait(v.rs, "rs")
    total_rs = v.rs[0] + v.rs[1] + v.rs[2] + v.rs[3]
    v.acc0[...] = lax.rsqrt(as_column(total_rs[0:1]) / INNER + 1e-05)
    v.acc1[...] = as_column(total_rs[1:2]) / INNER

    v.pdt[...] = jnp.zeros((SEQ, SEQ), F32)
    v.ds_acc[...] = jnp.zeros((2, 64, SEQ), F32)
    head_rows = (
        lanes_of((8, SEQ)) // HEAD_DIM == rows_of((8, SEQ))
    ).astype(F32)

    def stage_c(j):
        inverse = v.acc0[...]
        lower = inverse * inverse * inverse * v.acc1[...]
        for k in range(2):
            pair = 2 * j + k
            xc = v.xc[pair]
            y = v.ys[pair]
            gate = v.gz[pair]
            skip = v.dsk[pair]
            gained = inverse * v.gain[pair]
            y_full = y + skip * xc
            gated = y_full * gate
            v.ga_mix[j, 128 * k : 128 * k + 128] = (gated * gained).T.astype(BF16)
            d_gated = gained * v.dm[pair] - gated * lower
            d_y = d_gated * gate
            d_gate = d_gated * y_full
            d_ys = jnp.concatenate([jnp.where(low, d_y, 0.0), jnp.where(low, 0.0, d_y)], axis=0)
            d_w = dot3(d_ys, xc, NT)
            scores = v.scores[0]
            weights = []
            d_scores = None
            for h in range(2):
                head = pl.ds(2 * pair + h, 1)
                decay = v.big_l[2 * pair + h]
                steps = v.dtT[0, head]
                scored = decay * scores
                weights.append(scored * steps)
                d_head = d_w[SEQ * h : SEQ * h + SEQ]
                term = d_head * (decay * steps)
                d_scores = term if d_scores is None else d_scores + term
                v.dirT[head] = jnp.sum(d_head * scored, axis=0, keepdims=True)
            v.ds_acc[0] += d_scores[:64]
            v.ds_acc[1] += d_scores[64:]
            sums = dot_full(head_rows, d_y * y, NT)
            v.rowT[pl.ds(2 * pair, 1)] = sums[0:1]
            v.rowT[pl.ds(2 * pair + 1, 1)] = sums[1:2]
            d_xc = dot3(jnp.concatenate(weights, axis=0), d_ys, TN) + skip * d_y
            d_x = conv_rows_back(d_xc * v.dcv[pair], v.cx[pair])
            d_z = d_gate * v.dzs[pair]
            first, second = split_pair(d_x, d_z)
            first = first.astype(BF16)
            second = second.astype(BF16)
            v.ga_round[me, j, :, 256 * k : 256 * k + 128] = first
            v.ga_round[me, j, :, 256 * k + 128 : 256 * k + 256] = second
            v.pdt[...] += (
                first.astype(F32) * v.raw[j, :, 256 * k : 256 * k + 128]
                + second.astype(F32) * v.raw[j, :, 256 * k + 128 : 256 * k + 256]
            )
        gather(v.ga_round, "rd", me, j, mate).start()
        send_mix("md2", j, mate).start()

    loop(stage_c)
    hand_out(me).start()
    keep_mix().start()

    v.dsd_s[...] = v.ds_acc[1 - core]
    dsd().start()
    d_cum = v.rowT[...] - v.dtT[0] * v.dirT[...]
    d_a = dot_full(d_cum, (row_id >= lane_id).astype(F32), NN)
    v.tg[me, 0:16] = (v.dirT[...] + v.negA[...] * d_a) * v.sgT[...]
    v.tg[me, 16:24] = row_sums(v.pdt[...])
    spread_start(v.tg, "tg")
    dsd().wait_recv()
    v.ds_tot[core] = v.ds_acc[core] + v.dsd_r[...]
    v.dsy_s[...] = v.ds_tot[core].astype(BF16)
    dsy().start()

    v.acc0[...] = jnp.zeros((SEQ, SEQ), F32)

    def stage_e(j):
        xzd(1, 1, j).wait_recv()
        xzy(1, j).wait_recv()
        follow(j, lambda i: gather(v.ga_round, "ry", me, i, ypeer).start())
        raw = raw_block(1, act, j)
        for k in range(2):
            pair = 2 * j + k
            gated = mix(1, pair, raw[:, 256 * k : 256 * k + 256], False)
            v.acc0[...] += gated * gated
            v.ga_fwd[me, j, :, 128 * k : 128 * k + 128] = (gated * v.gain[pair]).astype(BF16)
        gather(v.ga_fwd, "fd", me, j, mate).start()

    loop(stage_e)
    v.rf[me] = row_sums(v.acc0[...])
    spread_start(v.rf, "rf")

    v.dn[...] = jnp.zeros((SEQ, 512), F32)

    def add_dn(q, j):
        v.dn[...] += dot1(v.ga_round[q, j], v.w[4 * q + j], NT)

    loop(lambda j: add_dn(me, j))

    dsy().wait_recv()
    v.ds_tot[core] = v.ds_tot[core] + v.dsy_r[...].astype(F32)
    dst(core).start()

    def add_mate(j):
        gather(v.ga_round, "rd", mate, j, mate).wait_recv()
        add_dn(mate, j)

    loop(add_mate)
    hand_out(mate).start()
    dst(1 - core).wait_recv()
    d_scores = jnp.concatenate([v.ds_tot[0], v.ds_tot[1]], axis=0)
    ds_high, ds_low = halves(d_scores)
    maps = v.maps[...]
    d_input_map = dot1(ds_high, maps[:, NSTATE:], TN) + dot1(ds_low, maps[:, NSTATE:], TN)
    d_output_map = dot1(ds_high, maps[:, :NSTATE], NN) + dot1(ds_low, maps[:, :NSTATE], NN)
    d_maps = jnp.concatenate([d_input_map, d_output_map], axis=1)
    d_pre = conv_rows_back(d_maps * v.dcm[...], convbc[...])
    v.rbc[:, :MAPS] = d_pre.astype(BF16)
    spread_wait(v.tg, "tg")
    v.pdt[...] = jnp.zeros((SEQ, SEQ), F32)
    for q in range(4):
        v.pdt[16 * q : 16 * q + 16] = v.tg[q, 0:16]
    v.rbc[:, MAPS:] = v.pdt[...].T.astype(BF16)
    rbc_copy = pltpu.make_async_copy(v.rbc, rbc_o, v.s_out.at[9])
    rbc_copy.start()
    product = v.rbc[...].astype(F32) * v.sm[0]
    inner = row_sums(product[:, :128] + product[:, 128:256] + product[:, 256:])
    inner = inner + v.tg[0, 16:24] + v.tg[1, 16:24] + v.tg[2, 16:24] + v.tg[3, 16:24]
    v.acc1[...] = as_column(inner[0:1]) / D
    v.dn[...] += dot1(v.rbc[...], v.wbc[...], NN)

    def pass_on(j):
        gather(v.ga_round, "ry", ypeer, j, ypeer).wait_recv()
        follow(j, lambda i: gather(v.ga_fwd, "fy", me, i, ypeer).start())
        gather(v.ga_round, "rw", ypeer, j, mate).start()
        add_dn(ypeer, j)

    loop(pass_on)
    hand_out(ypeer).start()

    def add_diag(j):
        gather(v.ga_round, "rw", diag, j, mate).wait_recv()
        add_dn(diag, j)

    loop(add_diag)
    hand_out(diag).start()
    for k in range(4):
        cols = slice(128 * k, 128 * k + 128)
        scale = v.scale[0]
        d_in = scale * v.dn[:, cols] - saved[:, cols].astype(F32) * (
            scale * scale * scale
        ) * v.acc1[...]
        v.sec[0, :, cols] = (cot[:, cols].astype(F32) + d_in).astype(BF16)
    send_section(0).start()
    send_mix("my2", 0, ypeer).start()

    v.dn[...] = jnp.zeros((SEQ, 512), F32)

    def add_out(q, j):
        v.dn[...] += dot1(v.ga_fwd[q, j], v.wo[4 * q + j], NN)

    loop(lambda j: add_out(me, j))

    def out_mate(j):
        gather(v.ga_fwd, "fd", mate, j, mate).wait_recv()
        add_out(mate, j)

    loop(out_mate)
    loop(lambda j: take_mix("md2", mate, j).wait_recv())
    spread_wait(v.rf, "rf")
    total_rf = v.rf[0] + v.rf[1] + v.rf[2] + v.rf[3]
    v.acc0[...] = lax.rsqrt(as_column(total_rf[0:1]) / INNER + 1e-05)

    def out_peer(j):
        gather(v.ga_fwd, "fy", ypeer, j, ypeer).wait_recv()

        @pl.when(j >= 1)
        def _():
            send_mix("my2", j, ypeer).start()

        gather(v.ga_fwd, "fw", ypeer, j, mate).start()
        add_out(ypeer, j)

    loop(out_peer)

    def out_diag(j):
        gather(v.ga_fwd, "fw", diag, j, mate).wait_recv()
        add_out(diag, j)

    loop(out_diag)
    for k in range(4):
        cols = slice(128 * k, 128 * k + 128)
        mixed = v.dn[:, cols] * v.acc0[...]
        v.sec[1, :, cols] = (act[:, cols].astype(F32) + mixed).astype(BF16)
    send_section(1).start()

    smd().wait_send()
    smy().wait_send()
    smt(core).wait_send()
    dsd().wait_send()
    dsy().wait_send()
    dst(core).wait_send()
    for buf, kind in ((v.sq, "sq"), (v.rs, "rs"), (v.rf, "rf"), (v.tg, "tg")):
        for i in range(3):
            spread(buf, kind, i, me).wait_send()

    def drain(j):
        for mb in range(2):
            for role in range(2):
                xzd(mb, role, j).wait_send()
            xzy(mb, j).wait_send()
        md(0, j).wait_send()
        md(1, j).wait_send()
        my(j).wait_send()
        for buf, kinds in (
            (v.ga_round, ("ry", "rd", "rw")),
            (v.ga_fwd, ("fy", "fd", "fw")),
        ):
            gather(buf, kinds[0], me, j, ypeer).wait_send()
            gather(buf, kinds[1], me, j, mate).wait_send()
            gather(buf, kinds[2], ypeer, j, mate).wait_send()

    loop(drain)
    for q in range(4):
        hand_out(q).wait()

    def pass_mix(j):
        take_mix("my2", ypeer, j).wait_recv()
        take_mix("mw", ypeer, j).start()

    loop(pass_mix)
    loop(lambda j: take_mix("mw", diag, j).wait_recv())
    for i in range(2):
        send_section(i).wait()
    normed_copy.wait()
    rbc_copy.wait()

    def drain_mix(j):
        send_mix("my2", j, ypeer).wait_send()
        send_mix("md2", j, mate).wait_send()
        take_mix("mw", ypeer, j).wait_send()

    loop(drain_mix)
    keep_mix().wait()

def chain(saved, act, cot, wxz, wbc, wout, convx, convbc, dtb, alog, dskip, gain):
    table = scratch_table()
    vm = pl.BlockSpec(memory_space=pltpu.VMEM)
    hbm = pl.BlockSpec(memory_space=pl.ANY)
    shape = jax.ShapeDtypeStruct
    return pl.pallas_call(
        functools.partial(chain_kernel, tuple(table)),
        out_shape=(
            shape((4, 4, SEQ, 512), BF16),
            shape((4, 4, 256, SEQ), BF16),
            shape((512, SEQ), BF16),
            shape((SEQ, 384), BF16),
            shape((SEQ, 512), BF16),
            shape((SEQ, 512), BF16),
        ),
        in_specs=[pl.BlockSpec(memory_space=pltpu.HBM)] * 6 + [vm] * 6,
        out_specs=(hbm,) * 6,
        scratch_shapes=list(table.values()),
        compiler_params=pltpu.CompilerParams(
            collective_id=0, has_side_effects=True, vmem_limit_bytes=36 * 1024 * 1024
        ),
        cost_estimate=pl.CostEstimate(
            flops=4_300_000_000, bytes_accessed=18_000_000, transcendentals=2_000_000
        ),
        name="chain",
    )(*(
        pltpu.with_memory_space_constraint(x, pltpu.HBM)
        for x in (saved, act, cot, wxz, wbc, wout, convx, convbc, dtb, alog, dskip, gain)
    ))


def grads_kernel(
    round_ref, mixed_ref, normed_ref, rbc_ref, cot_ref, prev_ref, next_ref,
    xz_o, out_o, bc_o, prev_o, next_o,
    xz_s, out_s, bc_s, s_xz, s_out, s_rest,
):
    small = [
        pltpu.make_async_copy(src, dst, s_rest.at[i])
        for i, (src, dst) in enumerate(((prev_ref, prev_o), (next_ref, next_o), (bc_s, bc_o)))
    ]
    small[0].start()
    small[1].start()

    def xz_copy(i):
        cols = pl.ds(pl.multiple_of(i * 512, 512), 512)
        return pltpu.make_async_copy(xz_s.at[i], xz_o.at[:, cols], s_xz.at[i])

    def out_copy(i):
        rows = pl.ds(pl.multiple_of(i * 256, 256), 256)
        return pltpu.make_async_copy(out_s.at[i], out_o.at[rows], s_out.at[i])

    def step(i, carry):
        out_s[i] = dot1(mixed_ref[i], cot_ref[...], NN)
        out_copy(i).start()
        xz_s[i] = dot1(normed_ref[...], round_ref[i], NN)
        xz_copy(i).start()
        return carry

    lax.fori_loop(0, 16, step, 0)
    bc_s[...] = dot1(rbc_ref[:, :320], normed_ref[...], (((0,), (1,)), ((), ())))
    small[2].start()

    def finish(i, carry):
        out_copy(i).wait()
        xz_copy(i).wait()
        return carry

    lax.fori_loop(0, 16, finish, 0)
    for copy in small:
        copy.wait()


def grads(round_all, mixed_all, normed, rbc, cot, prev_grad, next_act):
    shape = jax.ShapeDtypeStruct
    vm = pl.BlockSpec(memory_space=pltpu.VMEM)
    hbm = pl.BlockSpec(memory_space=pl.ANY)
    dma = pltpu.SemaphoreType.DMA
    return pl.pallas_call(
        grads_kernel,
        out_shape=(
            shape((512, 8192), F32),
            shape((4096, 512), F32),
            shape((320, 512), F32),
            shape((SEQ, 512), BF16),
            shape((SEQ, 512), BF16),
        ),
        in_specs=[vm] * 5 + [hbm] * 2,
        out_specs=(hbm,) * 5,
        scratch_shapes=[
            pltpu.VMEM((16, 512, 512), F32),
            pltpu.VMEM((16, 256, 512), F32),
            pltpu.VMEM((320, 512), F32),
            dma((16,)),
            dma((16,)),
            dma((3,)),
        ],
        compiler_params=pltpu.CompilerParams(vmem_limit_bytes=34 * 1024 * 1024),
        cost_estimate=pl.CostEstimate(
            flops=1_700_000_000, bytes_accessed=29_000_000, transcendentals=0
        ),
        name="grads",
    )(
        round_all.reshape(16, SEQ, 512),
        mixed_all.reshape(16, 256, SEQ),
        normed,
        rbc,
        cot,
        prev_grad,
        next_act,
    )


def per_device_four(
    act_in,
    saved_act,
    cotangent,
    weight_xz,
    weight_bcdt,
    weight_out,
    conv_x,
    conv_bc,
    dt_bias,
    a_log,
    d_skip,
    norm_gain,
):
    round_all, mixed_all, normed, rbc, prev_grad, next_act = chain(
        saved_act[0],
        act_in[0],
        cotangent[0],
        weight_xz[0],
        weight_bcdt[0],
        weight_out[0],
        conv_x[0],
        conv_bc[0],
        dt_bias,
        a_log,
        d_skip,
        norm_gain,
    )
    grad_xz, grad_out, grad_bcdt, prev_grad, next_act = grads(
        round_all, mixed_all, normed, rbc, cotangent[0], prev_grad, next_act
    )
    return (next_act[None], prev_grad[None], grad_xz[None], grad_bcdt[None], grad_out[None])


def solution(mesh):
    return jax.shard_map(
        per_device_four if mesh.shape["dp"] == 4 and mesh.shape["section"] > 1 else per_device,
        mesh=mesh,
        in_specs=(
            P("section", None, "dp"),
            P("section", None, "dp"),
            P("section", None, "dp"),
            P("section", "dp", None),
            P("section", None, "dp"),
            P("section", None, "dp"),
            P("section", None, "dp"),
            P("section", None, None),
            P("section", "dp"),
            P("section", "dp"),
            P("section", "dp"),
            P("section", "dp"),
        ),
        out_specs=(
            P("section", None, "dp"),
            P("section", None, "dp"),
            P("section", "dp", None),
            P("section", None, "dp"),
            P("section", None, "dp"),
        ),
        check_vma=False,
    )
```

```python
import functools

import jax
import jax.numpy as jnp
from jax import lax
from jax.experimental import pallas as pl
from jax.experimental.pallas import tpu as pltpu
from jax.sharding import PartitionSpec as P

D = 2048
HEAD_DIM = 64
NSTATE = 128
HEADS = 64
SEQ = 128
INNER = 4096
KCONV = 4
MAPS = 2 * NSTATE


def from_behind(x, axis, by):
    length = lax.axis_size(axis)
    return lax.ppermute(x, axis, [(i, (i + by) % length) for i in range(length)])


def swap(x, mask):
    length = lax.axis_size("dp")
    return lax.ppermute(x, "dp", [(i, i ^ mask) for i in range(length)])


def masks():
    length = lax.axis_size("dp")
    out = []
    bit = 1
    while bit < length:
        out.append(bit)
        bit *= 2
    return out


def sum_all(x):
    for bit in masks():
        x = x + swap(x, bit)
    return x


def tied(x, other):
    return lax.optimization_barrier((x, other))[0]


def sum_first(part):
    length = lax.axis_size("dp")
    came = {j - 1: swap(part(j).astype(jnp.bfloat16), 1) for j in range(1, length, 2)}
    return {j: part(j) + came[j].astype(jnp.float32) for j in sorted(came, reverse=True)}


def sum_rest(held, after=None):
    first = begun = None
    for bit in masks()[1:]:
        sent = {j: held[j].astype(jnp.bfloat16) for j in held if j & bit}
        if after is not None and first is None:
            sent = {j: tied(x, after) for j, x in sent.items()}
        came = {j ^ bit: swap(x, bit) for j, x in sent.items()}
        if first is None:
            first = came[0]
            begun = sent[bit]
        held = {j: held[j] + came[j].astype(jnp.float32) for j in came}
    return held[0], first, begun


def sum_both(x, after):
    me = lax.axis_index("dp")
    odd = (me & 1) != 0
    x = x + swap(x, 1)
    mine = tied(jnp.where(odd, x[SEQ:], x[:SEQ]), after)
    for bit in masks()[1:]:
        mine = mine + swap(mine, bit)
    other = swap(mine, 1)
    return jnp.where(odd, other, mine), jnp.where(odd, mine, other)


def gather_cols(block, after=None):
    me = lax.axis_index("dp")
    length = lax.axis_size("dp")
    if after is not None:
        block = tied(block, after)
    held = [block]
    order = [0]
    for bit in reversed(masks()):
        held = held + [swap(b, bit) for b in held]
        order = order + [j ^ bit for j in order]
    by_mask = {j: b for j, b in zip(order, held)}
    level = [by_mask[j] for j in range(length)]
    for bit in masks():
        flip = (me & bit) != 0
        level = [jnp.where(flip, level[j ^ bit], level[j]) for j in range(length)]
    return jnp.concatenate(level, axis=1), held[-1]


def causal_conv(values, kernel_taps):
    kernel = kernel_taps.shape[0]
    length = values.shape[0]
    padded = jnp.pad(values, ((kernel - 1, 0), (0, 0)))
    running = jnp.zeros_like(values)
    for offset in range(kernel):
        running = running + kernel_taps[offset] * padded[offset : offset + length]
    return running


def mixer(proj_x, proj_z, proj_dt, scores, conv_taps, dt_offset, log_rate, skip_gain):
    length, width = proj_x.shape
    nheads = dt_offset.shape[0]
    head_width = width // nheads
    xconv = jax.nn.silu(causal_conv(proj_x, conv_taps))
    steps = jax.nn.softplus(proj_dt + dt_offset)
    position = jnp.arange(length)
    causal = position[:, None] >= position[None, :]
    cumul = jnp.dot(
        causal.astype(jnp.float32), steps * -jnp.exp(log_rate), precision=lax.Precision.HIGHEST
    )
    heads_cum = cumul.T
    spread = heads_cum[:, :, None] - heads_cum[:, None, :]
    decay = jnp.where(causal[None], jnp.exp(jnp.where(causal[None], spread, 0.0)), 0.0)
    weights = decay * scores[None] * steps.T[:, None, :]
    heads_in = xconv.reshape(length, nheads, head_width)
    result = jnp.einsum("hts,shp->thp", weights, heads_in, precision=lax.Precision.HIGH)
    result = result + skip_gain[None, :, None] * heads_in
    gate_in = jax.nn.silu(proj_z.reshape(length, nheads, head_width))
    return (result * gate_in).reshape(length, width)


def times_transposed(left, right):
    return lax.dot_general(
        left, right, (((1,), (1,)), ((), ())), preferred_element_type=jnp.float32
    )


def transposed_times(left, right):
    return lax.dot_general(
        left, right, (((0,), (0,)), ((), ())), preferred_element_type=jnp.float32
    )


def per_device(
    act_in,
    saved_act,
    cotangent,
    weight_xz,
    weight_bcdt,
    weight_out,
    conv_x,
    conv_bc,
    dt_bias,
    a_log,
    d_skip,
    norm_gain,
):
    input_rows = act_in[0]
    saved_rows = saved_act[0]
    cot_rows = cotangent[0]
    local_xz = weight_xz[0]
    local_bcdt = weight_bcdt[0]
    local_out = weight_out[0]
    taps_x = conv_x[0]
    taps_bc = conv_bc[0]
    dt_offset = dt_bias[0]
    log_rate = a_log[0]
    skip_gain = d_skip[0]
    gain_local = norm_gain[0]
    own_heads = dt_offset.shape[0]
    me = lax.axis_index("dp")
    head_first = me * own_heads
    width = own_heads * HEAD_DIM

    def whole_act(pre_part):
        return jax.nn.silu(causal_conv(pre_part, taps_bc))

    both = jnp.concatenate([saved_rows, input_rows], axis=0)
    both_values = both.astype(jnp.float32)
    squares = jnp.sum(both_values * both_values, axis=1, keepdims=True)
    def xz_part(j):
        cols = lax.dynamic_slice_in_dim(local_xz, (me ^ j) * 2 * width, 2 * width, 1)
        return jnp.dot(both, cols, preferred_element_type=jnp.float32)

    held_xz = sum_first(xz_part)
    back_raw, back_first, back_begun = sum_rest({j: x[:SEQ] for j, x in held_xz.items()})
    back_small, forward_small = sum_both(
        jnp.concatenate([times_transposed(both, local_bcdt), squares], axis=1), back_begun
    )

    def mixed_part(j):
        taken = lax.dynamic_slice_in_dim(local_out, (me ^ j) * width, width, 0)
        return times_transposed(cot_rows, taken)

    d_mixed = sum_rest(sum_first(mixed_part), back_begun)[0]
    forward_raw = sum_rest({j: x[SEQ:] for j, x in held_xz.items()}, back_first)[0]

    def project(rows, small, raw_xz):
        raw_cols = small[:, : MAPS + HEADS]
        scales = lax.rsqrt(small[:, MAPS + HEADS :] / D + 1e-05)
        return (rows.astype(jnp.float32), scales, raw_xz, raw_cols)

    back_proj = project(saved_rows, back_small, back_raw)
    forward_proj = project(input_rows, forward_small, forward_raw)

    def gate_parts(projected):
        values, scales, raw_xz, raw_cols = projected
        own_xz = raw_xz * scales
        whole_cols = raw_cols * scales
        pre_part = whole_cols[:, :MAPS]
        maps = whole_act(pre_part).astype(jnp.bfloat16)
        own_dt = lax.dynamic_slice_in_dim(whole_cols[:, MAPS:], head_first, own_heads, 1)
        split_xz = own_xz.reshape(SEQ, own_heads, 2, HEAD_DIM)
        mix_x = split_xz[:, :, 0].reshape(SEQ, width)
        mix_z = split_xz[:, :, 1].reshape(SEQ, width)
        scores = times_transposed(maps[:, NSTATE:], maps[:, :NSTATE])

        def local_mix(in_x, in_z, in_dt, in_scores):
            return mixer(in_x, in_z, in_dt, in_scores, taps_x, dt_offset, log_rate, skip_gain)

        gated, mix_back = jax.vjp(local_mix, mix_x, mix_z, own_dt, scores)
        return (gated, mix_back, maps, pre_part)

    values, scales, raw_xz, raw_cols = back_proj
    gated, mix_back, maps, pre_part = gate_parts(back_proj)
    gained = gated * gain_local
    row_sums = sum_all(
        jnp.stack([jnp.sum(gated * gated, axis=1), jnp.sum(d_mixed * gained, axis=1)])
    )
    inverse = lax.rsqrt(row_sums[0] / INNER + 1e-05)[:, None]
    dots = row_sums[1][:, None]
    mixed_in = (gained * inverse).astype(jnp.bfloat16)
    d_gated = inverse * gain_local * d_mixed - gated * (inverse * inverse * inverse) * dots / INNER
    d_px, d_pz, d_pdt, d_scores = mix_back(d_gated)
    own_round = (
        jnp.stack(
            [
                d_px.reshape(SEQ, own_heads, HEAD_DIM),
                d_pz.reshape(SEQ, own_heads, HEAD_DIM),
            ],
            axis=2,
        )
        .reshape(SEQ, own_heads * 2 * HEAD_DIM)
        .astype(jnp.bfloat16)
    )
    round_xz, round_last = gather_cols(own_round)
    inner_own = jnp.sum(own_round.astype(jnp.float32) * raw_xz, axis=1, keepdims=True)
    wide_maps = maps.astype(jnp.float32)
    d_maps = jnp.concatenate(
        [
            jnp.dot(d_scores.T, wide_maps[:, NSTATE:], precision=lax.Precision.HIGH),
            jnp.dot(d_scores, wide_maps[:, :NSTATE], precision=lax.Precision.HIGH),
        ],
        axis=1,
    )
    d_dt_full = lax.dynamic_update_slice_in_dim(
        jnp.zeros((SEQ, HEADS), jnp.float32), d_pdt, head_first, 1
    )
    summed = sum_all(jnp.concatenate([d_maps, d_dt_full, inner_own], axis=1))
    conv_out, conv_back = jax.vjp(whole_act, pre_part)
    d_pre = conv_back(summed[:, :MAPS])[0]
    round_bcdt = jnp.concatenate([d_pre, summed[:, MAPS : MAPS + HEADS]], axis=1).astype(
        jnp.bfloat16
    )
    inner_sum = summed[:, MAPS + HEADS :] + jnp.sum(
        round_bcdt.astype(jnp.float32) * raw_cols, axis=1, keepdims=True
    )

    fwd_gated = gate_parts(forward_proj)[0]
    fwd_all, _ = gather_cols((fwd_gated * gain_local).astype(jnp.bfloat16), round_last)
    fwd_sum = sum_all(jnp.sum(fwd_gated * fwd_gated, axis=1)[None])
    fwd_inverse = lax.rsqrt(fwd_sum[0] / INNER + 1e-05)[:, None]
    mixed = jnp.dot(fwd_all, local_out, preferred_element_type=jnp.float32) * fwd_inverse
    section_out = (input_rows.astype(jnp.float32) + mixed).astype(jnp.bfloat16)
    next_act = from_behind(section_out, "section", 1)

    normed = (values * scales).astype(jnp.bfloat16)
    d_normed = times_transposed(round_xz, local_xz)
    d_normed = d_normed + jnp.dot(round_bcdt, local_bcdt, preferred_element_type=jnp.float32)
    d_norm_in = scales * d_normed - values * (scales * scales * scales) * inner_sum / D
    d_input = (cot_rows.astype(jnp.float32) + d_norm_in).astype(jnp.bfloat16)
    prev_grad = from_behind(d_input, "section", -1)

    grad_out = transposed_times(gather_cols(mixed_in, round_last)[0], cot_rows)
    grad_xz = transposed_times(normed, round_xz)
    grad_bcdt = transposed_times(round_bcdt, normed)
    return (next_act[None], prev_grad[None], grad_xz[None], grad_bcdt[None], grad_out[None])


BF16 = jnp.bfloat16
F32 = jnp.float32
MESH_ID = pl.DeviceIdType.MESH
NN = (((1,), (0,)), ((), ()))
NT = (((1,), (1,)), ((), ()))
TN = (((0,), (0,)), ((), ()))


def dot1(a, b, dims):
    return lax.dot_general(a, b, dims, preferred_element_type=F32)


def dot_full(a, b, dims):
    return lax.dot_general(
        a, b, dims, precision=lax.Precision.HIGHEST, preferred_element_type=F32
    )


def halves(x):
    high = x.astype(BF16)
    return high, (x - high.astype(F32)).astype(BF16)


def dot3(a, b, dims):
    a_high, a_low = halves(a)
    b_high, b_low = halves(b)
    return dot1(a_high, b_high, dims) + (dot1(a_high, b_low, dims) + dot1(a_low, b_high, dims))


def sigmoid(x):
    return 1.0 / (1.0 + jnp.exp(-x))


def d_silu(x, s):
    return s * (1.0 + x * (1.0 - s))


def rows_of(shape):
    return lax.broadcasted_iota(jnp.int32, shape, 0)


def lanes_of(shape):
    return lax.broadcasted_iota(jnp.int32, shape, 1)


def conv_rows(v, taps):
    row = rows_of(v.shape)
    out = taps[KCONV - 1 : KCONV] * v
    for s in range(1, KCONV):
        moved = jnp.where(row >= s, pltpu.roll(v, s, 0), 0.0)
        out = out + taps[KCONV - 1 - s : KCONV - s] * moved
    return out


def conv_rows_back(d, taps):
    row = rows_of(d.shape)
    out = taps[KCONV - 1 : KCONV] * d
    for s in range(1, KCONV):
        moved = jnp.where(row < SEQ - s, pltpu.roll(d, SEQ - s, 0), 0.0)
        out = out + taps[KCONV - 1 - s : KCONV - s] * moved
    return out


def as_column(row):
    return jnp.broadcast_to(row, (SEQ, SEQ)).T


def row_sums(values):
    return dot_full(jnp.ones((8, values.shape[1]), F32), values, NT)


def wide(col, n):
    return jnp.concatenate([col] * n, axis=1)


def scratch_table():
    dma = pltpu.SemaphoreType.DMA
    vm = pltpu.VMEM
    table = dict(
        w=vm((16, 512, 512), BF16),
        wo=vm((16, 256, 512), BF16),
        wbc=vm((384, 512), BF16),
        x2=vm((2, SEQ, 512), BF16),
        cot=vm((SEQ, 512), BF16),
        sec=vm((2, SEQ, 512), BF16),
        normed=vm((512, SEQ), BF16),
        xzd_s=vm((2, 2, 4, SEQ, 512), BF16),
        xzd_r=vm((2, 2, 4, SEQ, 512), BF16),
        xzy_s=vm((2, 4, SEQ, 512), BF16),
        xzy_r=vm((2, 4, SEQ, 512), BF16),
        md_s=vm((2, 4, SEQ, 256), BF16),
        md_r=vm((2, 4, SEQ, 256), BF16),
        my_s=vm((4, SEQ, 256), BF16),
        my_r=vm((4, SEQ, 256), BF16),
        smd_s=vm((SEQ, 384), F32),
        smd_r=vm((SEQ, 384), F32),
        smy_s=vm((320, SEQ), BF16),
        smy_r=vm((320, SEQ), BF16),
        sm=vm((2, SEQ, 384), F32),
        sq=vm((4, 8, SEQ), F32),
        rs=vm((4, 8, SEQ), F32),
        rf=vm((4, 8, SEQ), F32),
        tg=vm((4, 24, SEQ), F32),
        dsd_s=vm((64, SEQ), F32),
        dsd_r=vm((64, SEQ), F32),
        dsy_s=vm((64, SEQ), BF16),
        dsy_r=vm((64, SEQ), BF16),
        ds_tot=vm((2, 64, SEQ), F32),
        ds_acc=vm((2, 64, SEQ), F32),
        ga_round=vm((4, 4, SEQ, 512), BF16),
        ga_mix=vm((4, 256, SEQ), BF16),
        ga_fwd=vm((4, 4, SEQ, 256), BF16),
        big_l=vm((16, SEQ, SEQ), F32),
        xc=vm((8, SEQ, SEQ), F32),
        ys=vm((8, SEQ, SEQ), F32),
        gz=vm((8, SEQ, SEQ), F32),
        dcv=vm((8, SEQ, SEQ), F32),
        dzs=vm((8, SEQ, SEQ), F32),
        dm=vm((8, SEQ, SEQ), F32),
        raw=vm((4, SEQ, 512), F32),
        acc0=vm((SEQ, SEQ), F32),
        acc1=vm((SEQ, SEQ), F32),
        dn=vm((SEQ, 512), F32),
        total=vm((SEQ, 512), F32),
        pdt=vm((SEQ, SEQ), F32),
        dtT=vm((2, 16, SEQ), F32),
        cumT=vm((2, 16, SEQ), F32),
        sgT=vm((16, SEQ), F32),
        negA=vm((16, SEQ), F32),
        dirT=vm((16, SEQ), F32),
        rowT=vm((16, SEQ), F32),
        scores=vm((2, SEQ, SEQ), F32),
        maps=vm((SEQ, 256), BF16),
        dcm=vm((SEQ, 256), F32),
        scale=vm((2, SEQ, SEQ), F32),
        cx=vm((8, KCONV, SEQ), F32),
        gain=vm((8, 1, SEQ), F32),
        dsk=vm((8, 1, SEQ), F32),
        rbc=vm((SEQ, 384), BF16),
        s_w=dma((16,)),
        s_wo=dma((16,)),
        s_in=dma((4,)),
        s_out=dma((10,)),
    )
    for name, shape in dict(
        xzd=(2, 2, 4), xzy=(2, 4), md=(2, 4), my=(4,), smd=(1,), smy=(1,), smt=(1,), sq=(3,), rs=(3,),
        rf=(3,), tg=(3,), dsd=(1,), dsy=(1,), dst=(1,), ry=(4,), rd=(4,), rw=(4,), my2=(4,), md2=(4,),
        mw=(4,), fy=(4,), fd=(4,), fw=(4,), sec=(2,),
    ).items():
        table["a_" + name] = dma(shape)
        table["b_" + name] = dma(shape)
    return table


class Names:
    pass


def chain_kernel(names, *refs):
    (saved_h, act_h, cot_h, wxz_h, wbc_h, wout_h, convx, convbc, dtb, alog, dskip, gain_in,
     round_o, mixed_o, normed_o, rbc_o, prev_o, next_o) = refs[:18]
    v = Names()
    for name, ref in zip(names, refs[18:]):
        setattr(v, name, ref)
    saved, act, cot = v.x2.at[0], v.x2.at[1], v.cot

    me = lax.axis_index("dp")
    core = lax.rem(me, 2)
    mate = me + 1 - 2 * core
    ypeer = me + 2 - 4 * (me // 2)
    diag = 3 - me
    peers = (mate, ypeer, diag)
    sections = lax.axis_size("section")
    place = lax.axis_index("section")
    ahead = lax.rem(place + 1, sections)
    behind = lax.rem(place + sections - 1, sections)

    def remote(src, dst, kind, index, dev):
        return pltpu.make_async_remote_copy(
            src_ref=src,
            dst_ref=dst,
            send_sem=getattr(v, "a_" + kind).at[index],
            recv_sem=getattr(v, "b_" + kind).at[index],
            device_id={"dp": dev},
            device_id_type=MESH_ID,
        )

    def xzd(mb, role, j):
        return remote(v.xzd_s.at[mb, role, j], v.xzd_r.at[mb, role, j], "xzd", (mb, role, j), mate)

    def xzy(mb, j):
        return remote(v.xzy_s.at[mb, j], v.xzy_r.at[mb, j], "xzy", (mb, j), ypeer)

    def md(role, j):
        return remote(v.md_s.at[role, j], v.md_r.at[role, j], "md", (role, j), mate)

    def my(j):
        return remote(v.my_s.at[j], v.my_r.at[j], "my", (j,), ypeer)

    def smd():
        return remote(v.smd_s, v.smd_r, "smd", (0,), mate)

    def smy():
        return remote(v.smy_s, v.smy_r, "smy", (0,), ypeer)

    def smt(mb):
        return remote(v.sm.at[mb], v.sm.at[mb], "smt", (0,), mate)

    def spread(buf, kind, i, slot):
        return remote(buf.at[slot], buf.at[slot], kind, (i,), peers[i])

    def spread_start(buf, kind):
        for i in range(3):
            spread(buf, kind, i, me).start()

    def spread_wait(buf, kind):
        for i in range(3):
            spread(buf, kind, i, peers[i]).wait_recv()

    def dsd():
        return remote(v.dsd_s, v.dsd_r, "dsd", (0,), mate)

    def dsy():
        return remote(v.dsy_s, v.dsy_r, "dsy", (0,), ypeer)

    def dst(half):
        return remote(v.ds_tot.at[half], v.ds_tot.at[half], "dst", (0,), mate)

    def gather(buf, kind, q, j, dev):
        return remote(buf.at[q, j], buf.at[q, j], kind, (j,), dev)

    def send_section(i):
        return pltpu.make_async_remote_copy(
            src_ref=v.sec.at[i],
            dst_ref=(prev_o, next_o)[i],
            send_sem=v.a_sec.at[i],
            recv_sem=v.b_sec.at[i],
            device_id={"section": (behind, ahead)[i]},
            device_id_type=MESH_ID,
        )

    def hand_out(q):
        return pltpu.make_async_copy(v.ga_round.at[q], round_o.at[q], v.s_out.at[q])

    def keep_mix():
        return pltpu.make_async_copy(v.ga_mix, mixed_o.at[me], v.s_out.at[4])

    def send_mix(kind, j, dev):
        return remote(v.ga_mix.at[j], mixed_o.at[me, j], kind, (j,), dev)

    def take_mix(kind, q, j):
        return remote(mixed_o.at[q, j], mixed_o.at[q, j], kind, (j,), mate)

    def load_w(i):
        cols = pl.ds(pl.multiple_of(i * 512, 512), 512)
        return pltpu.make_async_copy(wxz_h.at[:, cols], v.w.at[i], v.s_w.at[i])

    def load_wo(i):
        return pltpu.make_async_copy(
            wout_h.at[pl.ds(pl.multiple_of(i * 256, 256), 256)], v.wo.at[i], v.s_wo.at[i]
        )

    def loop(fn, n=4):
        def step(j, carry):
            fn(j)
            return carry
        lax.fori_loop(0, n, step, 0)

    def follow(j, begin):
        @pl.when(j >= 1)
        def _():
            begin(j - 1)

        @pl.when(j == 3)
        def _():
            begin(3)

    barrier = pltpu.get_barrier_semaphore()
    for peer in peers:
        pl.semaphore_signal(barrier, 1, device_id={"dp": peer}, device_id_type=MESH_ID)
    for other in (ahead, behind):
        pl.semaphore_signal(barrier, 1, device_id={"section": other}, device_id_type=MESH_ID)

    loads = [
        pltpu.make_async_copy(src, dst, v.s_in.at[i])
        for i, (src, dst) in enumerate(
            ((saved_h, saved), (act_h, act), (wbc_h, v.wbc.at[0:320]), (cot_h, v.cot))
        )
    ]
    loads[0].start()
    load_w(4 * diag).start()
    load_w(4 * ypeer).start()
    load_w(4 * diag + 1).start()
    for load in loads[1:]:
        load.start()
    load_w(4 * ypeer + 1).start()
    load_w(4 * diag + 2).start()

    def xz_first(j, ready=None):
        load_w(4 * diag + j).wait()
        v.xzd_s[0, 0, j] = dot1(saved[...], v.w[4 * diag + j], NN).astype(BF16)
        if ready is not None:
            ready()
        xzd(0, 0, j).start()

    def xz_sum(mb, x_ref):
        def fn(j):
            part = dot1(x_ref[...], v.w[4 * ypeer + j], NN)
            xzd(mb, 0, j).wait_recv()
            v.xzy_s[mb, j] = (part + v.xzd_r[mb, 0, j].astype(F32)).astype(BF16)
        return fn

    def xz_back(j):
        load_w(4 * ypeer + j).wait()
        xz_sum(0, saved)(j)
        xzy(0, j).start()

    v.wbc[320:] = jnp.zeros((64, 512), BF16)
    loads[0].wait()
    xz_first(0, lambda: pl.semaphore_wait(barrier, 5))
    load_w(4 * ypeer + 2).start()
    load_w(4 * diag + 3).start()
    load_w(4 * ypeer + 3).start()
    xz_first(1)
    xz_back(0)
    for q in (diag, ypeer):
        loop(lambda j: load_wo(4 * q + j).start())
    for q in (mate, me):
        loop(lambda j: load_w(4 * q + j).start())
    for q in (mate, me):
        loop(lambda j: load_wo(4 * q + j).start())
    loads[1].wait()
    loads[2].wait()
    v.smd_s[...] = dot1(v.x2[1 - core], v.wbc[...], NT)
    smd().start()
    xz_first(2)
    xz_back(1)
    xz_first(3)
    own_small = dot1(v.x2[core], v.wbc[...], NT)
    smd().wait_recv()
    own_small = own_small + v.smd_r[...]
    v.smy_s[0:128] = own_small[:, 0:128].astype(BF16)
    v.smy_s[128:256] = own_small[:, 128:256].astype(BF16)
    v.smy_s[256:320] = own_small[:, 256:384].T[:64].astype(BF16)
    smy().start()
    v.sm[core] = own_small
    xz_back(2)
    squares = []
    for x_ref in (saved, act):
        wide_x = x_ref[...].astype(F32)
        squares.append(row_sums(wide_x * wide_x))
    v.sq[me] = jnp.where(rows_of((8, SEQ)) == 0, squares[0], squares[1])
    spread_start(v.sq, "sq")
    xz_back(3)
    loads[3].wait()

    def m_first(j):
        load_wo(4 * diag + j).wait()
        v.md_s[0, j] = dot1(cot[...], v.wo[4 * diag + j], NT).astype(BF16)
        md(0, j).start()

    loop(m_first)

    def m_sum(j):
        load_wo(4 * ypeer + j).wait()
        part = dot1(cot[...], v.wo[4 * ypeer + j], NT)
        md(0, j).wait_recv()
        v.my_s[j] = (part + v.md_r[0, j].astype(F32)).astype(BF16)

    loop(m_sum)

    def xz_mate(j):
        load_w(4 * mate + j).wait()
        v.xzd_s[0, 1, j] = dot1(saved[...], v.w[4 * mate + j], NN).astype(BF16)
        xzd(0, 1, j).start()

    loop(xz_mate)

    def m_mate(j):
        load_wo(4 * mate + j).wait()
        v.md_s[1, j] = dot1(cot[...], v.wo[4 * mate + j], NT).astype(BF16)
        md(1, j).start()

    loop(m_mate)

    def fwd_first(j):
        v.xzd_s[1, 0, j] = dot1(act[...], v.w[4 * diag + j], NN).astype(BF16)
        xzd(1, 0, j).start()

    loop(fwd_first)

    smy().wait_recv()
    steps_there = jnp.concatenate(
        [v.smy_r[256:320].astype(F32), jnp.zeros((64, SEQ), F32)], axis=0
    ).T
    v.sm[core] = v.sm[core] + jnp.concatenate(
        [v.smy_r[0:128].astype(F32), v.smy_r[128:256].astype(F32), steps_there], axis=1
    )
    smt(core).start()

    expand = (lanes_of((16, 1024)) // HEAD_DIM == rows_of((16, 1024))).astype(F32)
    skip_wide = dot_full(dskip[...], expand, NN)
    for p in range(8):
        cols = slice(128 * p, 128 * p + 128)
        v.cx[p] = convx[:, cols]
        v.gain[p] = gain_in[:, cols]
        v.dsk[p] = skip_wide[:, cols]
    bias_col = jnp.broadcast_to(dtb[...], (SEQ, 16)).T
    v.negA[...] = -jnp.exp(jnp.broadcast_to(alog[...], (SEQ, 16)).T)
    row_id = rows_of((SEQ, SEQ))
    lane_id = lanes_of((SEQ, SEQ))
    causal = row_id >= lane_id
    low = lane_id < HEAD_DIM

    spread_wait(v.sq, "sq")
    total_sq = v.sq[0] + v.sq[1] + v.sq[2] + v.sq[3]
    for mb in range(2):
        v.scale[mb] = lax.rsqrt(as_column(total_sq[mb : mb + 1]) / D + 1e-05)

    smt(1 - core).wait_recv()

    def prepare(mb):
        scale = v.scale[mb]
        small = v.sm[mb] * wide(scale, 3)
        conv = conv_rows(small[:, :MAPS], convbc[...])
        sig = sigmoid(conv)
        maps = (conv * sig).astype(BF16)
        v.scores[mb] = dot1(maps[:, NSTATE:], maps[:, :NSTATE], NT)
        if mb == 0:
            v.maps[...] = maps
            v.dcm[...] = d_silu(conv, sig)
        v.pdt[...] = small[:, MAPS:].T
        logits = v.pdt[pl.ds(pl.multiple_of(16 * me, 16), 16)] + bias_col
        steps = jnp.maximum(logits, 0.0) + jnp.log1p(jnp.exp(-jnp.abs(logits)))
        if mb == 0:
            v.sgT[...] = sigmoid(logits)
        v.dtT[mb] = steps
        v.cumT[mb] = dot_full(
            steps * v.negA[...], (row_id <= lane_id).astype(F32), NN
        )

    prepare(0)

    def split_pair(first, second):
        head_x = jnp.where(low, first, pltpu.roll(second, 64, 1))
        head_z = jnp.where(low, pltpu.roll(first, 64, 1), second)
        return head_x, head_z

    def mix(mb, pair, block, save):
        scale = v.scale[mb]
        x, z = split_pair(block[:, :128] * scale, block[:, 128:] * scale)
        conv = conv_rows(x, v.cx[pair])
        sig = sigmoid(conv)
        xc = conv * sig
        sig_z = sigmoid(z)
        gate = z * sig_z
        weights = []
        for k in range(2):
            head = pl.ds(2 * pair + k, 1)
            row = v.cumT[mb, head]
            decay = jnp.exp(jnp.where(causal, as_column(row) - row, -1e30))
            if save:
                v.big_l[2 * pair + k] = decay
            weights.append(decay * v.scores[mb] * v.dtT[mb, head])
        stacked = jnp.concatenate([jnp.where(low, xc, 0.0), jnp.where(low, 0.0, xc)], axis=0)
        y = dot3(jnp.concatenate(weights, axis=1), stacked, NN)
        if save:
            v.xc[pair] = xc
            v.ys[pair] = y
            v.gz[pair] = gate
            v.dcv[pair] = d_silu(conv, sig)
            v.dzs[pair] = d_silu(z, sig_z)
        return (y + v.dsk[pair] * xc) * gate

    def raw_block(mb, x_ref, j):
        return (
            dot1(x_ref[...], v.w[4 * me + j], NN)
            + v.xzd_r[mb, 1, j].astype(F32)
            + v.xzy_r[mb, j].astype(F32)
        )

    v.acc0[...] = jnp.zeros((SEQ, SEQ), F32)

    def stage_a(j):
        load_w(4 * me + j).wait()
        xzd(0, 1, j).wait_recv()
        xzy(0, j).wait_recv()
        follow(j, lambda i: my(i).start())
        raw = raw_block(0, saved, j)
        v.raw[j] = raw
        for k in range(2):
            gated = mix(0, 2 * j + k, raw[:, 256 * k : 256 * k + 256], True)
            v.acc0[...] += gated * gated

    loop(stage_a)

    def fwd_mate(j):
        v.xzd_s[1, 1, j] = dot1(act[...], v.w[4 * mate + j], NN).astype(BF16)
        xzd(1, 1, j).start()

    loop(xz_sum(1, act))
    loop(fwd_mate)

    v.acc1[...] = jnp.zeros((SEQ, SEQ), F32)

    def stage_b(j):
        load_wo(4 * me + j).wait()
        md(1, j).wait_recv()
        my(j).wait_recv()

        @pl.when(j == 2)
        def _():
            xzy(1, 0).start()

        d_mixed = (
            dot1(cot[...], v.wo[4 * me + j], NT)
            + v.md_r[1, j].astype(F32)
            + v.my_r[j].astype(F32)
        )
        for k in range(2):
            pair = 2 * j + k
            part = d_mixed[:, 128 * k : 128 * k + 128]
            v.dm[pair] = part
            gated = (v.ys[pair] + v.dsk[pair] * v.xc[pair]) * v.gz[pair]
            v.acc1[...] += part * v.gain[pair] * gated

    loop(stage_b)

    v.rs[me] = jnp.where(
        rows_of((8, SEQ)) == 0, row_sums(v.acc0[...]), row_sums(v.acc1[...])
    )
    spread_start(v.rs, "rs")
    loop(lambda j: xzy(1, j + 1).start(), 3)
    prepare(1)
    for k in range(4):
        cols = slice(128 * k, 128 * k + 128)
        normed = (saved[:, cols].astype(F32) * v.scale[0]).astype(BF16)
        v.normed[cols] = normed.astype(F32).T.astype(BF16)
    normed_copy = pltpu.make_async_copy(v.normed, normed_o, v.s_out.at[8])
    normed_copy.start()
    spread_wait(v.rs, "rs")
    total_rs = v.rs[0] + v.rs[1] + v.rs[2] + v.rs[3]
    v.acc0[...] = lax.rsqrt(as_column(total_rs[0:1]) / INNER + 1e-05)
    v.acc1[...] = as_column(total_rs[1:2]) / INNER

    v.pdt[...] = jnp.zeros((SEQ, SEQ), F32)
    v.ds_acc[...] = jnp.zeros((2, 64, SEQ), F32)
    head_rows = (
        lanes_of((8, SEQ)) // HEAD_DIM == rows_of((8, SEQ))
    ).astype(F32)

    def stage_c(j):
        inverse = v.acc0[...]
        lower = inverse * inverse * inverse * v.acc1[...]
        for k in range(2):
            pair = 2 * j + k
            xc = v.xc[pair]
            y = v.ys[pair]
            gate = v.gz[pair]
            skip = v.dsk[pair]
            gained = inverse * v.gain[pair]
            y_full = y + skip * xc
            gated = y_full * gate
            v.ga_mix[j, 128 * k : 128 * k + 128] = (gated * gained).T.astype(BF16)
            d_gated = gained * v.dm[pair] - gated * lower
            d_y = d_gated * gate
            d_gate = d_gated * y_full
            d_ys = jnp.concatenate([jnp.where(low, d_y, 0.0), jnp.where(low, 0.0, d_y)], axis=0)
            d_w = dot3(d_ys, xc, NT)
            scores = v.scores[0]
            weights = []
            d_scores = None
            for h in range(2):
                head = pl.ds(2 * pair + h, 1)
                decay = v.big_l[2 * pair + h]
                steps = v.dtT[0, head]
                scored = decay * scores
                weights.append(scored * steps)
                d_head = d_w[SEQ * h : SEQ * h + SEQ]
                term = d_head * (decay * steps)
                d_scores = term if d_scores is None else d_scores + term
                v.dirT[head] = jnp.sum(d_head * scored, axis=0, keepdims=True)
            v.ds_acc[0] += d_scores[:64]
            v.ds_acc[1] += d_scores[64:]
            sums = dot_full(head_rows, d_y * y, NT)
            v.rowT[pl.ds(2 * pair, 1)] = sums[0:1]
            v.rowT[pl.ds(2 * pair + 1, 1)] = sums[1:2]
            d_xc = dot3(jnp.concatenate(weights, axis=0), d_ys, TN) + skip * d_y
            d_x = conv_rows_back(d_xc * v.dcv[pair], v.cx[pair])
            d_z = d_gate * v.dzs[pair]
            first, second = split_pair(d_x, d_z)
            first = first.astype(BF16)
            second = second.astype(BF16)
            v.ga_round[me, j, :, 256 * k : 256 * k + 128] = first
            v.ga_round[me, j, :, 256 * k + 128 : 256 * k + 256] = second
            v.pdt[...] += (
                first.astype(F32) * v.raw[j, :, 256 * k : 256 * k + 128]
                + second.astype(F32) * v.raw[j, :, 256 * k + 128 : 256 * k + 256]
            )
        gather(v.ga_round, "rd", me, j, mate).start()
        send_mix("md2", j, mate).start()

    loop(stage_c)
    hand_out(me).start()
    keep_mix().start()

    v.dsd_s[...] = v.ds_acc[1 - core]
    dsd().start()
    d_cum = v.rowT[...] - v.dtT[0] * v.dirT[...]
    d_a = dot_full(d_cum, (row_id >= lane_id).astype(F32), NN)
    v.tg[me, 0:16] = (v.dirT[...] + v.negA[...] * d_a) * v.sgT[...]
    v.tg[me, 16:24] = row_sums(v.pdt[...])
    spread_start(v.tg, "tg")
    dsd().wait_recv()
    v.ds_tot[core] = v.ds_acc[core] + v.dsd_r[...]
    v.dsy_s[...] = v.ds_tot[core].astype(BF16)
    dsy().start()

    v.acc0[...] = jnp.zeros((SEQ, SEQ), F32)

    def stage_e(j):
        xzd(1, 1, j).wait_recv()
        xzy(1, j).wait_recv()
        follow(j, lambda i: gather(v.ga_round, "ry", me, i, ypeer).start())
        raw = raw_block(1, act, j)
        for k in range(2):
            pair = 2 * j + k
            gated = mix(1, pair, raw[:, 256 * k : 256 * k + 256], False)
            v.acc0[...] += gated * gated
            v.ga_fwd[me, j, :, 128 * k : 128 * k + 128] = (gated * v.gain[pair]).astype(BF16)
        gather(v.ga_fwd, "fd", me, j, mate).start()

    loop(stage_e)
    v.rf[me] = row_sums(v.acc0[...])
    spread_start(v.rf, "rf")

    v.dn[...] = jnp.zeros((SEQ, 512), F32)

    def add_dn(q, j):
        v.dn[...] += dot1(v.ga_round[q, j], v.w[4 * q + j], NT)

    loop(lambda j: add_dn(me, j))

    dsy().wait_recv()
    v.ds_tot[core] = v.ds_tot[core] + v.dsy_r[...].astype(F32)
    dst(core).start()

    def add_mate(j):
        gather(v.ga_round, "rd", mate, j, mate).wait_recv()
        add_dn(mate, j)

    loop(add_mate)
    hand_out(mate).start()
    dst(1 - core).wait_recv()
    d_scores = jnp.concatenate([v.ds_tot[0], v.ds_tot[1]], axis=0)
    ds_high, ds_low = halves(d_scores)
    maps = v.maps[...]
    d_input_map = dot1(ds_high, maps[:, NSTATE:], TN) + dot1(ds_low, maps[:, NSTATE:], TN)
    d_output_map = dot1(ds_high, maps[:, :NSTATE], NN) + dot1(ds_low, maps[:, :NSTATE], NN)
    d_maps = jnp.concatenate([d_input_map, d_output_map], axis=1)
    d_pre = conv_rows_back(d_maps * v.dcm[...], convbc[...])
    v.rbc[:, :MAPS] = d_pre.astype(BF16)
    spread_wait(v.tg, "tg")
    v.pdt[...] = jnp.zeros((SEQ, SEQ), F32)
    for q in range(4):
        v.pdt[16 * q : 16 * q + 16] = v.tg[q, 0:16]
    v.rbc[:, MAPS:] = v.pdt[...].T.astype(BF16)
    rbc_copy = pltpu.make_async_copy(v.rbc, rbc_o, v.s_out.at[9])
    rbc_copy.start()
    product = v.rbc[...].astype(F32) * v.sm[0]
    inner = row_sums(product[:, :128] + product[:, 128:256] + product[:, 256:])
    inner = inner + v.tg[0, 16:24] + v.tg[1, 16:24] + v.tg[2, 16:24] + v.tg[3, 16:24]
    v.acc1[...] = as_column(inner[0:1]) / D
    v.dn[...] += dot1(v.rbc[...], v.wbc[...], NN)

    v.total[...] = jnp.zeros((SEQ, 512), F32)

    def add_out(q, j):
        v.total[...] += dot1(v.ga_fwd[q, j], v.wo[4 * q + j], NN)

    loop(lambda j: add_out(me, j))

    def out_mate(j):
        gather(v.ga_fwd, "fd", mate, j, mate).wait_recv()
        add_out(mate, j)

    loop(out_mate)
    def pass_on(j):
        gather(v.ga_round, "ry", ypeer, j, ypeer).wait_recv()
        follow(j, lambda i: gather(v.ga_fwd, "fy", me, i, ypeer).start())
        gather(v.ga_round, "rw", ypeer, j, mate).start()
        add_dn(ypeer, j)

    loop(pass_on)
    hand_out(ypeer).start()

    def add_diag(j):
        gather(v.ga_round, "rw", diag, j, mate).wait_recv()
        add_dn(diag, j)

    loop(add_diag)
    hand_out(diag).start()
    for k in range(4):
        cols = slice(128 * k, 128 * k + 128)
        scale = v.scale[0]
        d_in = scale * v.dn[:, cols] - saved[:, cols].astype(F32) * (
            scale * scale * scale
        ) * v.acc1[...]
        v.sec[0, :, cols] = (cot[:, cols].astype(F32) + d_in).astype(BF16)
    send_section(0).start()

    loop(lambda j: take_mix("md2", mate, j).wait_recv())
    spread_wait(v.rf, "rf")
    total_rf = v.rf[0] + v.rf[1] + v.rf[2] + v.rf[3]
    v.acc0[...] = lax.rsqrt(as_column(total_rf[0:1]) / INNER + 1e-05)

    def out_peer(j):
        gather(v.ga_fwd, "fy", ypeer, j, ypeer).wait_recv()
        follow(j, lambda i: send_mix("my2", i, ypeer).start())
        gather(v.ga_fwd, "fw", ypeer, j, mate).start()
        add_out(ypeer, j)

    loop(out_peer)

    def out_diag(j):
        gather(v.ga_fwd, "fw", diag, j, mate).wait_recv()
        add_out(diag, j)

    loop(out_diag)
    for k in range(4):
        cols = slice(128 * k, 128 * k + 128)
        mixed = v.total[:, cols] * v.acc0[...]
        v.sec[1, :, cols] = (act[:, cols].astype(F32) + mixed).astype(BF16)
    send_section(1).start()

    smd().wait_send()
    smy().wait_send()
    smt(core).wait_send()
    dsd().wait_send()
    dsy().wait_send()
    dst(core).wait_send()
    for buf, kind in ((v.sq, "sq"), (v.rs, "rs"), (v.rf, "rf"), (v.tg, "tg")):
        for i in range(3):
            spread(buf, kind, i, me).wait_send()

    def drain(j):
        for mb in range(2):
            for role in range(2):
                xzd(mb, role, j).wait_send()
            xzy(mb, j).wait_send()
        md(0, j).wait_send()
        md(1, j).wait_send()
        my(j).wait_send()
        for buf, kinds in (
            (v.ga_round, ("ry", "rd", "rw")),
            (v.ga_fwd, ("fy", "fd", "fw")),
        ):
            gather(buf, kinds[0], me, j, ypeer).wait_send()
            gather(buf, kinds[1], me, j, mate).wait_send()
            gather(buf, kinds[2], ypeer, j, mate).wait_send()

    loop(drain)
    for q in range(4):
        hand_out(q).wait()

    def pass_mix(j):
        take_mix("my2", ypeer, j).wait_recv()
        take_mix("mw", ypeer, j).start()

    loop(pass_mix)
    loop(lambda j: take_mix("mw", diag, j).wait_recv())
    for i in range(2):
        send_section(i).wait()
    normed_copy.wait()
    rbc_copy.wait()

    def drain_mix(j):
        send_mix("my2", j, ypeer).wait_send()
        send_mix("md2", j, mate).wait_send()
        take_mix("mw", ypeer, j).wait_send()

    loop(drain_mix)
    keep_mix().wait()

def chain(saved, act, cot, wxz, wbc, wout, convx, convbc, dtb, alog, dskip, gain):
    table = scratch_table()
    vm = pl.BlockSpec(memory_space=pltpu.VMEM)
    hbm = pl.BlockSpec(memory_space=pl.ANY)
    shape = jax.ShapeDtypeStruct
    return pl.pallas_call(
        functools.partial(chain_kernel, tuple(table)),
        out_shape=(
            shape((4, 4, SEQ, 512), BF16),
            shape((4, 4, 256, SEQ), BF16),
            shape((512, SEQ), BF16),
            shape((SEQ, 384), BF16),
            shape((SEQ, 512), BF16),
            shape((SEQ, 512), BF16),
        ),
        in_specs=[pl.BlockSpec(memory_space=pltpu.HBM)] * 6 + [vm] * 6,
        out_specs=(hbm,) * 6,
        scratch_shapes=list(table.values()),
        compiler_params=pltpu.CompilerParams(
            collective_id=0, has_side_effects=True, vmem_limit_bytes=36 * 1024 * 1024
        ),
        cost_estimate=pl.CostEstimate(
            flops=4_300_000_000, bytes_accessed=18_000_000, transcendentals=2_000_000
        ),
        name="chain",
    )(*(
        pltpu.with_memory_space_constraint(x, pltpu.HBM)
        for x in (saved, act, cot, wxz, wbc, wout, convx, convbc, dtb, alog, dskip, gain)
    ))


def grads_kernel(
    round_ref, mixed_ref, normed_ref, rbc_ref, cot_ref, prev_ref, next_ref,
    xz_o, out_o, bc_o, prev_o, next_o,
    xz_s, out_s, bc_s, s_xz, s_out, s_rest,
):
    small = [
        pltpu.make_async_copy(src, dst, s_rest.at[i])
        for i, (src, dst) in enumerate(((prev_ref, prev_o), (next_ref, next_o), (bc_s, bc_o)))
    ]
    small[0].start()
    small[1].start()

    def xz_copy(i):
        cols = pl.ds(pl.multiple_of(i * 512, 512), 512)
        return pltpu.make_async_copy(xz_s.at[i], xz_o.at[:, cols], s_xz.at[i])

    def out_copy(i):
        rows = pl.ds(pl.multiple_of(i * 256, 256), 256)
        return pltpu.make_async_copy(out_s.at[i], out_o.at[rows], s_out.at[i])

    def step(i, carry):
        out_s[i] = dot1(mixed_ref[i], cot_ref[...], NN)
        out_copy(i).start()
        xz_s[i] = dot1(normed_ref[...], round_ref[i], NN)
        xz_copy(i).start()
        return carry

    lax.fori_loop(0, 16, step, 0)
    bc_s[...] = dot1(rbc_ref[:, :320], normed_ref[...], (((0,), (1,)), ((), ())))
    small[2].start()

    def finish(i, carry):
        out_copy(i).wait()
        xz_copy(i).wait()
        return carry

    lax.fori_loop(0, 16, finish, 0)
    for copy in small:
        copy.wait()


def grads(round_all, mixed_all, normed, rbc, cot, prev_grad, next_act):
    shape = jax.ShapeDtypeStruct
    vm = pl.BlockSpec(memory_space=pltpu.VMEM)
    hbm = pl.BlockSpec(memory_space=pl.ANY)
    dma = pltpu.SemaphoreType.DMA
    return pl.pallas_call(
        grads_kernel,
        out_shape=(
            shape((512, 8192), F32),
            shape((4096, 512), F32),
            shape((320, 512), F32),
            shape((SEQ, 512), BF16),
            shape((SEQ, 512), BF16),
        ),
        in_specs=[vm] * 5 + [hbm] * 2,
        out_specs=(hbm,) * 5,
        scratch_shapes=[
            pltpu.VMEM((16, 512, 512), F32),
            pltpu.VMEM((16, 256, 512), F32),
            pltpu.VMEM((320, 512), F32),
            dma((16,)),
            dma((16,)),
            dma((3,)),
        ],
        compiler_params=pltpu.CompilerParams(vmem_limit_bytes=34 * 1024 * 1024),
        cost_estimate=pl.CostEstimate(
            flops=1_700_000_000, bytes_accessed=29_000_000, transcendentals=0
        ),
        name="grads",
    )(
        round_all.reshape(16, SEQ, 512),
        mixed_all.reshape(16, 256, SEQ),
        normed,
        rbc,
        cot,
        prev_grad,
        next_act,
    )


def per_device_four(
    act_in,
    saved_act,
    cotangent,
    weight_xz,
    weight_bcdt,
    weight_out,
    conv_x,
    conv_bc,
    dt_bias,
    a_log,
    d_skip,
    norm_gain,
):
    round_all, mixed_all, normed, rbc, prev_grad, next_act = chain(
        saved_act[0],
        act_in[0],
        cotangent[0],
        weight_xz[0],
        weight_bcdt[0],
        weight_out[0],
        conv_x[0],
        conv_bc[0],
        dt_bias,
        a_log,
        d_skip,
        norm_gain,
    )
    grad_xz, grad_out, grad_bcdt, prev_grad, next_act = grads(
        round_all, mixed_all, normed, rbc, cotangent[0], prev_grad, next_act
    )
    return (next_act[None], prev_grad[None], grad_xz[None], grad_bcdt[None], grad_out[None])


def solution(mesh):
    return jax.shard_map(
        per_device_four if mesh.shape["dp"] == 4 and mesh.shape["section"] > 1 else per_device,
        mesh=mesh,
        in_specs=(
            P("section", None, "dp"),
            P("section", None, "dp"),
            P("section", None, "dp"),
            P("section", "dp", None),
            P("section", None, "dp"),
            P("section", None, "dp"),
            P("section", None, "dp"),
            P("section", None, None),
            P("section", "dp"),
            P("section", "dp"),
            P("section", "dp"),
            P("section", "dp"),
        ),
        out_specs=(
            P("section", None, "dp"),
            P("section", None, "dp"),
            P("section", "dp", None),
            P("section", None, "dp"),
            P("section", None, "dp"),
        ),
        check_vma=False,
    )
```
